32 devices in a mesh: dp: 8 (over z, x), tensor: 4 (over y, core).
Axes of the slice: x: 2, y: 2, z: 4, core: 2. Of those that a mesh axis runs over, the one named last changes fastest.
Arguments:
- tokens: bfloat16 [8192, 1024], P(('dp', 'tensor')), may hold values from -6 to 6
- segments: int32 [8, 1024], P('dp'), may hold values from 0 to 11, never falling along the last dimension, each value on 1 to 512 neighbouring positions
- ln1_gain: float32 [1024], replicated, may hold values from 0.1 to 1.9
- ln1_bias: float32 [1024], replicated, may hold values from -1.75 to 1.75
- w_query: bfloat16 [1024, 1024], P('dp', 'tensor'), may hold values from -0.25 to 0.25
- b_query: float32 [1024], replicated, may hold values from -3 to 3
- w_key: bfloat16 [1024, 1024], P('dp', 'tensor'), may hold values from -0.25 to 0.25
- w_value: bfloat16 [1024, 1024], P('dp', 'tensor'), may hold values from -0.1875 to 0.1875
- b_value: float32 [1024], replicated, may hold values from -3 to 3
- head_scale: float32 [16], replicated, may hold values from 0.5 to 2
- w_out: bfloat16 [1024, 1024], P('tensor', 'dp'), may hold values from -0.1875 to 0.1875
- b_out: float32 [1024], replicated, may hold values from -3 to 3
- post_gain: float32 [1024], replicated, may hold values from 0.1 to 1.9
- post_bias: float32 [1024], replicated, may hold values from -1.75 to 1.75
- ln2_gain: float32 [1024], replicated, may hold values from 0.1 to 1.9
- ln2_bias: float32 [1024], replicated, may hold values from -1.75 to 1.75
- w_up: bfloat16 [1024, 4096], P('dp', 'tensor'), may hold values from -0.1875 to 0.1875
- b_up: float32 [4096], replicated, may hold values from -3 to 3
- ffn_gain: float32 [4096], replicated, may hold values from 0.1 to 1.9
- ffn_bias: float32 [4096], replicated, may hold values from -1.75 to 1.75
- w_down: bfloat16 [4096, 1024], P('tensor', 'dp'), may hold values from -0.09375 to 0.09375
- b_down: float32 [1024], replicated, may hold values from -1.75 to 1.75
- cotangent: bfloat16 [8192, 1024], P(('dp', 'tensor')), may hold values from -6 to 6
Outputs:
- output: bfloat16 [8192, 1024], P(('dp', 'tensor'))
- input_grad: float32 [8192, 1024], P(('dp', 'tensor'))
- grad_ln1_gain: float32 [1024], replicated
- grad_ln1_bias: float32 [1024], replicated
- grad_w_query: float32 [1024, 1024], P('dp', 'tensor')
- grad_b_query: float32 [1024], replicated
- grad_w_key: float32 [1024, 1024], P('dp', 'tensor')
- grad_w_value: float32 [1024, 1024], P('dp', 'tensor')
- grad_b_value: float32 [1024], replicated
- grad_head_scale: float32 [16], replicated
- grad_w_out: float32 [1024, 1024], P('tensor', 'dp')
- grad_b_out: float32 [1024], replicated
- grad_post_gain: float32 [1024], replicated
- grad_post_bias: float32 [1024], replicated
- grad_ln2_gain: float32 [1024], replicated
- grad_ln2_bias: float32 [1024], replicated
- grad_w_up: float32 [1024, 4096], P('dp', 'tensor')
- grad_b_up: float32 [4096], replicated
- grad_ffn_gain: float32 [4096], replicated
- grad_ffn_bias: float32 [4096], replicated
- grad_w_down: float32 [4096, 1024], P('tensor', 'dp')
- grad_b_down: float32 [1024], replicated
The draws below stay inside these ranges and needn't reach their ends.
Inputs may be any that keep to these rules, and one draw needn't show every extreme that they name: `segments`: along each sequence segment numbers never fall; a document covers at most 512 positions, and some document covers exactly that many.
All inputs are finite; a program needn't handle non-finite values.
Results may differ from the reference program's by a relative error of at most 0.013.
The reference program's roundings to bfloat16 on the way count: a program that leaves them out, or rounds other values in their place, can miss the bound.
Values may be sent and summed in bfloat16 or wider, within the bound.
No kernel may reach another device: no remote copies, remote signals or barrier semaphores. Data moves between devices by JAX's collectives and lax.ppermute only.
A program may use at most 128 MiB of HBM per device.

```python
import math
import jax
import jax.numpy as jnp
import numpy as np
from jax import lax

D = 1024
HEADS = 16
HD = 64
FF = 4096
SEQ = 1024
DOCS = 12
SEQS = 8
TOKENS = 8192


def raised(entries, rng, source, target, blocks, factor):
    def block_of(position):
        return (jnp.arange(entries.shape[position]) // (entries.shape[position] // blocks)).reshape((-1,) + (1,) * (entries.ndim - 1 - position))

    one_side = jax.random.permutation(rng, blocks)[block_of(target)]
    other_side = (block_of(target) + blocks // 2) % blocks
    return jnp.where((block_of(source) == one_side) | (block_of(source) == other_side), factor * entries, entries)


def levels(rng, extent, split, least, largest):
    def one(position, parts):
        heights = jax.random.uniform(jax.random.fold_in(jax.random.fold_in(rng, 6), position), (parts,), jnp.float32, least / len(split), largest / len(split))
        return jnp.repeat(jnp.exp(heights), extent[position] // parts).reshape((-1,) + (1,) * (len(extent) - position - 1))

    factor_of = one(*split[0])
    for cut in split[1:]:
        factor_of = factor_of * one(*cut)
    return factor_of


def length_profile(amount, total, most, lean):
    portions = [(1 << 20) // math.isqrt(rank ** lean) + 1 for rank in range(2, amount + 1)]
    spare, given = total - most - (amount - 1), [1] * (amount - 1)
    while spare > 0:
        free = [i for i in range(amount - 1) if given[i] < most]
        pool, remaining = sum([portions[i] for i in free]), spare
        for i in free:
            addition = min(most - given[i], max(1, remaining * portions[i] // pool), spare)
            given[i] = given[i] + addition
            spare = spare - addition
    return np.array([most] + given)


def uneven_parts(stream_key, number_of, total, bound, lean):
    if number_of == 2:
        one = jax.random.randint(stream_key, (), max(1, total - bound), min(bound, total - 1) + 1)
        return jnp.stack([one, total - one])
    sizes = jnp.asarray(length_profile(number_of, total, bound, lean), jnp.int32)
    pairs = (number_of - 1) // 2
    donor, sink = sizes[1:1 + 2 * pairs:2], sizes[2:2 + 2 * pairs:2]
    room = jnp.minimum(donor - 1, bound - sink)
    moved = jax.random.randint(jax.random.fold_in(stream_key, 1), (pairs,), 0, 1 << 20) % (room + 1)
    sizes = sizes.at[1:1 + 2 * pairs:2].set(donor - moved).at[2:2 + 2 * pairs:2].set(sink + moved)
    return sizes[jax.random.permutation(jax.random.fold_in(stream_key, 2), number_of)]


def normal_values(stream_key, dims, scale, limit, shards=(), held_as=jnp.bfloat16):
    entries = scale * jax.random.normal(stream_key, dims, jnp.float32)
    if shards:
        entries = entries * levels(stream_key, dims, shards, -0.22, 0.18)
    return jnp.clip(entries, -limit, limit).astype(held_as)


def bell_draw_with(key, dims, width, bound, cuts, heavy, kind=jnp.bfloat16):
    values = width * jax.random.normal(key, dims, jnp.float32)
    if cuts:
        values = values * levels(key, dims, cuts, -0.22, 0.18)
    return jnp.clip(raised(values, jax.random.fold_in(key, 3), *heavy), -bound, bound).astype(kind)


def setup_inputs(seed: int = 0) -> dict:
    arg_keys = jax.random.split(jax.random.key(seed), 24)
    tokens = normal_values(arg_keys[0], (TOKENS, D), 1.0, 6.0, ((0, 32),))
    segments = jax.vmap(lambda own: jnp.searchsorted(jnp.cumsum(uneven_parts(own, DOCS, SEQ, SEQ // 2, 2)), jnp.arange(SEQ), side="right"))(jax.random.split(arg_keys[1], SEQS)).reshape((SEQS, SEQ)).astype(jnp.int32)
    ln1_gain = jnp.clip(1.0 + 0.18 * jax.random.normal(arg_keys[2], (D,), jnp.float32), 0.1, 1.9)
    ln1_bias = normal_values(arg_keys[3], (D,), 0.3, 1.75, (), jnp.float32)
    w_query = normal_values(arg_keys[4], (D, D), (D // 2) ** -0.5, 0.25, ((0, 8), (1, 4)))
    b_query = normal_values(arg_keys[5], (D,), 0.5, 3.0, (), jnp.float32)
    w_key = normal_values(arg_keys[6], (D, D), (D // 2) ** -0.5, 0.25, ((0, 8), (1, 4)))
    w_value = normal_values(arg_keys[7], (D, D), D ** -0.5, 0.1875, ((0, 8), (1, 4)))
    b_value = normal_values(arg_keys[8], (D,), 0.5, 3.0, (), jnp.float32)
    head_scale = jnp.clip(jnp.exp(jax.random.uniform(arg_keys[9], (HEADS,), jnp.float32, math.log(0.5), math.log(2.0))), 0.5, 2.0)
    w_out = normal_values(arg_keys[10], (D, D), D ** -0.5, 0.1875, ((0, 4), (1, 8)))
    b_out = normal_values(arg_keys[11], (D,), 0.5, 3.0, (), jnp.float32)
    post_gain = jnp.clip(1.0 + 0.18 * jax.random.normal(arg_keys[12], (D,), jnp.float32), 0.1, 1.9)
    post_bias = normal_values(arg_keys[13], (D,), 0.3, 1.75, (), jnp.float32)
    ln2_gain = jnp.clip(1.0 + 0.18 * jax.random.normal(arg_keys[14], (D,), jnp.float32), 0.1, 1.9)
    ln2_bias = normal_values(arg_keys[15], (D,), 0.3, 1.75, (), jnp.float32)
    w_up = normal_values(arg_keys[16], (D, FF), D ** -0.5, 0.1875, ((0, 8), (1, 4)))
    b_up = normal_values(arg_keys[17], (FF,), 0.5, 3.0, (), jnp.float32)
    ffn_gain = jnp.clip(1.0 + 0.18 * jax.random.normal(arg_keys[18], (FF,), jnp.float32), 0.1, 1.9)
    ffn_bias = normal_values(arg_keys[19], (FF,), 0.3, 1.75, (), jnp.float32)
    w_down = normal_values(arg_keys[20], (FF, D), FF ** -0.5, 0.09375, ((0, 4), (1, 8)))
    b_down = normal_values(arg_keys[21], (D,), 0.3, 1.75, (), jnp.float32)
    cotangent = bell_draw_with(arg_keys[22], (TOKENS, D), 1.0, 6.0, ((0, 32),), (0, 1, 32, 2.75))
    return {"tokens": tokens, "segments": segments, "ln1_gain": ln1_gain, "ln1_bias": ln1_bias, "w_query": w_query, "b_query": b_query, "w_key": w_key, "w_value": w_value, "b_value": b_value, "head_scale": head_scale, "w_out": w_out, "b_out": b_out, "post_gain": post_gain, "post_bias": post_bias, "ln2_gain": ln2_gain, "ln2_bias": ln2_bias, "w_up": w_up, "b_up": b_up, "ffn_gain": ffn_gain, "ffn_bias": ffn_bias, "w_down": w_down, "b_down": b_down, "cotangent": cotangent}


EPS = 1e-05
HIGH = lax.Precision.HIGHEST

@jax.custom_vjp
def low(v):
    return lax.optimization_barrier(v.astype(jnp.bfloat16)).astype(jnp.float32)

@jax.custom_vjp
def low_back(v):
    return v

def low_keep(v):
    return (low(v), None)

def low_pass(kept, grad):
    return (grad,)

def back_keep(v):
    return (v, None)

def back_low(kept, grad):
    return (low(grad),)
low.defvjp(low_keep, low_pass)
low_back.defvjp(back_keep, back_low)

def matmul(left, right):
    return jnp.dot(left, right, precision=HIGH, preferred_element_type=jnp.float32)

def normalize(values, gain, shift):
    mean = lax.optimization_barrier(jnp.mean(values, axis=-1, keepdims=True))
    centered = values - mean
    variance = lax.optimization_barrier(jnp.mean(centered * centered, axis=-1, keepdims=True))
    return centered * lax.rsqrt(variance + EPS) * gain + shift

def layer(inputs, segment, params):
    ln1_gain, ln1_bias, w_query, b_query, w_key, w_value, b_value, head_scale, w_out, b_out, post_gain, post_bias, ln2_gain, ln2_bias, w_up, b_up, ffn_gain, ffn_bias, w_down, b_down = params
    length = inputs.shape[0]
    normed = low(normalize(inputs, ln1_gain, ln1_bias))
    query = low_back(low(matmul(normed, w_query) + b_query)).reshape(length, HEADS, HD)
    keys = low_back(low(matmul(normed, w_key))).reshape(length, HEADS, HD)
    values = low_back(low(matmul(normed, w_value) + b_value)).reshape(length, HEADS, HD)
    block = min(512, length)
    positions = jnp.arange(length, dtype=jnp.int32)
    scale = HD ** (-0.5)

    def attend(start):
        rows = lax.dynamic_slice_in_dim(query, start, block, 0)
        row_pos = start + jnp.arange(block, dtype=jnp.int32)
        row_seg = lax.dynamic_slice_in_dim(segment, start, block, 0)
        allowed = (positions[None, :] <= row_pos[:, None]) & (segment[None, :] == row_seg[:, None])
        raw = low_back(jnp.einsum('qhd,khd->hqk', rows, keys, precision=HIGH))
        scores = jnp.where(allowed[None], raw * scale, -1000000000.0)
        probs = low(jax.nn.softmax(scores, axis=-1))
        return jnp.einsum('hqk,khd->qhd', probs, values, precision=HIGH)
    starts = jnp.arange(0, length, block, dtype=jnp.int32)
    heads_out = lax.map(jax.checkpoint(attend), starts).reshape(length, HEADS, HD)
    heads_out = low_back(heads_out)
    mixed = low(heads_out * head_scale[None, :, None]).reshape(length, D)
    projected = low_back(matmul(mixed, w_out) + b_out)
    hidden = inputs + normalize(projected, post_gain, post_bias)
    ffn_in = low(normalize(hidden, ln2_gain, ln2_bias))
    before_gelu = low_back(matmul(ffn_in, w_up) + b_up)
    active = jax.nn.gelu(before_gelu, approximate=False)
    inner = low(normalize(active, ffn_gain, ffn_bias))
    branch = low_back(matmul(inner, w_down) + b_down)
    return hidden + branch

def reference(tokens, segments, ln1_gain, ln1_bias, w_query, b_query, w_key, w_value, b_value, head_scale, w_out, b_out, post_gain, post_bias, ln2_gain, ln2_bias, w_up, b_up, ffn_gain, ffn_bias, w_down, b_down, cotangent):
    params = tuple((item.astype(jnp.float32) for item in (ln1_gain, ln1_bias, w_query, b_query, w_key, w_value, b_value, head_scale, w_out, b_out, post_gain, post_bias, ln2_gain, ln2_bias, w_up, b_up, ffn_gain, ffn_bias, w_down, b_down)))
    inputs = tokens.astype(jnp.float32).reshape(SEQS, SEQ, D)
    grads = cotangent.astype(jnp.float32).reshape(SEQS, SEQ, D)

    def one_sequence(carry, item):
        rows, segment, grad_out = item
        result, pullback = jax.vjp(lambda values, weights: layer(values, segment, weights), rows, params)
        grad_in, grad_params = pullback(grad_out)
        carry = tuple((first + second for first, second in zip(carry, grad_params)))
        return (carry, (result, grad_in))
    zero_grads = tuple((jnp.zeros_like(item) for item in params))
    totals, (results, grad_inputs) = lax.scan(one_sequence, zero_grads, (inputs, segments, grads))
    g_ln1_gain, g_ln1_bias, g_w_query, g_b_query, g_w_key, g_w_value, g_b_value, g_head_scale, g_w_out, g_b_out, g_post_gain, g_post_bias, g_ln2_gain, g_ln2_bias, g_w_up, g_b_up, g_ffn_gain, g_ffn_bias, g_w_down, g_b_down = totals
    return (results.reshape(TOKENS, D).astype(jnp.bfloat16), grad_inputs.reshape(TOKENS, D), g_ln1_gain, g_ln1_bias, g_w_query, g_b_query, g_w_key, g_w_value, g_b_value, g_head_scale, g_w_out, g_b_out, g_post_gain, g_post_bias, g_ln2_gain, g_ln2_bias, g_w_up, g_b_up, g_ffn_gain, g_ffn_bias, g_w_down, g_b_down)
```

```python
import functools

import jax
import jax.numpy as jnp
from jax import lax
from jax.experimental import pallas as pl
from jax.experimental.pallas import tpu as pltpu
from jax.sharding import PartitionSpec as P

D = 1024
HEADS = 16
HD = 64
FF = 4096
LONGEST = 512
EPS = 1e-05
SCALE = HD ** (-0.5)
F32 = jnp.float32
BF16 = jnp.bfloat16


def dot(left, right, left_dim=1, right_dim=0):
    return lax.dot_general(
        left, right, (((left_dim,), (right_dim,)), ((), ())), preferred_element_type=F32
    )


def norm_parts(values):
    mean = jnp.mean(values, axis=-1, keepdims=True)
    centered = values - mean
    inverse = lax.rsqrt(jnp.mean(centered * centered, axis=-1, keepdims=True) + EPS)
    return centered * inverse, inverse


def norm_backward(grad, unit, inverse, gain):
    scaled = grad * gain
    return inverse * (
        scaled
        - jnp.mean(scaled, axis=-1, keepdims=True)
        - unit * jnp.mean(scaled * unit, axis=-1, keepdims=True)
    )


def gelu_slope(values):
    normal_cdf = 0.5 * (1.0 + lax.erf(values * 0.7071067811865476))
    density = jnp.exp(-0.5 * values * values) * 0.3989422804014327
    return normal_cdf + values * density


def swap(value, axis, mask):
    size = lax.axis_size(axis)
    return lax.ppermute(value, axis, [(i, i ^ mask) for i in range(size)])


def bit_of(axis, mask):
    return (lax.axis_index(axis) // mask) % 2


def join(mine, other, bit, axis):
    return jnp.where(
        bit == 0, jnp.stack([mine, other], axis), jnp.stack([other, mine], axis)
    )


def gather_shards(shard, axis):
    size = lax.axis_size(axis)
    shape = shard.shape
    mask, steps = size // 2, 0
    while mask:
        shard = join(shard, swap(shard, axis, mask), bit_of(axis, mask), steps)
        mask, steps = mask // 2, steps + 1
    return shard.reshape((size,) + shape)


def pick_cols(value, width, bit):
    rows, cols = value.shape
    pairs = cols // (2 * width)
    if width % 128:
        return lax.dynamic_index_in_dim(
            value.reshape(rows, pairs, 2, width), bit, 2, keepdims=False
        ).reshape(rows, pairs * width)
    return jnp.concatenate(
        [
            lax.dynamic_slice_in_dim(value, (2 * p + bit) * width, width, 1)
            for p in range(pairs)
        ],
        1,
    )


def pick_rows(value, height, bit):
    rows, cols = value.shape
    return lax.dynamic_index_in_dim(
        value.reshape(rows // (2 * height), 2, height, cols), bit, 1, keepdims=False
    ).reshape(rows // 2, cols)


def scatter_sum(send, keep, axis, pick, extent):
    size = lax.axis_size(axis)
    total = keep + swap(send, axis, 1).astype(F32)
    mask = 2
    while mask < size:
        bit = bit_of(axis, mask)
        other = swap(pick(total, extent, 1 - bit).astype(BF16), axis, mask)
        total = pick(total, extent, bit) + other.astype(F32)
        mask *= 2
    return total


def sum_everywhere(value):
    for axis in ("tensor", "dp"):
        mask = 1
        while mask < lax.axis_size(axis):
            value = value + swap(value, axis, mask)
            mask *= 2
    return value


def key_range(block, size):
    low = max(0, block * size - (LONGEST // size) * size)
    return low, (block + 1) * size - low


def write_bias(bias_ref, seg_col_ref, seg_row_ref, block, size):
    low, count = key_range(block, size)
    key_pos = low + lax.broadcasted_iota(jnp.int32, (count, size), 0)
    row_pos = block * size + lax.broadcasted_iota(jnp.int32, (count, size), 1)
    same = seg_col_ref[low : low + count, :] == seg_row_ref[:, block * size : (block + 1) * size]
    bias_ref[:count, :] = jnp.where((key_pos <= row_pos) & same, 0.0, -1000000000.0)


def attend_kernel(size, qkv_ref, seg_col_ref, seg_row_ref, scale_ref, o_ref, u_ref, lse_ref,
                  bias_ref, vt_ref, ot_ref):
    length, width = o_ref.shape
    heads = width // HD
    vt_ref[...] = qkv_ref[:, 2 * width :].astype(F32).T.astype(BF16)
    head_of = lax.broadcasted_iota(jnp.int32, (size, width), 1) // HD
    for block in range(length // size):
        low, count = key_range(block, size)
        write_bias(bias_ref, seg_col_ref, seg_row_ref, block, size)
        query = qkv_ref[block * size : (block + 1) * size, :width].astype(F32) * SCALE
        keys = qkv_ref[low : low + count, width : 2 * width]

        def one_head(head, carry):
            masked = jnp.where(head_of == head, query, 0.0).astype(BF16)
            scores = dot(keys, masked, 1, 1) + bias_ref[:count, :]
            highest = jnp.max(scores, axis=0, keepdims=True)
            raised = jnp.exp(scores - highest)
            total = jnp.sum(raised, axis=0, keepdims=True)
            lse_ref[pl.ds(block * heads + head, 1), :] = highest + jnp.log(total)
            probs = (raised * (1.0 / total)).astype(BF16)
            row = pl.multiple_of(head * HD, HD)
            ot_ref[pl.ds(row, HD), :] = dot(vt_ref[pl.ds(row, HD), low : low + count], probs)
            return carry

        lax.fori_loop(0, heads, one_head, 0)
        mixed = ot_ref[...].T
        o_ref[block * size : (block + 1) * size, :] = mixed
        u_ref[block * size : (block + 1) * size, :] = (mixed * scale_ref[...]).astype(BF16)


def attend_back_kernel(size, qkv_ref, du_ref, o_ref, lse_ref, seg_col_ref, seg_row_ref, scale_ref,
                       dqkv_ref, sums_ref,
                       bias_ref, kt_ref, dqt_ref, probs_ref, ds_ref, q_ref, do_ref, dk_ref, dv_ref):
    length, width = o_ref.shape
    heads = width // HD
    kt_ref[...] = qkv_ref[:, width : 2 * width].astype(F32).T.astype(BF16)
    dk_ref[...] = jnp.zeros_like(dk_ref)
    dv_ref[...] = jnp.zeros_like(dv_ref)
    head_of = lax.broadcasted_iota(jnp.int32, (size, width), 1) // HD
    scale_sum = jnp.zeros((1, width), F32)
    bias_sum = jnp.zeros((1, width), F32)
    for block in range(length // size):
        low, count = key_range(block, size)
        rows = slice(block * size, (block + 1) * size)
        write_bias(bias_ref, seg_col_ref, seg_row_ref, block, size)
        query = qkv_ref[rows, :width].astype(F32) * SCALE
        keys = qkv_ref[low : low + count, width : 2 * width]
        values = qkv_ref[low : low + count, 2 * width :]
        du = du_ref[rows, :]
        scale_sum = scale_sum + jnp.sum(du * o_ref[rows, :], axis=0, keepdims=True)
        grad = du * scale_ref[...]

        def one_head(head, carry):
            masked = jnp.where(head_of == head, query, 0.0).astype(BF16)
            grad_here = jnp.where(head_of == head, grad, 0.0).astype(BF16)
            here = pl.ds(pl.multiple_of(head * size, size), size)
            q_ref[here, :] = masked
            do_ref[here, :] = grad_here
            scores = dot(keys, masked, 1, 1) + bias_ref[:count, :]
            full = jnp.exp(scores - lse_ref[pl.ds(block * heads + head, 1), :])
            probs_ref[:count, here] = full.astype(BF16)
            dp = dot(values, grad_here, 1, 1)
            delta = jnp.sum(full * dp, axis=0, keepdims=True)
            ds = (full * (dp - delta)).astype(BF16)
            ds_ref[:count, here] = ds
            row = pl.multiple_of(head * HD, HD)
            dqt_ref[pl.ds(row, HD), :] = dot(kt_ref[pl.ds(row, HD), low : low + count], ds)
            return carry

        lax.fori_loop(0, heads, one_head, 0)
        dq = (dqt_ref[...].T * SCALE).astype(BF16)
        dqkv_ref[rows, :width] = dq
        bias_sum = bias_sum + jnp.sum(dq.astype(F32), axis=0, keepdims=True)
        dk_ref[low : low + count, :] += dot(ds_ref[:count, :], q_ref[...])
        dv_ref[low : low + count, :] += dot(probs_ref[:count, :], do_ref[...])
    dqkv_ref[:, width : 2 * width] = dk_ref[...].astype(BF16)
    dv = dv_ref[...].astype(BF16)
    dqkv_ref[:, 2 * width :] = dv
    sums_ref[0:1, :] = bias_sum
    sums_ref[1:2, :] = jnp.sum(dv.astype(F32), axis=0, keepdims=True)
    sums_ref[2:3, :] = scale_sum
    sums_ref[3:8, :] = jnp.zeros((5, width), F32)


def whole(count):
    return [pl.BlockSpec(memory_space=pltpu.VMEM)] * count


def attend(qkv, seg_col, seg_row, scale_row):
    length, width = qkv.shape[0], qkv.shape[1] // 3
    size = 256
    blocks, heads = length // size, width // HD
    most = LONGEST + size
    cost = blocks * heads * most * size
    return pl.pallas_call(
        functools.partial(attend_kernel, size),
        out_shape=(
            jax.ShapeDtypeStruct((length, width), F32),
            jax.ShapeDtypeStruct((length, width), BF16),
            jax.ShapeDtypeStruct((blocks * heads, size), F32),
        ),
        in_specs=whole(4),
        out_specs=tuple(whole(3)),
        scratch_shapes=[
            pltpu.VMEM((most, size), F32),
            pltpu.VMEM((width, length), BF16),
            pltpu.VMEM((width, size), F32),
        ],
        cost_estimate=pl.CostEstimate(
            flops=cost * 4 * width, bytes_accessed=length * width * 12, transcendentals=cost
        ),
        name="attend",
    )(qkv, seg_col, seg_row, scale_row)


def attend_back(qkv, du, mixed, lse, seg_col, seg_row, scale_row):
    length, width = mixed.shape
    size = 256
    blocks, heads = length // size, width // HD
    most = LONGEST + size
    cost = blocks * heads * most * size
    return pl.pallas_call(
        functools.partial(attend_back_kernel, size),
        out_shape=(
            jax.ShapeDtypeStruct((length, 3 * width), BF16),
            jax.ShapeDtypeStruct((8, width), F32),
        ),
        in_specs=whole(7),
        out_specs=tuple(whole(2)),
        scratch_shapes=[
            pltpu.VMEM((most, size), F32),
            pltpu.VMEM((width, length), BF16),
            pltpu.VMEM((width, size), F32),
            pltpu.VMEM((most, heads * size), BF16),
            pltpu.VMEM((most, heads * size), BF16),
            pltpu.VMEM((heads * size, width), BF16),
            pltpu.VMEM((heads * size, width), BF16),
            pltpu.VMEM((length, width), F32),
            pltpu.VMEM((length, width), F32),
        ],
        cost_estimate=pl.CostEstimate(
            flops=cost * 10 * width, bytes_accessed=length * width * 20, transcendentals=cost
        ),
        name="attend_back",
    )(qkv, du, mixed, lse, seg_col, seg_row, scale_row)


def per_device(
    tokens,
    segments,
    ln1_gain,
    ln1_bias,
    w_query,
    b_query,
    w_key,
    w_value,
    b_value,
    head_scale,
    w_out,
    b_out,
    post_gain,
    post_bias,
    ln2_gain,
    ln2_bias,
    w_up,
    b_up,
    ffn_gain,
    ffn_bias,
    w_down,
    b_down,
    cotangent,
):
    index = lax.axis_index("tensor")
    side, half = index % 2, index // 2
    rows = tokens.shape[0]
    length = rows * lax.axis_size("tensor")
    columns = w_query.shape[1]
    hidden_here = w_up.shape[1]
    near = bit_of("dp", 1)

    def own_part(vector, width):
        return lax.dynamic_slice_in_dim(vector, index * width, width, 0)

    def pair_rows(value):
        return join(value, swap(value, "tensor", 2), half, 0)

    def all_rows(pair):
        full = join(pair, swap(pair, "tensor", 1), side, 1)
        return full.reshape((length,) + pair.shape[2:])

    def side_rows(value, which):
        picked = lax.dynamic_index_in_dim(
            value.reshape((2, 2, rows) + value.shape[1:]), which, 1, keepdims=False
        )
        return picked.reshape((2 * rows,) + value.shape[1:])

    def side_sum(left, right, right_dim):
        send = dot(side_rows(left, 1 - side), right, 1, right_dim).astype(BF16)
        other = swap(send, "tensor", 1)
        return dot(side_rows(left, side), right, 1, right_dim) + other.astype(F32)

    def half_sum(part):
        part = part.reshape(2, rows, D)
        send = lax.dynamic_index_in_dim(part, 1 - half, 0, keepdims=False).astype(BF16)
        keep = lax.dynamic_index_in_dim(part, half, 0, keepdims=False)
        return keep + swap(send, "tensor", 2).astype(F32)

    x_pair = pair_rows(tokens)
    x_all = all_rows(x_pair)
    qkv_w = gather_shards(jnp.concatenate([w_query, w_key, w_value], 1), "dp").reshape(
        D, 3 * columns
    )
    out_w = jnp.moveaxis(gather_shards(w_out, "dp"), 0, 1).reshape(columns, D)
    up_w = gather_shards(w_up, "dp").reshape(D, hidden_here)
    down_w = jnp.moveaxis(gather_shards(w_down, "dp"), 0, 1).reshape(hidden_here, D)
    g_pair = pair_rows(cotangent)
    g_all = all_rows(g_pair)

    segment = segments[0]
    seg_col, seg_row = segment[:, None], segment[None, :]
    scale_row = jnp.repeat(own_part(head_scale, columns // HD), HD)[None, :]
    shard = D // lax.axis_size("dp")

    unit_all, _ = norm_parts(x_all.astype(F32))
    normed = (unit_all * ln1_gain + ln1_bias).astype(BF16)
    qkv_b = jnp.concatenate(
        [own_part(b_query, columns), jnp.zeros((columns,), F32), own_part(b_value, columns)]
    )
    qkv = (dot(normed, qkv_w) + qkv_b).astype(BF16)
    mixed, scaled, lse = attend(qkv, seg_col, seg_row, scale_row)
    part = side_sum(scaled, out_w, 0)
    projected = part + swap(part.astype(BF16), "tensor", 2).astype(F32) + b_out
    unit_two, inverse_two = norm_parts(projected)
    hidden = x_pair.reshape(2 * rows, D).astype(F32) + (unit_two * post_gain + post_bias)
    unit_three, inverse_three = norm_parts(hidden)
    ffn_in = (unit_three * ln2_gain + ln2_bias).astype(BF16)
    ffn_all = all_rows(ffn_in.reshape(2, rows, D))

    gain_here, shift_here = own_part(ffn_gain, hidden_here), own_part(ffn_bias, hidden_here)
    grad_inner = dot(g_all, down_w, 1, 1)
    scaled_grad = grad_inner * gain_here
    before = dot(ffn_all, up_w) + own_part(b_up, hidden_here)
    active = jax.nn.gelu(before, approximate=False)
    mean = jnp.mean(active, axis=-1)
    off_mean = active - mean[:, None]
    square = jnp.sum(off_mean * off_mean, axis=-1)
    plain = jnp.sum(scaled_grad, axis=-1)
    cross = jnp.sum(scaled_grad * off_mean, axis=-1)
    stats = jnp.stack([mean, square, plain, cross])
    count = hidden_here
    for mask in (1, 2):
        other = swap(stats, "tensor", mask)
        middle = 0.5 * (stats[0] + other[0])
        gap = stats[0] - other[0]
        stats = jnp.stack(
            [
                middle,
                stats[1] + other[1] + (0.5 * count) * gap * gap,
                stats[2] + other[2],
                stats[3]
                + other[3]
                + ((stats[0] - middle) * stats[2] + (other[0] - middle) * other[2]),
            ]
        )
        count *= 2
    mean, square, plain, cross = (stats[i][:, None] for i in range(4))
    inverse_four = lax.rsqrt(square / FF + EPS)
    unit_four = (active - mean) * inverse_four
    inner = (unit_four * gain_here + shift_here).astype(BF16)
    grad_active = inverse_four * (
        scaled_grad - plain / FF - unit_four * (cross * inverse_four / FF)
    )
    grad_before = (grad_active * gelu_slope(before)).astype(BF16)

    part = side_sum(grad_before, up_w, 1)
    grad_ffn_in = part + swap(part.astype(BF16), "tensor", 2).astype(F32)
    grad_hidden = g_pair.reshape(2 * rows, D).astype(F32) + norm_backward(
        grad_ffn_in, unit_three, inverse_three, ln2_gain
    )
    grad_proj = norm_backward(grad_hidden, unit_two, inverse_two, post_gain).astype(BF16)
    grad_proj_all = all_rows(grad_proj.reshape(2, rows, D))

    grad_scaled = dot(grad_proj_all, out_w, 1, 1)
    grad_qkv, sums = attend_back(qkv, grad_scaled, mixed, lse, seg_col, seg_row, scale_row)
    grad_normed = half_sum(side_sum(grad_qkv, qkv_w, 1))
    unit_one, inverse_one = norm_parts(tokens.astype(F32))
    own_grad_hidden = lax.dynamic_index_in_dim(
        grad_hidden.reshape(2, rows, D), half, 0, keepdims=False
    )
    input_grad = own_grad_hidden + norm_backward(grad_normed, unit_one, inverse_one, ln1_gain)

    own_hidden = lax.dynamic_index_in_dim(hidden.reshape(2, rows, D), half, 0, keepdims=False)
    branch = half_sum(side_sum(inner, down_w, 0))
    output = (own_hidden + (branch + b_down)).astype(BF16)

    def down_part(bit):
        return dot(inner, pick_cols(g_all, shard, bit), 0, 0)

    g_down_w = scatter_sum(
        down_part(1 - near).astype(BF16), down_part(near), "dp", pick_cols, shard
    )

    def up_part(bit):
        return dot(pick_cols(ffn_all, shard, bit), grad_before, 0, 0)

    g_up_w = scatter_sum(up_part(1 - near).astype(BF16), up_part(near), "dp", pick_rows, shard)

    def out_part(bit):
        return dot(scaled, pick_cols(grad_proj_all, shard, bit), 0, 0)

    g_out_w = scatter_sum(out_part(1 - near).astype(BF16), out_part(near), "dp", pick_cols, shard)

    def qkv_part(bit):
        return dot(pick_cols(normed, shard, bit), grad_qkv, 0, 0)

    g_qkv_w = scatter_sum(qkv_part(1 - near).astype(BF16), qkv_part(near), "dp", pick_rows, shard)

    def columns_sum(value):
        return jnp.sum(value, axis=0)

    def place(vector, width, count_rows):
        return lax.dynamic_update_slice_in_dim(
            jnp.zeros((count_rows * D,), F32), vector, index * width, 0
        ).reshape(count_rows, D)

    early = jnp.concatenate(
        [
            jnp.stack(
                [
                    columns_sum(cotangent.astype(F32)),
                    0.5 * columns_sum(grad_ffn_in * unit_three),
                    0.5 * columns_sum(grad_ffn_in),
                    0.5 * columns_sum(grad_hidden * unit_two),
                    0.5 * columns_sum(grad_hidden),
                    0.5 * columns_sum(grad_proj.astype(F32)),
                ]
            ),
            place(columns_sum(grad_before.astype(F32)), hidden_here, FF // D),
            place(columns_sum(grad_inner * unit_four), hidden_here, FF // D),
            place(columns_sum(grad_inner), hidden_here, FF // D),
        ]
    )
    early = sum_everywhere(early)
    heads_sum = jnp.sum(sums[2].reshape(columns // HD, HD), axis=1)
    late = jnp.concatenate(
        [
            jnp.stack([columns_sum(grad_normed * unit_one), columns_sum(grad_normed)]),
            place(sums[0], columns, 1),
            place(sums[1], columns, 1),
            place(heads_sum, columns // HD, 1),
        ]
    )
    late = sum_everywhere(late)
    blocks = FF // D
    return (
        output,
        input_grad,
        late[0],
        late[1],
        g_qkv_w[:, :columns],
        late[2],
        g_qkv_w[:, columns : 2 * columns],
        g_qkv_w[:, 2 * columns :],
        late[3],
        late[4, :HEADS],
        g_out_w,
        early[5],
        early[3],
        early[4],
        early[1],
        early[2],
        g_up_w,
        early[6 : 6 + blocks].reshape(FF),
        early[6 + blocks : 6 + 2 * blocks].reshape(FF),
        early[6 + 2 * blocks : 6 + 3 * blocks].reshape(FF),
        g_down_w,
        early[0],
    )


def solution(mesh):
    return jax.shard_map(
        per_device,
        mesh=mesh,
        in_specs=(
            P(("dp", "tensor"), None),
            P("dp", None),
            P(),
            P(),
            P("dp", "tensor"),
            P(),
            P("dp", "tensor"),
            P("dp", "tensor"),
            P(),
            P(),
            P("tensor", "dp"),
            P(),
            P(),
            P(),
            P(),
            P(),
            P("dp", "tensor"),
            P(),
            P(),
            P(),
            P("tensor", "dp"),
            P(),
            P(("dp", "tensor"), None),
        ),
        out_specs=(
            P(("dp", "tensor"), None),
            P(("dp", "tensor"), None),
            P(),
            P(),
            P("dp", "tensor"),
            P(),
            P("dp", "tensor"),
            P("dp", "tensor"),
            P(),
            P(),
            P("tensor", "dp"),
            P(),
            P(),
            P(),
            P(),
            P(),
            P("dp", "tensor"),
            P(),
            P(),
            P(),
            P("tensor", "dp"),
            P(),
        ),
        check_vma=False,
    )
```

```python
import functools

import jax
import jax.numpy as jnp
from jax import lax
from jax.experimental import pallas as pl
from jax.experimental.pallas import tpu as pltpu
from jax.sharding import PartitionSpec as P

D = 1024
HEADS = 16
HD = 64
FF = 4096
LONGEST = 512
EPS = 1e-05
SCALE = HD ** (-0.5)
F32 = jnp.float32
BF16 = jnp.bfloat16


def dot(left, right, left_dim=1, right_dim=0):
    return lax.dot_general(
        left, right, (((left_dim,), (right_dim,)), ((), ())), preferred_element_type=F32
    )


def swap(value, axis, mask):
    size = lax.axis_size(axis)
    return lax.ppermute(value, axis, [(i, i ^ mask) for i in range(size)])


def bit_of(axis, mask):
    return (lax.axis_index(axis) // mask) % 2


def after(value, *others):
    return lax.optimization_barrier((value,) + others)[0]


def row(vector):
    return vector[None, :]


def each_rows(count, step, body):
    def one(k, carry):
        body(pl.ds(pl.multiple_of(k * step, step), step))
        return carry

    lax.fori_loop(0, count // step, one, 0)


STEP = 128


def fold(value):
    return jnp.sum(value.reshape(value.shape[0] // 8, 8, value.shape[1]), axis=0)


def norm_stats(values):
    mean = jnp.mean(values, axis=-1, keepdims=True)
    centered = values - mean
    inverse = lax.rsqrt(jnp.mean(centered * centered, axis=-1, keepdims=True) + EPS)
    return centered * inverse, inverse


def norm_backward(grad, unit, inverse, gain):
    scaled = grad * gain
    return inverse * (
        scaled
        - jnp.mean(scaled, axis=-1, keepdims=True)
        - unit * jnp.mean(scaled * unit, axis=-1, keepdims=True)
    )


VMEM = pl.BlockSpec(memory_space=pltpu.VMEM)
SMEM = pl.BlockSpec(memory_space=pltpu.SMEM)


def shaped(shape, kind):
    return jax.ShapeDtypeStruct(shape, kind)


def cost(flops, moved, hard=0):
    return pl.CostEstimate(flops=flops, bytes_accessed=moved, transcendentals=hard)


class Shards:
    def __init__(self, shard):
        self.pieces, self.held = [], shard[None]
        self.masks, self.mask = [0], lax.axis_size("dp") // 2

    def far(self, last=False):
        other = [m ^ self.mask for m in self.masks]
        got = swap(self.held, "dp", self.mask)
        if last:
            self.pieces = [(self.masks, self.held), (other, got)]
        else:
            self.masks, self.held = self.masks + other, jnp.concatenate([self.held, got], 0)
        self.mask //= 2

    def near(self, which):
        masks, value = ((self.masks, self.held), self.pieces[-1])[which]
        return [m ^ 1 for m in masks], swap(value, "dp", 1)


def phase(*values):
    return lax.optimization_barrier(values)


def fill(axis, masks, order_ref, piece_refs, full_ref, start=0, width=None):
    if masks is None:
        full_ref[...] = piece_refs[0][...]
        return
    for group, piece in zip(masks, piece_refs):
        height = piece.shape[1]
        for k, mask in enumerate(group):
            place = order_ref[mask]
            if axis == 0:
                there = pl.ds(pl.multiple_of(place * height, height), height)
                full_ref[there, :] = piece[k, :, start : start + full_ref.shape[1]]
            else:
                there = pl.ds(pl.multiple_of(place * width, width), width)
                for low in range(0, full_ref.shape[0], height):
                    at = start + low // height * width
                    full_ref[low : low + height, there] = piece[k, :, at : at + width]


def pack_kernel(q_ref, k_ref, v_ref, o_ref, out_ref):
    height, width = q_ref.shape
    for k, ref in enumerate((q_ref, k_ref, v_ref)):
        out_ref[:, k * width : (k + 1) * width] = ref[...]
    wide = o_ref.shape[1]
    for k in range(o_ref.shape[0] // height):
        at = 3 * width + k * wide
        out_ref[:, at : at + wide] = o_ref[k * height : (k + 1) * height, :]


def pack(w_query, w_key, w_value, w_out):
    height, width = w_query.shape
    total = 3 * width + w_out.size // height
    return pl.pallas_call(
        pack_kernel,
        out_shape=shaped((height, total), BF16),
        in_specs=[VMEM] * 4,
        out_specs=VMEM,
        cost_estimate=cost(0, 0),
        name="pack",
    )(w_query, w_key, w_value, w_out)


def pick_cols(value, width, bit):
    rows, cols = value.shape
    pairs = cols // (2 * width)
    if width % 128:
        return lax.dynamic_index_in_dim(
            value.reshape(rows, pairs, 2, width), bit, 2, keepdims=False
        ).reshape(rows, pairs * width)
    return jnp.concatenate(
        [
            lax.dynamic_slice_in_dim(value, (2 * p + bit) * width, width, 1)
            for p in range(pairs)
        ],
        1,
    )


def pick_rows(value, height, bit):
    rows, cols = value.shape
    return lax.dynamic_index_in_dim(
        value.reshape(rows // (2 * height), 2, height, cols), bit, 1, keepdims=False
    ).reshape(rows // 2, cols)


class Scatter:
    def __init__(self, send, keep, pick, extent):
        self.total = keep + swap(send, "dp", 1).astype(F32)
        self.pick, self.extent, self.mask = pick, extent, 2

    def step(self):
        if self.mask < lax.axis_size("dp"):
            bit = bit_of("dp", self.mask)
            send = self.pick(self.total, self.extent, 1 - bit).astype(BF16)
            other = swap(send, "dp", self.mask)
            self.total = self.pick(self.total, self.extent, bit) + other.astype(F32)
            self.mask *= 2

    def finish(self):
        while self.mask < lax.axis_size("dp"):
            self.step()
        return self.total


def sum_everywhere(value):
    for axis in ("tensor", "dp"):
        mask = 1
        while mask < lax.axis_size(axis):
            value = value + swap(value, axis, mask)
            mask *= 2
    return value


def norm_one_kernel(a_ref, b_ref, c_ref, d_ref, gain_ref, bias_ref, out_ref, all_ref, cols_ref):
    step = pl.program_id(0)
    per = pl.num_programs(0) // 4
    value = jnp.where(
        step < 2 * per,
        jnp.where(step < per, a_ref[...], b_ref[...]),
        jnp.where(step < 3 * per, c_ref[...], d_ref[...]),
    )
    all_ref[...] = value
    value = value.astype(F32)
    mean = jnp.mean(value, axis=-1, keepdims=True)
    centered = value - mean
    inverse = lax.rsqrt(jnp.mean(centered * centered, axis=-1, keepdims=True) + EPS)
    lane = lax.broadcasted_iota(jnp.int32, cols_ref.shape, 1)
    cols_ref[...] = jnp.where(lane == 0, mean, inverse)
    out_ref[...] = (centered * inverse * gain_ref[...] + bias_ref[...]).astype(BF16)


def norm_one(parts, gain, bias):
    rows, width = parts[0].shape
    per = rows // STEP

    def spec(first, count, width=width):
        return pl.BlockSpec((STEP, width), lambda i: (jnp.clip(i - first, 0, count - 1), 0))

    return pl.pallas_call(
        norm_one_kernel,
        grid=(4 * per,),
        out_shape=(
            shaped((4 * rows, width), BF16),
            shaped((4 * rows, width), BF16),
            shaped((4 * rows, 128), F32),
        ),
        in_specs=[spec(k * per, per) for k in range(4)] + [VMEM, VMEM],
        out_specs=(spec(0, 4 * per), spec(0, 4 * per), spec(0, 4 * per, 128)),
        cost_estimate=cost(0, 0),
        name="norm_one",
    )(*parts, row(gain), row(bias))


def key_range(block, size):
    low = max(0, block * size - (LONGEST // size) * size)
    return low, (block + 1) * size - low


def write_bias(bias_ref, seg_col_ref, seg_row_ref, block, size):
    low, count = key_range(block, size)
    key_pos = low + lax.broadcasted_iota(jnp.int32, (count, size), 0)
    row_pos = block * size + lax.broadcasted_iota(jnp.int32, (count, size), 1)
    same = seg_col_ref[low : low + count, :] == seg_row_ref[:, block * size : (block + 1) * size]
    bias_ref[:count, :] = jnp.where((key_pos <= row_pos) & same, 0.0, -1000000000.0)


def attend_kernel(size, masks, place_ref, order_ref, normed_ref, qkv_b_ref, seg_col_ref, seg_row_ref,
                  scale_ref, *refs):
    *pieces, qkv_ref, o_ref, u_ref, lse_ref, qkv_w_ref, out_w_ref, send_ref, keep_ref = refs[:-3]
    bias_ref, vt_ref, ot_ref = refs[-3:]
    length, width = o_ref.shape
    heads = width // HD
    if masks is None:
        qkv_w_ref[...] = pieces[0][...]
        out_w_ref[...] = pieces[1][...]
    else:
        fill(0, masks, order_ref, pieces, qkv_w_ref)
        fill(1, masks, order_ref, pieces, out_w_ref, 3 * width, pieces[0].shape[1])
    head_of = lax.broadcasted_iota(jnp.int32, (size, width), 1) // HD
    for block in range(length // size):
        rows = slice(block * size, (block + 1) * size)
        here = pl.ds(pl.multiple_of(place_ref[block] * size, size), size)
        product = dot(normed_ref[here, :], qkv_w_ref[...]) + qkv_b_ref[...]
        qkv_ref[rows, :] = product.astype(BF16)
        vt_ref[:, rows] = product[:, 2 * width :].T.astype(BF16)
        low, count = key_range(block, size)
        write_bias(bias_ref, seg_col_ref, seg_row_ref, block, size)
        query = qkv_ref[rows, :width].astype(F32) * SCALE
        keys = qkv_ref[low : low + count, width : 2 * width]
        for head in range(heads):
            masked = jnp.where(head_of == head, query, 0.0).astype(BF16)
            scores = dot(keys, masked, 1, 1) + bias_ref[:count, :]
            highest = jnp.max(scores, axis=0, keepdims=True)
            raised = jnp.exp(scores - highest)
            total = jnp.sum(raised, axis=0, keepdims=True)
            lse_ref[block * heads + head : block * heads + head + 1, :] = highest + jnp.log(total)
            probs = (raised * (1.0 / total)).astype(BF16)
            part = slice(head * HD, (head + 1) * HD)
            ot_ref[part, :] = dot(vt_ref[part, low : low + count], probs)
        mixed = ot_ref[...].T
        o_ref[rows, :] = mixed
        u_ref[here, :] = (mixed * scale_ref[...]).astype(BF16)
    half = length // 2
    send_ref[...] = dot(u_ref[half:, :], out_w_ref[...]).astype(BF16)
    keep_ref[...] = dot(u_ref[:half, :], out_w_ref[...])


def attend_back_kernel(size, place_ref, qkv_ref, own_ref, rest_ref, out_w_ref, o_ref, lse_ref,
                       seg_col_ref, seg_row_ref, scale_ref, dqkv_ref, sums_ref,
                       bias_ref, kt_ref, dqt_ref, probs_ref, ds_ref, q_ref, do_ref, dk_ref, dv_ref,
                       du_ref):
    length, width = o_ref.shape
    heads = width // HD
    du_ref[: length // 2, :] = dot(own_ref[...], out_w_ref[...], 1, 1)
    du_ref[length // 2 :, :] = dot(rest_ref[...], out_w_ref[...], 1, 1)
    kt_ref[...] = qkv_ref[:, width : 2 * width].astype(F32).T.astype(BF16)
    head_of = lax.broadcasted_iota(jnp.int32, (size, width), 1) // HD
    scale_sum = jnp.zeros((1, width), F32)
    q_sum = jnp.zeros((1, width), F32)
    v_sum = jnp.zeros((1, width), F32)
    blocks = length // size
    for block in range(blocks):
        low, count = key_range(block, size)
        rows = slice(block * size, (block + 1) * size)
        here = pl.ds(pl.multiple_of(place_ref[block] * size, size), size)
        write_bias(bias_ref, seg_col_ref, seg_row_ref, block, size)
        query = qkv_ref[rows, :width].astype(F32) * SCALE
        keys = qkv_ref[low : low + count, width : 2 * width]
        values = qkv_ref[low : low + count, 2 * width :]
        du = du_ref[here, :]
        scale_sum = scale_sum + jnp.sum(du * o_ref[rows, :], axis=0, keepdims=True)
        grad = du * scale_ref[...]
        for head in range(heads):
            masked = jnp.where(head_of == head, query, 0.0).astype(BF16)
            grad_here = jnp.where(head_of == head, grad, 0.0).astype(BF16)
            stack = slice(head * size, (head + 1) * size)
            q_ref[stack, :] = masked
            do_ref[stack, :] = grad_here
            scores = dot(keys, masked, 1, 1) + bias_ref[:count, :]
            full = jnp.exp(scores - lse_ref[block * heads + head : block * heads + head + 1, :])
            probs_ref[:count, stack] = full.astype(BF16)
            dp = dot(values, grad_here, 1, 1)
            delta = jnp.sum(full * dp, axis=0, keepdims=True)
            ds = (full * (dp - delta)).astype(BF16)
            ds_ref[:count, stack] = ds
            part = slice(head * HD, (head + 1) * HD)
            dqt_ref[part, :] = dot(kt_ref[part, low : low + count], ds)
        dq = (dqt_ref[...].T * SCALE).astype(BF16)
        dqkv_ref[here, :width] = dq
        q_sum = q_sum + jnp.sum(dq.astype(F32), axis=0, keepdims=True)
        dk = dot(ds_ref[:count, :], q_ref[...])
        dv = dot(probs_ref[:count, :], do_ref[...])
        old = count - size
        if old:
            dk_ref[low : low + old, :] += dk[:old]
            dv_ref[low : low + old, :] += dv[:old]
        dk_ref[rows, :] = dk[old:]
        dv_ref[rows, :] = dv[old:]
    for block in range(blocks):
        rows = slice(block * size, (block + 1) * size)
        here = pl.ds(pl.multiple_of(place_ref[block] * size, size), size)
        dqkv_ref[here, width : 2 * width] = dk_ref[rows, :].astype(BF16)
        dv = dv_ref[rows, :].astype(BF16)
        dqkv_ref[here, 2 * width :] = dv
        v_sum = v_sum + jnp.sum(dv.astype(F32), axis=0, keepdims=True)
    sums_ref[...] = jnp.concatenate(
        [q_sum, v_sum, scale_sum, jnp.zeros((5, width), F32)], axis=0
    )


def attend(place, order, normed, masks, pieces, qkv_b, seg_col, seg_row, scale_row):
    length, width = normed.shape[0], scale_row.shape[1]
    size = length // 4
    heads = width // HD
    most = LONGEST + size
    return pl.pallas_call(
        functools.partial(attend_kernel, size, masks),
        out_shape=(
            shaped((length, 3 * width), BF16),
            shaped((length, width), F32),
            shaped((length, width), BF16),
            shaped((4 * heads, size), F32),
            shaped((D, 3 * width), BF16),
            shaped((width, D), BF16),
            shaped((length // 2, D), BF16),
            shaped((length // 2, D), F32),
        ),
        in_specs=[SMEM] * 2 + [VMEM] * (5 + len(pieces)),
        out_specs=(VMEM,) * 8,
        scratch_shapes=[
            pltpu.VMEM((most, size), F32),
            pltpu.VMEM((width, length), BF16),
            pltpu.VMEM((width, size), F32),
        ],
        cost_estimate=cost(0, 0),
        name="attend",
    )(place, order, normed, qkv_b, seg_col, seg_row, scale_row, *pieces)


def attend_back(place, qkv, own, rest, out_w, mixed, lse, seg_col, seg_row, scale_row):
    length, width = mixed.shape
    size = length // 4
    heads = width // HD
    most = LONGEST + size
    pairs = 4 * heads * most * size
    return pl.pallas_call(
        functools.partial(attend_back_kernel, size),
        out_shape=(shaped((length, 3 * width), BF16), shaped((8, width), F32)),
        in_specs=[SMEM] + [VMEM] * 9,
        out_specs=(VMEM,) * 2,
        scratch_shapes=[
            pltpu.VMEM((most, size), F32),
            pltpu.VMEM((width, length), BF16),
            pltpu.VMEM((width, size), F32),
            pltpu.VMEM((most, heads * size), BF16),
            pltpu.VMEM((most, heads * size), BF16),
            pltpu.VMEM((heads * size, width), BF16),
            pltpu.VMEM((heads * size, width), BF16),
            pltpu.VMEM((length, width), F32),
            pltpu.VMEM((length, width), F32),
            pltpu.VMEM((length, width), F32),
        ],
        cost_estimate=cost(0, 0),
        name="attend_back",
    )(place, qkv, own, rest, out_w, mixed, lse, seg_col, seg_row, scale_row)


def middle_kernel(keep_ref, got_ref, other_ref, mine_ref, pair_ref, b_out_ref, post_g_ref, post_b_ref,
                  ln2_g_ref, ln2_b_ref, ffn_in_ref, unit2_ref, cols_ref):
    first = pl.program_id(0) < pl.num_programs(0) // 2
    tokens = jnp.where(first, mine_ref[...], pair_ref[...]).astype(F32)
    part = keep_ref[...] + got_ref[...].astype(F32)
    projected = part + other_ref[...].astype(F32) + b_out_ref[...]
    unit2, inv2 = norm_stats(projected)
    unit2_ref[...] = unit2
    hidden = tokens + (unit2 * post_g_ref[...] + post_b_ref[...])
    mean3 = jnp.mean(hidden, axis=-1, keepdims=True)
    centered = hidden - mean3
    inv3 = lax.rsqrt(jnp.mean(centered * centered, axis=-1, keepdims=True) + EPS)
    ffn_in_ref[...] = (centered * inv3 * ln2_g_ref[...] + ln2_b_ref[...]).astype(BF16)
    lane = lax.broadcasted_iota(jnp.int32, cols_ref.shape, 1)
    cols_ref[...] = jnp.where(lane == 0, inv2, jnp.where(lane == 1, mean3, inv3))


def pair_specs(rows, width):
    half = rows // 2 // STEP
    straight = pl.BlockSpec((STEP, width), lambda i: (i, 0))
    crossed = pl.BlockSpec((STEP, width), lambda i: ((i + half) % (2 * half), 0))
    mine = pl.BlockSpec((STEP, width), lambda i: (jnp.minimum(i, half - 1), 0))
    theirs = pl.BlockSpec((STEP, width), lambda i: (jnp.maximum(i - half, 0), 0))
    return straight, crossed, mine, theirs


def middle(keep, got, other, mine, pair, b_out, post_gain, post_bias, ln2_gain, ln2_bias):
    rows, width = keep.shape
    straight, crossed, own, theirs = pair_specs(rows, width)
    columns = pl.BlockSpec((STEP, 128), lambda i: (i, 0))
    return pl.pallas_call(
        middle_kernel,
        grid=(rows // STEP,),
        out_shape=(
            shaped((rows, width), BF16),
            shaped((rows, width), F32),
            shaped((rows, 128), F32),
        ),
        in_specs=[straight, straight, crossed, own, theirs] + [VMEM] * 5,
        out_specs=(straight, straight, columns),
        cost_estimate=cost(0, 0),
        name="middle",
    )(keep, got, other, mine, pair, row(b_out), row(post_gain), row(post_bias), row(ln2_gain),
      row(ln2_bias))


def middle_back_kernel(keep_ref, got_ref, other_ref, mine_ref, pair_ref, tokens_ref, tokens2_ref,
                       unit2_ref, cols_ref, post_g_ref, post_b_ref, ln2_g_ref, proj_ref, grad_ref, sums_ref,
                       acc_ref):
    step = pl.program_id(0)
    half = pl.num_programs(0) // 2
    first = step < half

    @pl.when(step == 0)
    def _():
        acc_ref[...] = jnp.zeros_like(acc_ref)

    part = keep_ref[...] + got_ref[...].astype(F32)
    incoming = part + other_ref[...].astype(F32)
    tokens = jnp.where(first, tokens_ref[...], tokens2_ref[...]).astype(F32)
    unit2 = unit2_ref[...]
    inv2, mean3, inv3 = (cols_ref[:, k : k + 1] for k in range(3))
    hidden = tokens + (unit2 * post_g_ref[...] + post_b_ref[...])
    unit3 = (hidden - mean3) * inv3
    outgoing = jnp.where(first, mine_ref[...], pair_ref[...]).astype(F32)
    grad = outgoing + norm_backward(incoming, unit3, inv3, ln2_g_ref[...])
    proj = norm_backward(grad, unit2, inv2, post_g_ref[...]).astype(BF16)
    proj_ref[...] = proj

    @pl.when(first)
    def _():
        grad_ref[...] = grad
        for k, value in enumerate(
            (incoming * unit3, incoming, grad * unit2, grad, proj.astype(F32), outgoing)
        ):
            acc_ref[8 * k : 8 * k + 8, :] += fold(value)

    @pl.when(step == half - 1)
    def _():
        sums_ref[...] = jnp.concatenate(
            [jnp.sum(acc_ref[8 * k : 8 * k + 8, :], axis=0, keepdims=True) for k in range(6)]
            + [jnp.zeros((2, acc_ref.shape[1]), F32)],
            axis=0,
        )


def middle_back(keep, got, other, mine, pair, tokens, tokens2, unit2, cols, post_gain, post_bias,
                ln2_gain):
    rows, width = keep.shape
    straight, crossed, own, theirs = pair_specs(rows, width)
    columns = pl.BlockSpec((STEP, 128), lambda i: (i, 0))
    return pl.pallas_call(
        middle_back_kernel,
        grid=(rows // STEP,),
        out_shape=(
            shaped((rows, width), BF16),
            shaped((rows // 2, width), F32),
            shaped((8, width), F32),
        ),
        in_specs=[straight, straight, crossed, own, theirs, own, theirs, straight, columns] + [VMEM] * 3,
        out_specs=(straight, own, VMEM),
        scratch_shapes=[pltpu.VMEM((48, width), F32)],
        cost_estimate=cost(0, 0),
        name="middle_back",
    )(keep, got, other, mine, pair, tokens, tokens2, unit2, cols, row(post_gain), row(post_bias),
      row(ln2_gain))


def ffn_one_kernel(masks, order_ref, in_ref, b_up_ref, *refs):
    *pieces, active_ref, slope_ref, stats_ref, up_ref, cols_ref = refs

    @pl.when(pl.program_id(0) == 0)
    def _():
        fill(0, masks, order_ref, pieces, up_ref)

    active_ref[...] = dot(in_ref[...], up_ref[...]) + b_up_ref[...]
    lane = lax.broadcasted_iota(jnp.int32, (STEP, 128), 1)

    def body(rows):
        before = active_ref[rows, :]
        cdf = 0.5 * (1.0 + lax.erf(before * 0.7071067811865476))
        active = before * cdf
        density = jnp.exp(-0.5 * before * before) * 0.3989422804014327
        slope_ref[rows, :] = cdf + before * density
        active_ref[rows, :] = active
        mean = jnp.mean(active, axis=-1, keepdims=True)
        off = active - mean
        square = jnp.sum(off * off, axis=-1, keepdims=True)
        cols_ref[rows, :] = jnp.where(lane == 0, mean, square)

    each_rows(active_ref.shape[0], STEP, body)
    stats_ref[...] = cols_ref[...].T[:8, :]


def ffn_one(ffn_in, order, masks, pieces, b_up):
    rows, width = ffn_in.shape[0], b_up.shape[0]
    size = 256
    tile = pl.BlockSpec((size, width), lambda i: (i, 0))
    return pl.pallas_call(
        functools.partial(ffn_one_kernel, masks),
        grid=(rows // size,),
        out_shape=(
            shaped((rows, width), F32),
            shaped((rows, width), F32),
            shaped((8, rows), F32),
            shaped((D, width), BF16),
        ),
        in_specs=[SMEM, pl.BlockSpec((size, D), lambda i: (i, 0)), VMEM] + [VMEM] * len(pieces),
        out_specs=(tile, tile, pl.BlockSpec((8, size), lambda i: (0, i)), VMEM),
        scratch_shapes=[pltpu.VMEM((size, 128), F32)],
        cost_estimate=cost(0, 0),
        name="ffn_one",
    )(order, ffn_in, row(b_up), *pieces)


def ffn_grad_kernel(masks, order_ref, grad_ref, keep_ref, send_ref, stats_k_ref, stats_s_ref, gain_ref,
                    *refs):
    *pieces, inner_ref, stats_ref, down_ref, cols_ref = refs
    step = pl.program_id(0)
    first = step < pl.num_programs(0) // 2

    @pl.when(step == 0)
    def _():
        fill(1, masks, order_ref, pieces, down_ref, 0, pieces[0].shape[-1])

    inner_ref[...] = dot(grad_ref[...], down_ref[...], 1, 1)
    lane = lax.broadcasted_iota(jnp.int32, (STEP, 128), 1)

    def body(rows):
        active = jnp.where(first, keep_ref[rows, :], send_ref[rows, :])
        scaled = inner_ref[rows, :] * gain_ref[...]
        plain = jnp.sum(scaled, axis=-1, keepdims=True)
        cross = jnp.sum(scaled * active, axis=-1, keepdims=True)
        cols_ref[rows, :] = jnp.where(lane == 2, plain, cross)

    each_rows(inner_ref.shape[0], STEP, body)
    stats = jnp.where(first, stats_k_ref[...], stats_s_ref[...])
    index = lax.broadcasted_iota(jnp.int32, stats.shape, 0)
    stats_ref[...] = jnp.where(index < 2, stats, cols_ref[...].T[:8, :])


def ffn_grad(grad, order, masks, pieces, active_k, active_s, stats_k, stats_s, gain):
    rows, width = grad.shape[0], gain.shape[0]
    size = 256
    half = rows // size // 2
    keep = lambda i: jnp.minimum(i, half - 1)
    send = lambda i: jnp.maximum(i - half, 0)
    tile = (size, width)
    return pl.pallas_call(
        functools.partial(ffn_grad_kernel, masks),
        grid=(rows // size,),
        out_shape=(
            shaped((rows, width), F32),
            shaped((8, rows), F32),
            shaped((width, D), BF16),
        ),
        in_specs=[
            SMEM,
            pl.BlockSpec((size, D), lambda i: (i, 0)),
            pl.BlockSpec(tile, lambda i: (keep(i), 0)),
            pl.BlockSpec(tile, lambda i: (send(i), 0)),
            pl.BlockSpec((8, size), lambda i: (0, keep(i))),
            pl.BlockSpec((8, size), lambda i: (0, send(i))),
            VMEM,
        ]
        + [VMEM] * len(pieces),
        out_specs=(
            pl.BlockSpec(tile, lambda i: (i, 0)),
            pl.BlockSpec((8, size), lambda i: (0, i)),
            VMEM,
        ),
        scratch_shapes=[pltpu.VMEM((size, 128), F32)],
        cost_estimate=cost(0, 0),
        name="ffn_grad",
    )(order, grad, active_k, active_s, stats_k, stats_s, row(gain), *pieces)


def ffn_two_kernel(mk_ref, ms_ref, sk_ref, ss_ref, grad_ref, s0_ref, s1_ref, s2_ref, s3_ref, gain_ref,
                   shift_ref, up_ref, inner_ref, before_ref, send_ref, keep_ref, sums_ref, cols_ref,
                   acc_ref):
    step = pl.program_id(0)
    half = pl.num_programs(0) // 2
    count, width = inner_ref.shape

    @pl.when(step == 0)
    def _():
        acc_ref[...] = jnp.zeros_like(acc_ref)

    values = [ref[...] for ref in (s0_ref, s1_ref, s2_ref, s3_ref)]
    mean = 0.25 * ((values[0][0:1] + values[1][0:1]) + (values[2][0:1] + values[3][0:1]))
    square = plain = cross = jnp.zeros_like(mean)
    for value in values:
        gap = value[0:1] - mean
        square = square + (value[1:2] + width * (gap * gap))
        plain = plain + value[2:3]
        cross = cross + value[3:4]
    inverse = lax.rsqrt(square / FF + EPS)
    cross = (cross - mean * plain) * inverse
    table = jnp.concatenate(
        [mean, inverse, plain / FF, cross / FF, jnp.zeros((124, count), F32)], axis=0
    )
    cols_ref[...] = table.T

    def work(active_ref, slope_ref, out_ref):
        def body(rows):
            cols = cols_ref[rows, :]
            mean, inverse, plain, cross = (cols[:, k : k + 1] for k in range(4))
            unit = (active_ref[rows, :] - mean) * inverse
            inner_ref[rows, :] = (unit * gain_ref[...] + shift_ref[...]).astype(BF16)
            grad = grad_ref[rows, :]
            moved = inverse * (grad * gain_ref[...] - plain - unit * cross)
            before = (moved * slope_ref[rows, :]).astype(BF16)
            before_ref[rows, :] = before
            for k, value in enumerate((before.astype(F32), grad * unit, grad)):
                acc_ref[8 * k : 8 * k + 8, :] += fold(value)

        each_rows(count, STEP, body)
        out_ref[...] = dot(before_ref[...], up_ref[...], 1, 1).astype(out_ref.dtype)

    @pl.when(step < half)
    def _():
        work(ms_ref, ss_ref, send_ref)

    @pl.when(step >= half)
    def _():
        work(mk_ref, sk_ref, keep_ref)

    @pl.when(step == 2 * half - 1)
    def _():
        sums_ref[...] = jnp.concatenate(
            [jnp.sum(acc_ref[8 * k : 8 * k + 8, :], axis=0, keepdims=True) for k in range(3)]
            + [jnp.zeros((5, width), F32)],
            axis=0,
        )


def ffn_two(active_k, active_s, slope_k, slope_s, inner_grad, stats, gain, shift, up_w):
    rows, width = active_k.shape
    size = 256
    half = rows // size
    keep = lambda i: jnp.maximum(i - half, 0)
    send = lambda i: jnp.minimum(i, half - 1)
    keep_spec = lambda shape: pl.BlockSpec(shape, lambda i: (keep(i), 0))
    send_spec = lambda shape: pl.BlockSpec(shape, lambda i: (send(i), 0))
    tile = (size, width)
    block = lambda i: (i + half) % (2 * half)
    both = pl.BlockSpec(tile, lambda i: (block(i), 0))
    held = (lambda b: b, lambda b: (b + 2) % 4, lambda b: b + 1 - 2 * (b % 2), lambda b: 3 - b)
    return pl.pallas_call(
        ffn_two_kernel,
        grid=(2 * half,),
        out_shape=(
            shaped((2 * rows, width), BF16),
            shaped((2 * rows, width), BF16),
            shaped((rows, D), BF16),
            shaped((rows, D), F32),
            shaped((8, width), F32),
        ),
        in_specs=[keep_spec(tile), send_spec(tile), keep_spec(tile), send_spec(tile), both]
        + [pl.BlockSpec((8, size), lambda i, at=at: (0, at(block(i)))) for at in held]
        + [VMEM] * 3,
        out_specs=(both, both, send_spec((size, D)), keep_spec((size, D)), VMEM),
        scratch_shapes=[pltpu.VMEM((size, 128), F32), pltpu.VMEM((24, width), F32)],
        cost_estimate=cost(0, 0),
        name="ffn_two",
    )(active_k, active_s, slope_k, slope_s, inner_grad, *stats, row(gain), row(shift), up_w)


def normed_grad_kernel(side_ref, grad_ref, weight_ref, all_ref, cols_ref, sums_ref, middle_ref, ffn_ref,
                       send_ref, keep_ref, late_ref, acc_ref):
    step = pl.program_id(0)
    half = pl.num_programs(0) // 2
    width = late_ref.shape[1]

    @pl.when(step == 0)
    def _():
        acc_ref[...] = jnp.zeros_like(acc_ref)

    grad = dot(grad_ref[...], weight_ref[...], 1, 1)
    unit = (all_ref[...].astype(F32) - cols_ref[:, 0:1]) * cols_ref[:, 1:2]
    for k, value in enumerate((grad * unit, grad)):
        acc_ref[8 * k : 8 * k + 8, :] += fold(value)

    @pl.when(step < half)
    def _():
        send_ref[...] = grad.astype(BF16)

    @pl.when(step >= half)
    def _():
        keep_ref[...] = grad

    @pl.when(step == 2 * half - 1)
    def _():
        here = side_ref[0]
        wide = [
            jnp.concatenate(
                [jnp.where(here == k, sums_ref[r : r + 1, :], 0.0) for k in range(4)], axis=1
            )
            for r in range(3)
        ]
        place = lax.broadcasted_iota(jnp.int32, (4, width), 0) == here
        late_ref[...] = jnp.concatenate(
            [jnp.sum(acc_ref[8 * k : 8 * k + 8, :], axis=0, keepdims=True) for k in range(2)]
            + wide
            + [middle_ref[0:6, :], jnp.zeros((1, width), F32)]
            + [jnp.where(place, ffn_ref[k : k + 1, :], 0.0) for k in range(3)],
            axis=0,
        )


def normed_grad(here, grad_qkv, qkv_w, x_all, cols, sums, middle_sums, ffn_sums):
    length, width = x_all.shape
    size = 256
    half = length // size // 2
    block = lambda i: ((i + half) % (2 * half), 0)
    return pl.pallas_call(
        normed_grad_kernel,
        grid=(2 * half,),
        out_shape=(
            shaped((length // 2, width), BF16),
            shaped((length // 2, width), F32),
            shaped((24, width), F32),
        ),
        in_specs=[
            SMEM,
            pl.BlockSpec((size, grad_qkv.shape[1]), block),
            VMEM,
            pl.BlockSpec((size, width), block),
            pl.BlockSpec((size, 128), block),
            VMEM,
            VMEM,
            VMEM,
        ],
        out_specs=(
            pl.BlockSpec((size, width), lambda i: (jnp.minimum(i, half - 1), 0)),
            pl.BlockSpec((size, width), lambda i: (jnp.maximum(i - half, 0), 0)),
            VMEM,
        ),
        scratch_shapes=[pltpu.VMEM((16, width), F32)],
        cost_estimate=cost(0, 0),
        name="normed_grad",
    )(here, grad_qkv, qkv_w, x_all, cols, sums, middle_sums, ffn_sums)


def last_kernel(keep_ref, got_ref, other_ref, tokens_ref, cols_ref, gain_ref, hidden_ref, grad_ref):
    incoming = keep_ref[...] + got_ref[...].astype(F32) + other_ref[...].astype(F32)
    inverse = cols_ref[:, 1:2]
    unit = (tokens_ref[...].astype(F32) - cols_ref[:, 0:1]) * inverse
    grad_ref[...] = hidden_ref[...] + norm_backward(incoming, unit, inverse, gain_ref[...])


def last(keep, got, other, tokens, cols, gain, grad_hidden):
    rows, width = tokens.shape
    tile = pl.BlockSpec((STEP, width), lambda i: (i, 0))
    return pl.pallas_call(
        last_kernel,
        grid=(rows // STEP,),
        out_shape=shaped((rows, width), F32),
        in_specs=[tile] * 4 + [pl.BlockSpec((STEP, 128), lambda i: (i, 0)), VMEM, tile],
        out_specs=tile,
        cost_estimate=cost(0, 0),
        name="last",
    )(keep, got, other, tokens, cols, row(gain), grad_hidden)


def output_kernel(keep_ref, got_ref, other_ref, tokens_ref, unit2_ref, post_g_ref, post_b_ref, b_down_ref,
                  out_ref):
    hidden = tokens_ref[...].astype(F32) + (unit2_ref[...] * post_g_ref[...] + post_b_ref[...])
    branch = keep_ref[...] + got_ref[...].astype(F32) + other_ref[...].astype(F32)
    out_ref[...] = (hidden + (branch + b_down_ref[...])).astype(BF16)


def output_rows(keep, got, other, tokens, unit2, post_gain, post_bias, b_down):
    rows, width = tokens.shape
    tile = pl.BlockSpec((STEP, width), lambda i: (i, 0))
    return pl.pallas_call(
        output_kernel,
        grid=(rows // STEP,),
        out_shape=shaped((rows, width), BF16),
        in_specs=[tile] * 5 + [VMEM] * 3,
        out_specs=tile,
        cost_estimate=cost(0, 0),
        name="output_rows",
    )(keep, got, other, tokens, unit2, row(post_gain), row(post_bias), row(b_down))


def per_device(
    tokens,
    segments,
    ln1_gain,
    ln1_bias,
    w_query,
    b_query,
    w_key,
    w_value,
    b_value,
    head_scale,
    w_out,
    b_out,
    post_gain,
    post_bias,
    ln2_gain,
    ln2_bias,
    w_up,
    b_up,
    ffn_gain,
    ffn_bias,
    w_down,
    b_down,
    cotangent,
):
    index = lax.axis_index("tensor")
    rows = tokens.shape[0]
    two = 2 * rows
    columns = w_query.shape[1]
    hidden_here = w_up.shape[1]
    near = bit_of("dp", 1)
    shard = D // lax.axis_size("dp")
    order = jnp.array([0, 2, 1, 3], jnp.int32)
    place = order[jnp.arange(4, dtype=jnp.int32) ^ index]
    here = jnp.full((1,), index, jnp.int32)

    def own_part(vector, width):
        return lax.dynamic_slice_in_dim(vector, index * width, width, 0)

    def halves(value, pick):
        return pick(value, shard, 1 - near), pick(value, shard, near)

    segment = segments[0]
    seg_col, seg_row = segment[:, None], segment[None, :]
    scale_row = row(jnp.repeat(own_part(head_scale, columns // HD), HD))
    qkv_b = jnp.concatenate(
        [own_part(b_query, columns), jnp.zeros((columns,), F32), own_part(b_value, columns)]
    )
    gain_here, shift_here = own_part(ffn_gain, hidden_here), own_part(ffn_bias, hidden_here)
    b_up_here = own_part(b_up, hidden_here)

    order_dp = lax.axis_index("dp") ^ jnp.arange(lax.axis_size("dp"), dtype=jnp.int32)
    quick = shard % 128 == 0 and lax.axis_size("dp") == 8

    x_pair = swap(tokens, "tensor", 2)
    x_side = swap(tokens, "tensor", 1)
    if quick:
        attn = Shards(pack(w_query, w_key, w_value, w_out))
        up_s, down_s = Shards(w_up), Shards(w_down)
        attn.far()
    else:
        attn, up_s, down_s = (Shards(tokens[:16, :128]) for _ in range(3))
        attn_full = [
            lax.all_gather(jnp.concatenate([w_query, w_key, w_value], 1), "dp", axis=0, tiled=True),
            lax.all_gather(w_out, "dp", axis=1, tiled=True),
        ]
        up_full = [lax.all_gather(w_up, "dp", axis=0, tiled=True)]
        down_full = [lax.all_gather(w_down, "dp", axis=1, tiled=True)]
    (x_pair, x_side, attn.held, up_s.held, down_s.held, cotangent, b_up_here, gain_here, shift_here,
     qkv_b, scale_row, seg_col) = phase(
        x_pair, x_side, attn.held, up_s.held, down_s.held, cotangent, b_up_here, gain_here, shift_here,
        qkv_b, scale_row, seg_col)

    x_cross = swap(x_pair, "tensor", 1)
    if quick:
        attn.far(True)
        attn_near = attn.near(0)
        attn.pieces[1] = (attn.pieces[1][0], attn.pieces[1][1])
        arrived = attn.pieces[1][1]
    else:
        arrived = attn.held
    x_cross, arrived, up_s.held, down_s.held, cotangent = phase(
        x_cross, arrived, up_s.held, down_s.held, cotangent
    )

    if quick:
        attn.pieces[1] = (attn.pieces[1][0], arrived)
        attn.pieces += [attn_near, attn.near(1)]
        up_s.far()
    g_pair = swap(cotangent, "tensor", 2)
    normed, x_all, cols1 = norm_one([tokens, x_pair, x_side, x_cross], ln1_gain, ln1_bias)
    if quick:
        attn_masks = [masks for masks, _ in attn.pieces]
        attn_full = [piece for _, piece in attn.pieces]
    else:
        attn_masks = None
    (normed, up_s.held, down_s.held, g_pair), attn_full = phase(
        (normed, up_s.held, down_s.held, g_pair), attn_full
    )

    if quick:
        up_s.far(True)
        up_near = up_s.near(0)
        down_s.far()
    g_side = swap(cotangent, "tensor", 1)
    qkv, mixed, scaled, lse, qkv_w, out_w, send, keep = attend(
        place, order_dp, normed, attn_masks, attn_full, row(qkv_b), seg_col, seg_row, scale_row
    )
    arrived = up_s.pieces[1][1] if quick else up_s.held
    (qkv, mixed, scaled, lse, qkv_w, out_w, send, keep, g_side, g_pair, arrived, down_s.held) = phase(
        qkv, mixed, scaled, lse, qkv_w, out_w, send, keep, g_side, g_pair, arrived, down_s.held
    )

    got = swap(send, "tensor", 1)
    other = swap((keep + got.astype(F32)).astype(BF16), "tensor", 2)
    g_cross = swap(g_pair, "tensor", 1)
    if quick:
        up_s.pieces[1] = (up_s.pieces[1][0], arrived)
        up_s.pieces += [up_near, up_s.near(1)]
        up_masks = [masks for masks, _ in up_s.pieces]
        up_full = [piece for _, piece in up_s.pieces]
        down_s.far(True)
        down_near = down_s.near(0)
        down_s.pieces += [down_near, down_s.near(1)]
        down_masks = [masks for masks, _ in down_s.pieces]
        down_full = [piece for _, piece in down_s.pieces]
    else:
        up_masks = down_masks = None
    g_all = jnp.concatenate([cotangent, g_pair, g_side, g_cross], 0)
    g_send, g_keep = halves(g_all, pick_cols)
    a_send, a_keep = halves(normed, pick_cols)
    (other, g_all, g_send, g_keep, a_send, a_keep), up_full = phase(
        (other, g_all, g_send, g_keep, a_send, a_keep), up_full
    )

    ffn_in, unit2, cols = middle(
        keep, got, other, tokens, x_pair, b_out, post_gain, post_bias, ln2_gain, ln2_bias
    )
    ffn_rest = swap(ffn_in, "tensor", 1)
    active_k, slope_k, stats_k, up_w = ffn_one(ffn_in, order_dp, up_masks, up_full, b_up_here)
    active_s, slope_s, stats_s, _ = ffn_one(ffn_rest, order_dp, None, [up_w], b_up_here)
    inner_grad, stats, down_w = ffn_grad(
        g_all, order_dp, down_masks, down_full, active_k, active_s, stats_k, stats_s, gain_here
    )
    stats = [stats] + [swap(stats, "tensor", mask) for mask in (1, 2, 3)]
    inner, grad_before, send, keep, ffn_sums = ffn_two(
        active_k, active_s, slope_k, slope_s, inner_grad, stats, gain_here, shift_here, up_w
    )

    got = swap(send, "tensor", 1)
    low = (keep + got.astype(F32)).astype(BF16)
    inner, grad_before, low = phase(inner, grad_before, low)
    other = swap(low, "tensor", 2)
    down_g = Scatter(dot(inner, g_send, 0, 0).astype(BF16), dot(inner, g_keep, 0, 0), pick_cols, shard)
    f_send, f_keep = halves(jnp.concatenate([ffn_in, ffn_rest], 0), pick_cols)
    up_g = Scatter(
        dot(f_send, grad_before, 0, 0).astype(BF16), dot(f_keep, grad_before, 0, 0), pick_rows, shard
    )
    other, down_g.total = phase(other, down_g.total)

    grad_proj, grad_hidden, middle_sums = middle_back(
        keep, got, other, cotangent, g_pair, tokens, x_pair, unit2, cols, post_gain, post_bias,
        ln2_gain,
    )
    proj_rest = swap(grad_proj, "tensor", 1)
    down_g.step()
    grad_proj, proj_rest = phase(grad_proj, proj_rest)

    grad_qkv, sums = attend_back(
        place, qkv, grad_proj, proj_rest, out_w, mixed, lse, seg_col, seg_row, scale_row
    )
    grad_qkv, sums, grad_proj, proj_rest, inner, up_g.total, down_g.total = phase(
        grad_qkv, sums, grad_proj, proj_rest, inner, up_g.total, down_g.total
    )

    send, keep, late = normed_grad(
        here, grad_qkv, qkv_w, x_all, cols1, sums, middle_sums, ffn_sums
    )
    got = swap(send, "tensor", 1)
    other = swap((keep[rows:] + got[rows:].astype(F32)).astype(BF16), "tensor", 2)
    qkv_g = Scatter(
        dot(a_send, grad_qkv, 0, 0).astype(BF16), dot(a_keep, grad_qkv, 0, 0), pick_rows, shard
    )
    late = sum_everywhere(late)
    input_grad = last(keep, got, other, tokens, cols1, ln1_gain, grad_hidden)
    p_send, p_keep = halves(jnp.concatenate([grad_proj, proj_rest], 0), pick_cols)
    out_g = Scatter(
        dot(scaled, p_send, 0, 0).astype(BF16), dot(scaled, p_keep, 0, 0), pick_cols, shard
    )
    send = dot(inner[two:], down_w).astype(BF16)
    keep = dot(inner[:two], down_w)
    got = swap(send, "tensor", 1)
    other = swap((keep[rows:] + got[rows:].astype(F32)).astype(BF16), "tensor", 2)
    output = output_rows(keep, got, other, tokens, unit2, post_gain, post_bias, b_down)
    g_qkv_w = qkv_g.finish()
    blocks = FF // D
    return (
        output,
        input_grad,
        late[0],
        late[1],
        g_qkv_w[:, :columns],
        late[2],
        g_qkv_w[:, columns : 2 * columns],
        g_qkv_w[:, 2 * columns :],
        late[3],
        jnp.sum(late[4].reshape(HEADS, HD), axis=1),
        out_g.finish(),
        late[9],
        late[7],
        late[8],
        late[5],
        late[6],
        up_g.finish(),
        late[12 : 12 + blocks].reshape(FF),
        late[12 + blocks : 12 + 2 * blocks].reshape(FF),
        late[12 + 2 * blocks : 12 + 3 * blocks].reshape(FF),
        down_g.finish(),
        late[10],
    )


def solution(mesh):
    return jax.shard_map(
        per_device,
        mesh=mesh,
        in_specs=(
            P(("dp", "tensor"), None),
            P("dp", None),
            P(),
            P(),
            P("dp", "tensor"),
            P(),
            P("dp", "tensor"),
            P("dp", "tensor"),
            P(),
            P(),
            P("tensor", "dp"),
            P(),
            P(),
            P(),
            P(),
            P(),
            P("dp", "tensor"),
            P(),
            P(),
            P(),
            P("tensor", "dp"),
            P(),
            P(("dp", "tensor"), None),
        ),
        out_specs=(
            P(("dp", "tensor"), None),
            P(("dp", "tensor"), None),
            P(),
            P(),
            P("dp", "tensor"),
            P(),
            P("dp", "tensor"),
            P("dp", "tensor"),
            P(),
            P(),
            P("tensor", "dp"),
            P(),
            P(),
            P(),
            P(),
            P(),
            P("dp", "tensor"),
            P(),
            P(),
            P(),
            P("tensor", "dp"),
            P(),
        ),
        check_vma=False,
    )
```

```python
import functools

import jax
import jax.numpy as jnp
from jax import lax
from jax.experimental import pallas as pl
from jax.experimental.pallas import tpu as pltpu
from jax.sharding import PartitionSpec as P

D = 1024
HEADS = 16
HD = 64
FF = 4096
LONGEST = 512
EPS = 1e-05
SCALE = HD ** (-0.5)
F32 = jnp.float32
BF16 = jnp.bfloat16


def dot(left, right, left_dim=1, right_dim=0):
    return lax.dot_general(
        left, right, (((left_dim,), (right_dim,)), ((), ())), preferred_element_type=F32
    )


def swap(value, axis, mask):
    size = lax.axis_size(axis)
    return lax.ppermute(value, axis, [(i, i ^ mask) for i in range(size)])


def bit_of(axis, mask):
    return (lax.axis_index(axis) // mask) % 2


def after(value, *others):
    return lax.optimization_barrier((value,) + others)[0]


def row(vector):
    return vector[None, :]


def each_rows(count, step, body):
    def one(k, carry):
        body(pl.ds(pl.multiple_of(k * step, step), step))
        return carry

    lax.fori_loop(0, count // step, one, 0)


STEP = 128


def fold(value):
    return jnp.sum(value.reshape(value.shape[0] // 8, 8, value.shape[1]), axis=0)


def norm_stats(values):
    mean = jnp.mean(values, axis=-1, keepdims=True)
    centered = values - mean
    inverse = lax.rsqrt(jnp.mean(centered * centered, axis=-1, keepdims=True) + EPS)
    return centered * inverse, inverse


def norm_backward(grad, unit, inverse, gain):
    scaled = grad * gain
    return inverse * (
        scaled
        - jnp.mean(scaled, axis=-1, keepdims=True)
        - unit * jnp.mean(scaled * unit, axis=-1, keepdims=True)
    )


VMEM = pl.BlockSpec(memory_space=pltpu.VMEM)
SMEM = pl.BlockSpec(memory_space=pltpu.SMEM)


def shaped(shape, kind):
    return jax.ShapeDtypeStruct(shape, kind)


def cost(flops, moved, hard=0):
    return pl.CostEstimate(flops=flops, bytes_accessed=moved, transcendentals=hard)


class Shards:
    def __init__(self, shard):
        self.held = {0: shard[None]}

    def send(self, mask, *which):
        for k in which:
            self.held[k ^ mask] = swap(self.held[k], "dp", mask)

    def get(self, *which):
        return [self.held[k] for k in which]

    def put(self, which, values):
        for k, value in zip(which, values):
            self.held[k] = value

    def all(self):
        masks = sorted(self.held)
        return [[k] for k in masks], [self.held[k] for k in masks]


def phase(*values):
    return lax.optimization_barrier(values)


def fill(axis, masks, order_ref, piece_refs, full_ref, start=0, width=None):
    if masks is None:
        full_ref[...] = piece_refs[0][...]
        return
    for group, piece in zip(masks, piece_refs):
        height = piece.shape[1]
        for k, mask in enumerate(group):
            place = order_ref[mask]
            if axis == 0:
                there = pl.ds(pl.multiple_of(place * height, height), height)
                full_ref[there, :] = piece[k, :, start : start + full_ref.shape[1]]
            else:
                there = pl.ds(pl.multiple_of(place * width, width), width)
                for low in range(0, full_ref.shape[0], height):
                    at = start + low // height * width
                    full_ref[low : low + height, there] = piece[k, :, at : at + width]


def pack_kernel(q_ref, k_ref, v_ref, o_ref, out_ref):
    height, width = q_ref.shape
    for k, ref in enumerate((q_ref, k_ref, v_ref)):
        out_ref[:, k * width : (k + 1) * width] = ref[...]
    wide = o_ref.shape[1]
    for k in range(o_ref.shape[0] // height):
        at = 3 * width + k * wide
        out_ref[:, at : at + wide] = o_ref[k * height : (k + 1) * height, :]


def pack(w_query, w_key, w_value, w_out):
    height, width = w_query.shape
    total = 3 * width + w_out.size // height
    return pl.pallas_call(
        pack_kernel,
        out_shape=shaped((height, total), BF16),
        in_specs=[VMEM] * 4,
        out_specs=VMEM,
        cost_estimate=cost(0, 0),
        name="pack",
    )(w_query, w_key, w_value, w_out)


def pick_cols(value, width, bit):
    rows, cols = value.shape
    pairs = cols // (2 * width)
    if width % 128:
        return lax.dynamic_index_in_dim(
            value.reshape(rows, pairs, 2, width), bit, 2, keepdims=False
        ).reshape(rows, pairs * width)
    return jnp.concatenate(
        [
            lax.dynamic_slice_in_dim(value, (2 * p + bit) * width, width, 1)
            for p in range(pairs)
        ],
        1,
    )


def pick_rows(value, height, bit):
    rows, cols = value.shape
    return lax.dynamic_index_in_dim(
        value.reshape(rows // (2 * height), 2, height, cols), bit, 1, keepdims=False
    ).reshape(rows // 2, cols)


def dp_masks(first):
    size = lax.axis_size("dp")
    masks = [1 << k for k in range(size.bit_length() - 1)]
    if first in masks:
        masks.remove(first)
        masks.insert(0, first)
    return masks


def outer_kernel(width, on_left, count, bit_ref, *refs):
    parts, (other_ref, send_ref, keep_ref, *picks) = refs[:count], refs[count:]

    @pl.when(pl.program_id(0) == 0)
    def _():
        for bit, pick_ref in zip((1 - bit_ref[0], bit_ref[0]), picks):
            for p in range(pick_ref.shape[1] // width):
                there = pl.ds(pl.multiple_of((2 * p + bit) * width, width), width)
                row = 0
                for part in parts:
                    pick_ref[row : row + part.shape[0], p * width : (p + 1) * width] = part[:, there]
                    row += part.shape[0]

    for pick_ref, out_ref in zip(picks, (send_ref, keep_ref)):
        if on_left:
            value = dot(pick_ref[...], other_ref[...], 0, 0)
        else:
            value = dot(other_ref[...], pick_ref[...], 0, 0)
        out_ref[...] = value.astype(out_ref.dtype)


def outer(bit, picked, other, width, on_left):
    rows, cols = other.shape
    half = picked[0].shape[1] // 2
    step = min(256, cols // 2)
    shape = (half, cols) if on_left else (cols, half)
    tile = (half, step) if on_left else (step, half)
    out = pl.BlockSpec(tile, (lambda i: (0, i)) if on_left else (lambda i: (i, 0)))
    return pl.pallas_call(
        functools.partial(outer_kernel, width, on_left, len(picked)),
        grid=(cols // step,),
        out_shape=(shaped(shape, BF16), shaped(shape, F32)),
        in_specs=[SMEM] + [VMEM] * len(picked) + [pl.BlockSpec((rows, step), lambda i: (0, i))],
        out_specs=(out,) * 2,
        scratch_shapes=[pltpu.VMEM((rows, half), BF16)] * 2,
        cost_estimate=cost(0, 0),
        name="outer",
    )(bit, *picked, other)


def split_kernel(axis, width, bit_ref, keep_ref, got_ref, send_ref, stay_ref):
    for bit, out_ref in ((1 - bit_ref[0], send_ref), (bit_ref[0], stay_ref)):
        for p in range(out_ref.shape[axis] // width):
            there = pl.ds(pl.multiple_of((2 * p + bit) * width, width), width)
            here = slice(p * width, (p + 1) * width)
            source, target = ((there, slice(None)), (here, slice(None)))
            if axis == 1:
                source, target = source[::-1], target[::-1]
            value = keep_ref[source] + got_ref[source].astype(F32)
            out_ref[target] = value.astype(out_ref.dtype)


def split(bit, keep, got, width, axis):
    cut = lambda shape: tuple(size // 2 if k == axis else size for k, size in enumerate(shape))
    step = keep.shape[1 - axis] // 2
    tile = tuple(size if k == axis else step for k, size in enumerate(keep.shape))
    index = (lambda i: (0, i)) if axis == 0 else (lambda i: (i, 0))
    return pl.pallas_call(
        functools.partial(split_kernel, axis, width),
        grid=(2,),
        out_shape=(shaped(cut(keep.shape), BF16), shaped(cut(keep.shape), F32)),
        in_specs=[SMEM, pl.BlockSpec(tile, index), pl.BlockSpec(tile, index)],
        out_specs=(pl.BlockSpec(cut(tile), index),) * 2,
        cost_estimate=cost(0, 0),
        name="split",
    )(bit, keep, got)


class Scatter:
    def __init__(self, axis, extent, first):
        self.axis, self.extent, self.masks = axis, extent, dp_masks(first)

    def place(self):
        mask = self.masks[0]
        lower = sum(1 for other in self.masks if other < mask)
        return bit_of("dp", mask), self.extent << lower

    def product(self, picked, other):
        bit, width = self.place()
        if width % 128 == 0:
            send, self.keep = outer(jnp.full((1,), bit, jnp.int32), picked, other, width, self.axis == 0)
            return send
        picked = jnp.concatenate(picked, 0)
        send, keep = pick_cols(picked, width, 1 - bit), pick_cols(picked, width, bit)
        if self.axis == 0:
            send, self.keep = dot(send, other, 0, 0), dot(keep, other, 0, 0)
        else:
            send, self.keep = dot(other, send, 0, 0), dot(other, keep, 0, 0)
        return send.astype(BF16)

    def start(self, send):
        self.got = swap(send, "dp", self.masks.pop(0))

    def split(self):
        bit, width = self.place()
        if width % 128 == 0:
            send, self.keep = split(jnp.full((1,), bit, jnp.int32), self.keep, self.got, width, self.axis)
            return send
        pick = (pick_rows, pick_cols)[self.axis]
        total = self.keep + self.got.astype(F32)
        self.keep = pick(total, width, bit)
        return pick(total, width, 1 - bit).astype(BF16)

    def finish(self):
        while self.masks:
            self.start(self.split())
        return self.keep + self.got.astype(F32)


def low_kernel(keep_ref, got_ref, out_ref):
    out_ref[...] = (keep_ref[...] + got_ref[...].astype(F32)).astype(BF16)


def low_rows(keep, got, rows):
    total, width = keep.shape
    step = rows // 2
    first = (total - rows) // step
    there = pl.BlockSpec((step, width), lambda i: (i + first, 0))
    return pl.pallas_call(
        low_kernel,
        grid=(rows // step,),
        out_shape=shaped((rows, width), BF16),
        in_specs=[there, there],
        out_specs=pl.BlockSpec((step, width), lambda i: (i, 0)),
        cost_estimate=cost(0, 0),
        name="low_rows",
    )(keep, got)


def stack_kernel(*refs):
    *parts, out_ref = refs
    row = 0
    for part in parts:
        out_ref[row : row + part.shape[0], :] = part[...]
        row += part.shape[0]


def stack(*parts):
    return pl.pallas_call(
        stack_kernel,
        out_shape=shaped((sum(part.shape[0] for part in parts), parts[0].shape[1]), parts[0].dtype),
        in_specs=[VMEM] * len(parts),
        out_specs=VMEM,
        cost_estimate=cost(0, 0),
        name="stack",
    )(*parts)


def project_kernel(inner_ref, weight_ref, send_ref, keep_ref):
    half = inner_ref.shape[0] // 2
    send_ref[...] = dot(inner_ref[half:, :], weight_ref[...]).astype(BF16)
    keep_ref[...] = dot(inner_ref[:half, :], weight_ref[...])


def project(inner, weight):
    half = inner.shape[0] // 2
    return pl.pallas_call(
        project_kernel,
        out_shape=(shaped((half, D), BF16), shaped((half, D), F32)),
        in_specs=[VMEM] * 2,
        out_specs=(VMEM,) * 2,
        cost_estimate=cost(0, 0),
        name="project",
    )(inner, weight)


def norm_one_kernel(a_ref, b_ref, c_ref, d_ref, gain_ref, bias_ref, out_ref, all_ref, cols_ref):
    step = pl.program_id(0)
    per = pl.num_programs(0) // 4
    value = jnp.where(
        step < 2 * per,
        jnp.where(step < per, a_ref[...], b_ref[...]),
        jnp.where(step < 3 * per, c_ref[...], d_ref[...]),
    )
    all_ref[...] = value
    value = value.astype(F32)
    mean = jnp.mean(value, axis=-1, keepdims=True)
    centered = value - mean
    inverse = lax.rsqrt(jnp.mean(centered * centered, axis=-1, keepdims=True) + EPS)
    lane = lax.broadcasted_iota(jnp.int32, cols_ref.shape, 1)
    cols_ref[...] = jnp.where(lane == 0, mean, inverse)
    out_ref[...] = (centered * inverse * gain_ref[...] + bias_ref[...]).astype(BF16)


def norm_one(parts, gain, bias):
    rows, width = parts[0].shape
    per = rows // STEP

    def spec(first, count, width=width):
        return pl.BlockSpec((STEP, width), lambda i: (jnp.clip(i - first, 0, count - 1), 0))

    return pl.pallas_call(
        norm_one_kernel,
        grid=(4 * per,),
        out_shape=(
            shaped((4 * rows, width), BF16),
            shaped((4 * rows, width), BF16),
            shaped((4 * rows, 128), F32),
        ),
        in_specs=[spec(k * per, per) for k in range(4)] + [VMEM, VMEM],
        out_specs=(spec(0, 4 * per), spec(0, 4 * per), spec(0, 4 * per, 128)),
        cost_estimate=cost(0, 0),
        name="norm_one",
    )(*parts, row(gain), row(bias))


def key_range(block, size):
    low = max(0, block * size - (LONGEST // size) * size)
    return low, (block + 1) * size - low


def write_bias(bias_ref, seg_col_ref, seg_row_ref, block, size):
    low, count = key_range(block, size)
    key_pos = low + lax.broadcasted_iota(jnp.int32, (count, size), 0)
    row_pos = block * size + lax.broadcasted_iota(jnp.int32, (count, size), 1)
    same = seg_col_ref[low : low + count, :] == seg_row_ref[:, block * size : (block + 1) * size]
    bias_ref[:count, :] = jnp.where((key_pos <= row_pos) & same, 0.0, -1000000000.0)


def attend_kernel(size, masks, place_ref, order_ref, normed_ref, qkv_b_ref, seg_col_ref, seg_row_ref,
                  scale_ref, *refs):
    *pieces, qkv_ref, o_ref, u_ref, lse_ref, qkv_w_ref, out_w_ref, send_ref, keep_ref = refs[:-3]
    bias_ref, vt_ref, ot_ref = refs[-3:]
    length, width = o_ref.shape
    heads = width // HD
    if masks is None:
        qkv_w_ref[...] = pieces[0][...]
        out_w_ref[...] = pieces[1][...]
    else:
        fill(0, masks, order_ref, pieces, qkv_w_ref)
        fill(1, masks, order_ref, pieces, out_w_ref, 3 * width, pieces[0].shape[1])
    head_of = lax.broadcasted_iota(jnp.int32, (size, width), 1) // HD
    for block in range(length // size):
        rows = slice(block * size, (block + 1) * size)
        here = pl.ds(pl.multiple_of(place_ref[block] * size, size), size)
        product = dot(normed_ref[here, :], qkv_w_ref[...]) + qkv_b_ref[...]
        qkv_ref[rows, :] = product.astype(BF16)
        vt_ref[:, rows] = product[:, 2 * width :].T.astype(BF16)
        low, count = key_range(block, size)
        write_bias(bias_ref, seg_col_ref, seg_row_ref, block, size)
        query = qkv_ref[rows, :width].astype(F32) * SCALE
        keys = qkv_ref[low : low + count, width : 2 * width]
        for head in range(heads):
            masked = jnp.where(head_of == head, query, 0.0).astype(BF16)
            scores = dot(keys, masked, 1, 1) + bias_ref[:count, :]
            highest = jnp.max(scores, axis=0, keepdims=True)
            raised = jnp.exp(scores - highest)
            total = jnp.sum(raised, axis=0, keepdims=True)
            lse_ref[block * heads + head : block * heads + head + 1, :] = highest + jnp.log(total)
            probs = (raised * (1.0 / total)).astype(BF16)
            part = slice(head * HD, (head + 1) * HD)
            ot_ref[part, :] = dot(vt_ref[part, low : low + count], probs)
        mixed = ot_ref[...].T
        o_ref[rows, :] = mixed
        u_ref[here, :] = (mixed * scale_ref[...]).astype(BF16)
    half = length // 2
    send_ref[...] = dot(u_ref[half:, :], out_w_ref[...]).astype(BF16)
    keep_ref[...] = dot(u_ref[:half, :], out_w_ref[...])


def attend_back_kernel(size, place_ref, qkv_ref, own_ref, rest_ref, out_w_ref, o_ref, lse_ref,
                       seg_col_ref, seg_row_ref, scale_ref, dqkv_ref, sums_ref,
                       bias_ref, kt_ref, dqt_ref, probs_ref, ds_ref, q_ref, do_ref, dk_ref, dv_ref,
                       du_ref):
    length, width = o_ref.shape
    heads = width // HD
    du_ref[: length // 2, :] = dot(own_ref[...], out_w_ref[...], 1, 1)
    du_ref[length // 2 :, :] = dot(rest_ref[...], out_w_ref[...], 1, 1)
    kt_ref[...] = qkv_ref[:, width : 2 * width].astype(F32).T.astype(BF16)
    head_of = lax.broadcasted_iota(jnp.int32, (size, width), 1) // HD
    scale_sum = jnp.zeros((1, width), F32)
    q_sum = jnp.zeros((1, width), F32)
    v_sum = jnp.zeros((1, width), F32)
    blocks = length // size
    for block in range(blocks):
        low, count = key_range(block, size)
        rows = slice(block * size, (block + 1) * size)
        here = pl.ds(pl.multiple_of(place_ref[block] * size, size), size)
        write_bias(bias_ref, seg_col_ref, seg_row_ref, block, size)
        query = qkv_ref[rows, :width].astype(F32) * SCALE
        keys = qkv_ref[low : low + count, width : 2 * width]
        values = qkv_ref[low : low + count, 2 * width :]
        du = du_ref[here, :]
        scale_sum = scale_sum + jnp.sum(du * o_ref[rows, :], axis=0, keepdims=True)
        grad = du * scale_ref[...]
        for head in range(heads):
            masked = jnp.where(head_of == head, query, 0.0).astype(BF16)
            grad_here = jnp.where(head_of == head, grad, 0.0).astype(BF16)
            stack = slice(head * size, (head + 1) * size)
            q_ref[stack, :] = masked
            do_ref[stack, :] = grad_here
            scores = dot(keys, masked, 1, 1) + bias_ref[:count, :]
            full = jnp.exp(scores - lse_ref[block * heads + head : block * heads + head + 1, :])
            probs_ref[:count, stack] = full.astype(BF16)
            dp = dot(values, grad_here, 1, 1)
            delta = jnp.sum(full * dp, axis=0, keepdims=True)
            ds = (full * (dp - delta)).astype(BF16)
            ds_ref[:count, stack] = ds
            part = slice(head * HD, (head + 1) * HD)
            dqt_ref[part, :] = dot(kt_ref[part, low : low + count], ds)
        dq = (dqt_ref[...].T * SCALE).astype(BF16)
        dqkv_ref[here, :width] = dq
        q_sum = q_sum + jnp.sum(dq.astype(F32), axis=0, keepdims=True)
        dk = dot(ds_ref[:count, :], q_ref[...])
        dv = dot(probs_ref[:count, :], do_ref[...])
        old = count - size
        if old:
            dk_ref[low : low + old, :] += dk[:old]
            dv_ref[low : low + old, :] += dv[:old]
        dk_ref[rows, :] = dk[old:]
        dv_ref[rows, :] = dv[old:]
    for block in range(blocks):
        rows = slice(block * size, (block + 1) * size)
        here = pl.ds(pl.multiple_of(place_ref[block] * size, size), size)
        dqkv_ref[here, width : 2 * width] = dk_ref[rows, :].astype(BF16)
        dv = dv_ref[rows, :].astype(BF16)
        dqkv_ref[here, 2 * width :] = dv
        v_sum = v_sum + jnp.sum(dv.astype(F32), axis=0, keepdims=True)
    sums_ref[...] = jnp.concatenate(
        [q_sum, v_sum, scale_sum, jnp.zeros((5, width), F32)], axis=0
    )


def attend(place, order, normed, masks, pieces, qkv_b, seg_col, seg_row, scale_row):
    length, width = normed.shape[0], scale_row.shape[1]
    size = length // 4
    heads = width // HD
    most = LONGEST + size
    return pl.pallas_call(
        functools.partial(attend_kernel, size, masks),
        out_shape=(
            shaped((length, 3 * width), BF16),
            shaped((length, width), F32),
            shaped((length, width), BF16),
            shaped((4 * heads, size), F32),
            shaped((D, 3 * width), BF16),
            shaped((width, D), BF16),
            shaped((length // 2, D), BF16),
            shaped((length // 2, D), F32),
        ),
        in_specs=[SMEM] * 2 + [VMEM] * (5 + len(pieces)),
        out_specs=(VMEM,) * 8,
        scratch_shapes=[
            pltpu.VMEM((most, size), F32),
            pltpu.VMEM((width, length), BF16),
            pltpu.VMEM((width, size), F32),
        ],
        cost_estimate=cost(0, 0),
        name="attend",
    )(place, order, normed, qkv_b, seg_col, seg_row, scale_row, *pieces)


def attend_back(place, qkv, own, rest, out_w, mixed, lse, seg_col, seg_row, scale_row):
    length, width = mixed.shape
    size = length // 4
    heads = width // HD
    most = LONGEST + size
    pairs = 4 * heads * most * size
    return pl.pallas_call(
        functools.partial(attend_back_kernel, size),
        out_shape=(shaped((length, 3 * width), BF16), shaped((8, width), F32)),
        in_specs=[SMEM] + [VMEM] * 9,
        out_specs=(VMEM,) * 2,
        scratch_shapes=[
            pltpu.VMEM((most, size), F32),
            pltpu.VMEM((width, length), BF16),
            pltpu.VMEM((width, size), F32),
            pltpu.VMEM((most, heads * size), BF16),
            pltpu.VMEM((most, heads * size), BF16),
            pltpu.VMEM((heads * size, width), BF16),
            pltpu.VMEM((heads * size, width), BF16),
            pltpu.VMEM((length, width), F32),
            pltpu.VMEM((length, width), F32),
            pltpu.VMEM((length, width), F32),
        ],
        cost_estimate=cost(0, 0),
        name="attend_back",
    )(place, qkv, own, rest, out_w, mixed, lse, seg_col, seg_row, scale_row)


def middle_kernel(keep_ref, got_ref, other_ref, mine_ref, pair_ref, b_out_ref, post_g_ref, post_b_ref,
                  ln2_g_ref, ln2_b_ref, ffn_in_ref, unit2_ref, cols_ref):
    first = pl.program_id(0) < pl.num_programs(0) // 2
    tokens = jnp.where(first, mine_ref[...], pair_ref[...]).astype(F32)
    part = keep_ref[...] + got_ref[...].astype(F32)
    projected = part + other_ref[...].astype(F32) + b_out_ref[...]
    unit2, inv2 = norm_stats(projected)
    unit2_ref[...] = unit2
    hidden = tokens + (unit2 * post_g_ref[...] + post_b_ref[...])
    mean3 = jnp.mean(hidden, axis=-1, keepdims=True)
    centered = hidden - mean3
    inv3 = lax.rsqrt(jnp.mean(centered * centered, axis=-1, keepdims=True) + EPS)
    ffn_in_ref[...] = (centered * inv3 * ln2_g_ref[...] + ln2_b_ref[...]).astype(BF16)
    lane = lax.broadcasted_iota(jnp.int32, cols_ref.shape, 1)
    cols_ref[...] = jnp.where(lane == 0, inv2, jnp.where(lane == 1, mean3, inv3))


def pair_specs(rows, width):
    half = rows // 2 // STEP
    straight = pl.BlockSpec((STEP, width), lambda i: (i, 0))
    crossed = pl.BlockSpec((STEP, width), lambda i: ((i + half) % (2 * half), 0))
    mine = pl.BlockSpec((STEP, width), lambda i: (jnp.minimum(i, half - 1), 0))
    theirs = pl.BlockSpec((STEP, width), lambda i: (jnp.maximum(i - half, 0), 0))
    return straight, crossed, mine, theirs


def middle(keep, got, other, mine, pair, b_out, post_gain, post_bias, ln2_gain, ln2_bias):
    rows, width = keep.shape
    straight, crossed, own, theirs = pair_specs(rows, width)
    columns = pl.BlockSpec((STEP, 128), lambda i: (i, 0))
    return pl.pallas_call(
        middle_kernel,
        grid=(rows // STEP,),
        out_shape=(
            shaped((rows, width), BF16),
            shaped((rows, width), F32),
            shaped((rows, 128), F32),
        ),
        in_specs=[straight, straight, crossed, own, theirs] + [VMEM] * 5,
        out_specs=(straight, straight, columns),
        cost_estimate=cost(0, 0),
        name="middle",
    )(keep, got, other, mine, pair, row(b_out), row(post_gain), row(post_bias), row(ln2_gain),
      row(ln2_bias))


def middle_back_kernel(keep_ref, got_ref, other_ref, mine_ref, pair_ref, tokens_ref, tokens2_ref,
                       unit2_ref, cols_ref, post_g_ref, post_b_ref, ln2_g_ref, proj_ref, grad_ref, sums_ref,
                       acc_ref):
    step = pl.program_id(0)
    half = pl.num_programs(0) // 2
    first = step < half

    @pl.when(step == 0)
    def _():
        acc_ref[...] = jnp.zeros_like(acc_ref)

    part = keep_ref[...] + got_ref[...].astype(F32)
    incoming = part + other_ref[...].astype(F32)
    tokens = jnp.where(first, tokens_ref[...], tokens2_ref[...]).astype(F32)
    unit2 = unit2_ref[...]
    inv2, mean3, inv3 = (cols_ref[:, k : k + 1] for k in range(3))
    hidden = tokens + (unit2 * post_g_ref[...] + post_b_ref[...])
    unit3 = (hidden - mean3) * inv3
    outgoing = jnp.where(first, mine_ref[...], pair_ref[...]).astype(F32)
    grad = outgoing + norm_backward(incoming, unit3, inv3, ln2_g_ref[...])
    proj = norm_backward(grad, unit2, inv2, post_g_ref[...]).astype(BF16)
    proj_ref[...] = proj

    @pl.when(first)
    def _():
        grad_ref[...] = grad
        for k, value in enumerate(
            (incoming * unit3, incoming, grad * unit2, grad, proj.astype(F32), outgoing)
        ):
            acc_ref[8 * k : 8 * k + 8, :] += fold(value)

    @pl.when(step == half - 1)
    def _():
        sums_ref[...] = jnp.concatenate(
            [jnp.sum(acc_ref[8 * k : 8 * k + 8, :], axis=0, keepdims=True) for k in range(6)]
            + [jnp.zeros((2, acc_ref.shape[1]), F32)],
            axis=0,
        )


def middle_back(keep, got, other, mine, pair, tokens, tokens2, unit2, cols, post_gain, post_bias,
                ln2_gain):
    rows, width = keep.shape
    straight, crossed, own, theirs = pair_specs(rows, width)
    columns = pl.BlockSpec((STEP, 128), lambda i: (i, 0))
    return pl.pallas_call(
        middle_back_kernel,
        grid=(rows // STEP,),
        out_shape=(
            shaped((rows, width), BF16),
            shaped((rows // 2, width), F32),
            shaped((8, width), F32),
        ),
        in_specs=[straight, straight, crossed, own, theirs, own, theirs, straight, columns] + [VMEM] * 3,
        out_specs=(straight, own, VMEM),
        scratch_shapes=[pltpu.VMEM((48, width), F32)],
        cost_estimate=cost(0, 0),
        name="middle_back",
    )(keep, got, other, mine, pair, tokens, tokens2, unit2, cols, row(post_gain), row(post_bias),
      row(ln2_gain))


def ffn_one_kernel(masks, order_ref, in_ref, b_up_ref, *refs):
    *pieces, active_ref, slope_ref, stats_ref, up_ref, cols_ref = refs

    @pl.when(pl.program_id(0) == 0)
    def _():
        fill(0, masks, order_ref, pieces, up_ref)

    active_ref[...] = dot(in_ref[...], up_ref[...]) + b_up_ref[...]
    lane = lax.broadcasted_iota(jnp.int32, (STEP, 128), 1)

    def body(rows):
        before = active_ref[rows, :]
        cdf = 0.5 * (1.0 + lax.erf(before * 0.7071067811865476))
        active = before * cdf
        density = jnp.exp(-0.5 * before * before) * 0.3989422804014327
        slope_ref[rows, :] = cdf + before * density
        active_ref[rows, :] = active
        mean = jnp.mean(active, axis=-1, keepdims=True)
        off = active - mean
        square = jnp.sum(off * off, axis=-1, keepdims=True)
        cols_ref[rows, :] = jnp.where(lane == 0, mean, square)

    each_rows(active_ref.shape[0], STEP, body)
    stats_ref[...] = cols_ref[...].T[:8, :]


def ffn_one(ffn_in, order, masks, pieces, b_up):
    rows, width = ffn_in.shape[0], b_up.shape[0]
    size = 256
    tile = pl.BlockSpec((size, width), lambda i: (i, 0))
    return pl.pallas_call(
        functools.partial(ffn_one_kernel, masks),
        grid=(rows // size,),
        out_shape=(
            shaped((rows, width), F32),
            shaped((rows, width), F32),
            shaped((8, rows), F32),
            shaped((D, width), BF16),
        ),
        in_specs=[SMEM, pl.BlockSpec((size, D), lambda i: (i, 0)), VMEM] + [VMEM] * len(pieces),
        out_specs=(tile, tile, pl.BlockSpec((8, size), lambda i: (0, i)), VMEM),
        scratch_shapes=[pltpu.VMEM((size, 128), F32)],
        cost_estimate=cost(0, 0),
        name="ffn_one",
    )(order, ffn_in, row(b_up), *pieces)


def ffn_grad_kernel(masks, order_ref, grad_ref, keep_ref, send_ref, stats_k_ref, stats_s_ref, gain_ref,
                    *refs):
    *pieces, inner_ref, stats_ref, down_ref, cols_ref = refs
    step = pl.program_id(0)
    first = step < pl.num_programs(0) // 2

    @pl.when(step == 0)
    def _():
        fill(1, masks, order_ref, pieces, down_ref, 0, pieces[0].shape[-1])

    inner_ref[...] = dot(grad_ref[...], down_ref[...], 1, 1)
    lane = lax.broadcasted_iota(jnp.int32, (STEP, 128), 1)

    def body(rows):
        active = jnp.where(first, keep_ref[rows, :], send_ref[rows, :])
        scaled = inner_ref[rows, :] * gain_ref[...]
        plain = jnp.sum(scaled, axis=-1, keepdims=True)
        cross = jnp.sum(scaled * active, axis=-1, keepdims=True)
        cols_ref[rows, :] = jnp.where(lane == 2, plain, cross)

    each_rows(inner_ref.shape[0], STEP, body)
    stats = jnp.where(first, stats_k_ref[...], stats_s_ref[...])
    index = lax.broadcasted_iota(jnp.int32, stats.shape, 0)
    stats_ref[...] = jnp.where(index < 2, stats, cols_ref[...].T[:8, :])


def ffn_grad(grad, order, masks, pieces, active_k, active_s, stats_k, stats_s, gain):
    rows, width = grad.shape[0], gain.shape[0]
    size = 256
    half = rows // size // 2
    keep = lambda i: jnp.minimum(i, half - 1)
    send = lambda i: jnp.maximum(i - half, 0)
    tile = (size, width)
    return pl.pallas_call(
        functools.partial(ffn_grad_kernel, masks),
        grid=(rows // size,),
        out_shape=(
            shaped((rows, width), F32),
            shaped((8, rows), F32),
            shaped((width, D), BF16),
        ),
        in_specs=[
            SMEM,
            pl.BlockSpec((size, D), lambda i: (i, 0)),
            pl.BlockSpec(tile, lambda i: (keep(i), 0)),
            pl.BlockSpec(tile, lambda i: (send(i), 0)),
            pl.BlockSpec((8, size), lambda i: (0, keep(i))),
            pl.BlockSpec((8, size), lambda i: (0, send(i))),
            VMEM,
        ]
        + [VMEM] * len(pieces),
        out_specs=(
            pl.BlockSpec(tile, lambda i: (i, 0)),
            pl.BlockSpec((8, size), lambda i: (0, i)),
            VMEM,
        ),
        scratch_shapes=[pltpu.VMEM((size, 128), F32)],
        cost_estimate=cost(0, 0),
        name="ffn_grad",
    )(order, grad, active_k, active_s, stats_k, stats_s, row(gain), *pieces)


def ffn_two_kernel(mk_ref, ms_ref, sk_ref, ss_ref, grad_ref, s0_ref, s1_ref, s2_ref, s3_ref, gain_ref,
                   shift_ref, up_ref, inner_ref, before_ref, send_ref, keep_ref, sums_ref, cols_ref,
                   acc_ref):
    step = pl.program_id(0)
    half = pl.num_programs(0) // 2
    count, width = inner_ref.shape

    @pl.when(step == 0)
    def _():
        acc_ref[...] = jnp.zeros_like(acc_ref)

    values = [ref[...] for ref in (s0_ref, s1_ref, s2_ref, s3_ref)]
    mean = 0.25 * ((values[0][0:1] + values[1][0:1]) + (values[2][0:1] + values[3][0:1]))
    square = plain = cross = jnp.zeros_like(mean)
    for value in values:
        gap = value[0:1] - mean
        square = square + (value[1:2] + width * (gap * gap))
        plain = plain + value[2:3]
        cross = cross + value[3:4]
    inverse = lax.rsqrt(square / FF + EPS)
    cross = (cross - mean * plain) * inverse
    table = jnp.concatenate(
        [mean, inverse, plain / FF, cross / FF, jnp.zeros((124, count), F32)], axis=0
    )
    cols_ref[...] = table.T

    def work(active_ref, slope_ref, out_ref):
        def body(rows):
            cols = cols_ref[rows, :]
            mean, inverse, plain, cross = (cols[:, k : k + 1] for k in range(4))
            unit = (active_ref[rows, :] - mean) * inverse
            inner_ref[rows, :] = (unit * gain_ref[...] + shift_ref[...]).astype(BF16)
            grad = grad_ref[rows, :]
            moved = inverse * (grad * gain_ref[...] - plain - unit * cross)
            before = (moved * slope_ref[rows, :]).astype(BF16)
            before_ref[rows, :] = before
            for k, value in enumerate((before.astype(F32), grad * unit, grad)):
                acc_ref[8 * k : 8 * k + 8, :] += fold(value)

        each_rows(count, STEP, body)
        out_ref[...] = dot(before_ref[...], up_ref[...], 1, 1).astype(out_ref.dtype)

    @pl.when(step < half)
    def _():
        work(ms_ref, ss_ref, send_ref)

    @pl.when(step >= half)
    def _():
        work(mk_ref, sk_ref, keep_ref)

    @pl.when(step == 2 * half - 1)
    def _():
        sums_ref[...] = jnp.concatenate(
            [jnp.sum(acc_ref[8 * k : 8 * k + 8, :], axis=0, keepdims=True) for k in range(3)]
            + [jnp.zeros((5, width), F32)],
            axis=0,
        )


def ffn_two(active_k, active_s, slope_k, slope_s, inner_grad, stats, gain, shift, up_w):
    rows, width = active_k.shape
    size = 256
    half = rows // size
    keep = lambda i: jnp.maximum(i - half, 0)
    send = lambda i: jnp.minimum(i, half - 1)
    keep_spec = lambda shape: pl.BlockSpec(shape, lambda i: (keep(i), 0))
    send_spec = lambda shape: pl.BlockSpec(shape, lambda i: (send(i), 0))
    tile = (size, width)
    block = lambda i: (i + half) % (2 * half)
    both = pl.BlockSpec(tile, lambda i: (block(i), 0))
    held = (lambda b: b, lambda b: (b + 2) % 4, lambda b: b + 1 - 2 * (b % 2), lambda b: 3 - b)
    return pl.pallas_call(
        ffn_two_kernel,
        grid=(2 * half,),
        out_shape=(
            shaped((2 * rows, width), BF16),
            shaped((2 * rows, width), BF16),
            shaped((rows, D), BF16),
            shaped((rows, D), F32),
            shaped((8, width), F32),
        ),
        in_specs=[keep_spec(tile), send_spec(tile), keep_spec(tile), send_spec(tile), both]
        + [pl.BlockSpec((8, size), lambda i, at=at: (0, at(block(i)))) for at in held]
        + [VMEM] * 3,
        out_specs=(both, both, send_spec((size, D)), keep_spec((size, D)), VMEM),
        scratch_shapes=[pltpu.VMEM((size, 128), F32), pltpu.VMEM((24, width), F32)],
        cost_estimate=cost(0, 0),
        name="ffn_two",
    )(active_k, active_s, slope_k, slope_s, inner_grad, *stats, row(gain), row(shift), up_w)


def normed_grad_kernel(side_ref, grad_ref, weight_ref, all_ref, cols_ref, sums_ref, middle_ref, ffn_ref,
                       send_ref, keep_ref, late_ref, acc_ref):
    step = pl.program_id(0)
    half = pl.num_programs(0) // 2
    width = late_ref.shape[1]

    @pl.when(step == 0)
    def _():
        acc_ref[...] = jnp.zeros_like(acc_ref)

    grad = dot(grad_ref[...], weight_ref[...], 1, 1)
    unit = (all_ref[...].astype(F32) - cols_ref[:, 0:1]) * cols_ref[:, 1:2]
    for k, value in enumerate((grad * unit, grad)):
        acc_ref[8 * k : 8 * k + 8, :] += fold(value)

    @pl.when(step < half)
    def _():
        send_ref[...] = grad.astype(BF16)

    @pl.when(step >= half)
    def _():
        keep_ref[...] = grad

    @pl.when(step == 2 * half - 1)
    def _():
        here = side_ref[0]
        wide = [
            jnp.concatenate(
                [jnp.where(here == k, sums_ref[r : r + 1, :], 0.0) for k in range(4)], axis=1
            )
            for r in range(3)
        ]
        place = lax.broadcasted_iota(jnp.int32, (4, width), 0) == here
        late_ref[...] = jnp.concatenate(
            [jnp.sum(acc_ref[8 * k : 8 * k + 8, :], axis=0, keepdims=True) for k in range(2)]
            + wide
            + [middle_ref[0:6, :], jnp.zeros((1, width), F32)]
            + [jnp.where(place, ffn_ref[k : k + 1, :], 0.0) for k in range(3)],
            axis=0,
        )


def normed_grad(here, grad_qkv, qkv_w, x_all, cols, sums, middle_sums, ffn_sums):
    length, width = x_all.shape
    size = 256
    half = length // size // 2
    block = lambda i: ((i + half) % (2 * half), 0)
    return pl.pallas_call(
        normed_grad_kernel,
        grid=(2 * half,),
        out_shape=(
            shaped((length // 2, width), BF16),
            shaped((length // 2, width), F32),
            shaped((24, width), F32),
        ),
        in_specs=[
            SMEM,
            pl.BlockSpec((size, grad_qkv.shape[1]), block),
            VMEM,
            pl.BlockSpec((size, width), block),
            pl.BlockSpec((size, 128), block),
            VMEM,
            VMEM,
            VMEM,
        ],
        out_specs=(
            pl.BlockSpec((size, width), lambda i: (jnp.minimum(i, half - 1), 0)),
            pl.BlockSpec((size, width), lambda i: (jnp.maximum(i - half, 0), 0)),
            VMEM,
        ),
        scratch_shapes=[pltpu.VMEM((16, width), F32)],
        cost_estimate=cost(0, 0),
        name="normed_grad",
    )(here, grad_qkv, qkv_w, x_all, cols, sums, middle_sums, ffn_sums)


def last_kernel(keep_ref, got_ref, other_ref, tokens_ref, cols_ref, gain_ref, hidden_ref, grad_ref):
    incoming = keep_ref[...] + got_ref[...].astype(F32) + other_ref[...].astype(F32)
    inverse = cols_ref[:, 1:2]
    unit = (tokens_ref[...].astype(F32) - cols_ref[:, 0:1]) * inverse
    grad_ref[...] = hidden_ref[...] + norm_backward(incoming, unit, inverse, gain_ref[...])


def last(keep, got, other, tokens, cols, gain, grad_hidden):
    rows, width = tokens.shape
    tile = pl.BlockSpec((STEP, width), lambda i: (i, 0))
    return pl.pallas_call(
        last_kernel,
        grid=(rows // STEP,),
        out_shape=shaped((rows, width), F32),
        in_specs=[tile] * 4 + [pl.BlockSpec((STEP, 128), lambda i: (i, 0)), VMEM, tile],
        out_specs=tile,
        cost_estimate=cost(0, 0),
        name="last",
    )(keep, got, other, tokens, cols, row(gain), grad_hidden)


def output_kernel(keep_ref, got_ref, other_ref, tokens_ref, unit2_ref, post_g_ref, post_b_ref, b_down_ref,
                  out_ref):
    hidden = tokens_ref[...].astype(F32) + (unit2_ref[...] * post_g_ref[...] + post_b_ref[...])
    branch = keep_ref[...] + got_ref[...].astype(F32) + other_ref[...].astype(F32)
    out_ref[...] = (hidden + (branch + b_down_ref[...])).astype(BF16)


def output_rows(keep, got, other, tokens, unit2, post_gain, post_bias, b_down):
    rows, width = tokens.shape
    tile = pl.BlockSpec((STEP, width), lambda i: (i, 0))
    return pl.pallas_call(
        output_kernel,
        grid=(rows // STEP,),
        out_shape=shaped((rows, width), BF16),
        in_specs=[tile] * 5 + [VMEM] * 3,
        out_specs=tile,
        cost_estimate=cost(0, 0),
        name="output_rows",
    )(keep, got, other, tokens, unit2, row(post_gain), row(post_bias), row(b_down))


def per_device(
    tokens,
    segments,
    ln1_gain,
    ln1_bias,
    w_query,
    b_query,
    w_key,
    w_value,
    b_value,
    head_scale,
    w_out,
    b_out,
    post_gain,
    post_bias,
    ln2_gain,
    ln2_bias,
    w_up,
    b_up,
    ffn_gain,
    ffn_bias,
    w_down,
    b_down,
    cotangent,
):
    index = lax.axis_index("tensor")
    rows = tokens.shape[0]
    two = 2 * rows
    columns = w_query.shape[1]
    hidden_here = w_up.shape[1]
    shard = D // lax.axis_size("dp")
    order = jnp.array([0, 2, 1, 3], jnp.int32)
    place = order[jnp.arange(4, dtype=jnp.int32) ^ index]
    here = jnp.full((1,), index, jnp.int32)

    def own_part(vector, width):
        return lax.dynamic_slice_in_dim(vector, index * width, width, 0)

    segment = segments[0]
    seg_col, seg_row = segment[:, None], segment[None, :]
    scale_row = row(jnp.repeat(own_part(head_scale, columns // HD), HD))
    qkv_b = jnp.concatenate(
        [own_part(b_query, columns), jnp.zeros((columns,), F32), own_part(b_value, columns)]
    )
    gain_here, shift_here = own_part(ffn_gain, hidden_here), own_part(ffn_bias, hidden_here)
    b_up_here = own_part(b_up, hidden_here)

    order_dp = lax.axis_index("dp") ^ jnp.arange(lax.axis_size("dp"), dtype=jnp.int32)
    quick = shard % 128 == 0 and lax.axis_size("dp") == 8

    attn = None
    if quick:
        packed, tokens = phase(pack(w_query, w_key, w_value, w_out), tokens)
        attn = Shards(packed)
        attn.send(4, 0)
        attn.send(1, 0)
        first = attn.get(4, 1)
    else:
        first = []
        attn_full = [
            lax.all_gather(jnp.concatenate([w_query, w_key, w_value], 1), "dp", axis=0, tiled=True),
            lax.all_gather(w_out, "dp", axis=1, tiled=True),
        ]
        up_full = [lax.all_gather(w_up, "dp", axis=0, tiled=True)]
        down_full = [lax.all_gather(w_down, "dp", axis=1, tiled=True)]
        attn_masks = up_masks = down_masks = None
    x_pair = swap(tokens, "tensor", 2)
    x_side = swap(tokens, "tensor", 1)
    up_s, down_s = Shards(w_up), Shards(w_down)
    own_up, own_down = up_s.held[0], down_s.held[0]
    (x_pair, x_side, own_up, own_down, cotangent, b_up_here, gain_here, shift_here, qkv_b, scale_row,
     seg_col, place, order_dp), first = phase(
        (x_pair, x_side, own_up, own_down, cotangent, b_up_here, gain_here, shift_here, qkv_b,
         scale_row, seg_col, place, order_dp), first)
    if quick:
        attn.put([4, 1], first)

    x_cross = swap(x_pair, "tensor", 1)
    if quick:
        attn.send(2, 0, 4)
        attn.send(1, 4)
        first = attn.get(2, 6, 5)
    g_pair = swap(cotangent, "tensor", 2)
    normed, x_all, cols1 = norm_one([tokens, x_pair, x_side, x_cross], ln1_gain, ln1_bias)
    (normed, x_all, cols1, own_up, own_down, g_pair, cotangent), first = phase(
        (normed, x_all, cols1, own_up, own_down, g_pair, cotangent), first)

    if quick:
        attn.put([2, 6, 5], first)
        attn.send(1, 2, 6)
        up_s.put([0], [own_up])
        up_s.send(4, 0)
        attn_masks, attn_full = attn.all()
        first = up_s.get(4)
    g_side = swap(cotangent, "tensor", 1)
    g_cross = swap(g_pair, "tensor", 1)
    (normed, own_down, own_up, g_side, g_cross), attn_full, first = phase(
        (normed, own_down, own_up, g_side, g_cross), attn_full, first)

    if quick:
        up_s.put([0, 4], [own_up] + first)
        up_s.send(2, 0, 4)
        up_s.send(1, 0, 4)
        first = up_s.get(2, 6, 1, 5)
    qkv, mixed, scaled, lse, qkv_w, out_w, send, keep = attend(
        place, order_dp, normed, attn_masks, attn_full, row(qkv_b), seg_col, seg_row, scale_row
    )
    (qkv, mixed, scaled, lse, qkv_w, out_w, send, keep, own_down, g_side, g_cross), first = phase(
        (qkv, mixed, scaled, lse, qkv_w, out_w, send, keep, own_down, g_side, g_cross), first)

    got = swap(send, "tensor", 1)
    if quick:
        up_s.put([2, 6, 1, 5], first)
        up_s.send(1, 2, 6)
        down_s.put([0], [own_down])
        down_s.send(4, 0)
        first = up_s.get(3, 7) + down_s.get(4)
    low, got, keep, g_side = phase(low_rows(keep, got, two), got, keep, g_side)
    other = swap(low, "tensor", 2)
    (g_all, own_down), first = phase((stack(cotangent, g_pair, g_side, g_cross), own_down), first)
    if quick:
        up_s.put([3, 7], first[:2])
        down_s.put([0, 4], [own_down, first[2]])
        down_s.send(2, 0, 4)
        down_s.send(1, 0, 4)
        (other, keep, got), first = phase((other, keep, got), down_s.get(1, 5))
        down_s.put([1, 5], first)
        up_masks, up_full = up_s.all()
        first = down_s.get(2, 6)

    ffn_in, unit2, cols = middle(
        keep, got, other, tokens, x_pair, b_out, post_gain, post_bias, ln2_gain, ln2_bias
    )
    (ffn_in, unit2, cols), first = phase((ffn_in, unit2, cols), first)
    ffn_rest = swap(ffn_in, "tensor", 1)
    if quick:
        down_s.put([2, 6], first)
        down_s.send(1, 2, 6)
        down_masks, down_full = down_s.all()
    active_k, slope_k, stats_k, up_w = ffn_one(ffn_in, order_dp, up_masks, up_full, b_up_here)
    active_k, slope_k, stats_k, up_w, ffn_rest = phase(active_k, slope_k, stats_k, up_w, ffn_rest)
    active_s, slope_s, stats_s, _ = ffn_one(ffn_rest, order_dp, None, [up_w], b_up_here)
    (active_s, stats_s, slope_s), down_full = phase((active_s, stats_s, slope_s), down_full)
    inner_grad, stats, down_w = ffn_grad(
        g_all, order_dp, down_masks, down_full, active_k, active_s, stats_k, stats_s, gain_here
    )
    stats = [stats] + [swap(stats, "tensor", mask) for mask in (1, 2, 3)]
    inner, grad_before, send, keep, ffn_sums = ffn_two(
        active_k, active_s, slope_k, slope_s, inner_grad, stats, gain_here, shift_here, up_w
    )

    down_g, up_g = Scatter(1, shard, 2), Scatter(0, shard, 1)
    qkv_g, out_g = Scatter(0, shard, 1), Scatter(1, shard, 1)
    got = swap(send, "tensor", 1)
    down_send = down_g.product([g_all], inner)
    down_send, down_g.keep, inner, grad_before, got, keep = phase(
        down_send, down_g.keep, inner, grad_before, got, keep
    )
    low, down_send, inner, grad_before = phase(low_rows(keep, got, two), down_send, inner, grad_before)
    other = swap(low, "tensor", 2)
    down_g.start(down_send)
    up_send = up_g.product([ffn_in, ffn_rest], grad_before)
    out_send, out_keep = project(inner, down_w)
    up_send, up_g.keep, out_send, out_keep = phase(up_send, up_g.keep, out_send, out_keep)
    up_g.start(up_send)
    other, down_g.got, out_send = phase(other, down_g.got, out_send)

    down_send = down_g.split()
    down_send, down_g.keep, other, out_send = phase(down_send, down_g.keep, other, out_send)
    down_g.start(down_send)
    out_got = swap(out_send, "tensor", 1)
    grad_proj, grad_hidden, middle_sums = middle_back(
        keep, got, other, cotangent, g_pair, tokens, x_pair, unit2, cols, post_gain, post_bias,
        ln2_gain,
    )
    grad_proj, up_g.got, out_got, out_keep = phase(grad_proj, up_g.got, out_got, out_keep)
    proj_rest = swap(grad_proj, "tensor", 1)
    up_send = up_g.split()
    out_low = low_rows(out_keep, out_got, rows)
    grad_proj, proj_rest, up_send, up_g.keep, out_low = phase(
        grad_proj, proj_rest, up_send, up_g.keep, out_low
    )
    w_send = out_g.product([grad_proj, proj_rest], scaled)
    w_send, out_g.keep, grad_proj, proj_rest, up_send, out_low = phase(
        w_send, out_g.keep, grad_proj, proj_rest, up_send, out_low
    )

    up_g.start(up_send)
    out_other = swap(out_low, "tensor", 2)
    out_g.start(w_send)
    grad_qkv, sums = attend_back(
        place, qkv, grad_proj, proj_rest, out_w, mixed, lse, seg_col, seg_row, scale_row
    )
    grad_qkv, sums, down_g.got, up_g.got, out_other, out_g.got = phase(
        grad_qkv, sums, down_g.got, up_g.got, out_other, out_g.got
    )

    masks = dp_masks(1)
    down_send, w_send = down_g.split(), out_g.split()
    down_send, down_g.keep, up_g.got, grad_qkv, w_send, out_g.keep = phase(
        down_send, down_g.keep, up_g.got, grad_qkv, w_send, out_g.keep
    )
    down_g.start(down_send)
    out_g.start(w_send)
    send, keep, late = normed_grad(
        here, grad_qkv, qkv_w, x_all, cols1, sums, middle_sums, ffn_sums
    )
    up_send = up_g.split()
    qkv_send = qkv_g.product([normed], grad_qkv)
    send, keep, late, up_send, up_g.keep, qkv_send, qkv_g.keep, down_g.got, out_g.got = phase(
        send, keep, late, up_send, up_g.keep, qkv_send, qkv_g.keep, down_g.got, out_g.got
    )

    got = swap(send, "tensor", 1)
    side = swap(late, "tensor", 1)
    qkv_g.start(qkv_send)
    up_g.start(up_send)
    w_send = out_g.split()
    out_g.start(w_send)
    late = late + side
    side = swap(late, "tensor", 2)
    low = low_rows(keep, got, rows)
    other = swap(low, "tensor", 2)
    output = output_rows(out_keep, out_got, out_other, tokens, unit2, post_gain, post_bias, b_down)
    g_down = down_g.finish()
    output, g_down, late, side, up_g.got, qkv_g.got, qkv_g.keep, other, out_g.got = phase(
        output, g_down, late, side, up_g.got, qkv_g.got, qkv_g.keep, other, out_g.got
    )
    qkv_send = qkv_g.split()
    qkv_send, qkv_g.keep, other, late, side = phase(qkv_send, qkv_g.keep, other, late, side)
    qkv_g.start(qkv_send)
    late = late + side
    late = late + swap(late, "dp", masks[0])
    side = swap(late, "dp", masks[1])
    input_grad = last(keep, got, other, tokens, cols1, ln1_gain, grad_hidden)
    g_up, g_out = up_g.finish(), out_g.finish()
    input_grad, g_up, g_out, late, side, qkv_g.got, qkv_g.keep = phase(
        input_grad, g_up, g_out, late, side, qkv_g.got, qkv_g.keep
    )
    late = late + side
    if quick:
        qkv_send, late = phase(qkv_g.split(), late)
        qkv_g.start(qkv_send)
    for mask in masks[2:]:
        late = late + swap(late, "dp", mask)
    g_qkv_w = qkv_g.finish()
    blocks = FF // D
    return (
        output,
        input_grad,
        late[0],
        late[1],
        g_qkv_w[:, :columns],
        late[2],
        g_qkv_w[:, columns : 2 * columns],
        g_qkv_w[:, 2 * columns :],
        late[3],
        jnp.sum(late[4].reshape(HEADS, HD), axis=1),
        g_out,
        late[9],
        late[7],
        late[8],
        late[5],
        late[6],
        g_up,
        late[12 : 12 + blocks].reshape(FF),
        late[12 + blocks : 12 + 2 * blocks].reshape(FF),
        late[12 + 2 * blocks : 12 + 3 * blocks].reshape(FF),
        g_down,
        late[10],
    )


def solution(mesh):
    return jax.shard_map(
        per_device,
        mesh=mesh,
        in_specs=(
            P(("dp", "tensor"), None),
            P("dp", None),
            P(),
            P(),
            P("dp", "tensor"),
            P(),
            P("dp", "tensor"),
            P("dp", "tensor"),
            P(),
            P(),
            P("tensor", "dp"),
            P(),
            P(),
            P(),
            P(),
            P(),
            P("dp", "tensor"),
            P(),
            P(),
            P(),
            P("tensor", "dp"),
            P(),
            P(("dp", "tensor"), None),
        ),
        out_specs=(
            P(("dp", "tensor"), None),
            P(("dp", "tensor"), None),
            P(),
            P(),
            P("dp", "tensor"),
            P(),
            P("dp", "tensor"),
            P("dp", "tensor"),
            P(),
            P(),
            P("tensor", "dp"),
            P(),
            P(),
            P(),
            P(),
            P(),
            P("dp", "tensor"),
            P(),
            P(),
            P(),
            P("tensor", "dp"),
            P(),
        ),
        check_vma=False,
    )
```

```python
import functools

import jax
import jax.numpy as jnp
from jax import lax
from jax.experimental import pallas as pl
from jax.experimental.pallas import tpu as pltpu
from jax.sharding import PartitionSpec as P

D = 1024
HEADS = 16
HD = 64
FF = 4096
LONGEST = 512
EPS = 1e-05
SCALE = HD ** (-0.5)
F32 = jnp.float32
BF16 = jnp.bfloat16


def dot(left, right, left_dim=1, right_dim=0):
    return lax.dot_general(
        left, right, (((left_dim,), (right_dim,)), ((), ())), preferred_element_type=F32
    )


def swap(value, axis, mask):
    size = lax.axis_size(axis)
    return lax.ppermute(value, axis, [(i, i ^ mask) for i in range(size)])


def bit_of(axis, mask):
    return (lax.axis_index(axis) // mask) % 2


def after(value, *others):
    return lax.optimization_barrier((value,) + others)[0]


def row(vector):
    return vector[None, :]


def each_rows(count, step, body):
    def one(k, carry):
        body(pl.ds(pl.multiple_of(k * step, step), step))
        return carry

    lax.fori_loop(0, count // step, one, 0)


STEP = 128


def fold(value):
    return jnp.sum(value.reshape(value.shape[0] // 8, 8, value.shape[1]), axis=0)


def norm_stats(values):
    mean = jnp.mean(values, axis=-1, keepdims=True)
    centered = values - mean
    inverse = lax.rsqrt(jnp.mean(centered * centered, axis=-1, keepdims=True) + EPS)
    return centered * inverse, inverse


def norm_backward(grad, unit, inverse, gain):
    scaled = grad * gain
    return inverse * (
        scaled
        - jnp.mean(scaled, axis=-1, keepdims=True)
        - unit * jnp.mean(scaled * unit, axis=-1, keepdims=True)
    )


VMEM = pl.BlockSpec(memory_space=pltpu.VMEM)
SMEM = pl.BlockSpec(memory_space=pltpu.SMEM)


def shaped(shape, kind):
    return jax.ShapeDtypeStruct(shape, kind)


def cost(flops, moved, hard=0):
    return pl.CostEstimate(flops=flops, bytes_accessed=moved, transcendentals=hard)


class Shards:
    def __init__(self, shard):
        self.held = {0: shard[None]}

    def send(self, mask, *which):
        for k in which:
            self.held[k ^ mask] = swap(self.held[k], "dp", mask)

    def get(self, *which):
        return [self.held[k] for k in which]

    def put(self, which, values):
        for k, value in zip(which, values):
            self.held[k] = value

    def all(self):
        masks = sorted(self.held)
        return [[k] for k in masks], [self.held[k] for k in masks]


def phase(*values):
    return lax.optimization_barrier(values)


def fill(axis, masks, order_ref, piece_refs, full_ref, start=0, width=None):
    if masks is None:
        full_ref[...] = piece_refs[0][...]
        return
    for group, piece in zip(masks, piece_refs):
        height = piece.shape[1]
        for k, mask in enumerate(group):
            place = order_ref[mask]
            if axis == 0:
                there = pl.ds(pl.multiple_of(place * height, height), height)
                full_ref[there, :] = piece[k, :, start : start + full_ref.shape[1]]
            else:
                there = pl.ds(pl.multiple_of(place * width, width), width)
                for low in range(0, full_ref.shape[0], height):
                    at = start + low // height * width
                    full_ref[low : low + height, there] = piece[k, :, at : at + width]


def pack_kernel(q_ref, k_ref, v_ref, o_ref, out_ref):
    height, width = q_ref.shape
    for k, ref in enumerate((q_ref, k_ref, v_ref)):
        out_ref[:, k * width : (k + 1) * width] = ref[...]
    wide = o_ref.shape[1]
    for k in range(o_ref.shape[0] // height):
        at = 3 * width + k * wide
        out_ref[:, at : at + wide] = o_ref[k * height : (k + 1) * height, :]


def pack(w_query, w_key, w_value, w_out):
    height, width = w_query.shape
    total = 3 * width + w_out.size // height
    return pl.pallas_call(
        pack_kernel,
        out_shape=shaped((height, total), BF16),
        in_specs=[VMEM] * 4,
        out_specs=VMEM,
        cost_estimate=cost(0, 0),
        name="pack",
    )(w_query, w_key, w_value, w_out)


def pick_cols(value, width, bit):
    rows, cols = value.shape
    pairs = cols // (2 * width)
    if width % 128:
        return lax.dynamic_index_in_dim(
            value.reshape(rows, pairs, 2, width), bit, 2, keepdims=False
        ).reshape(rows, pairs * width)
    return jnp.concatenate(
        [
            lax.dynamic_slice_in_dim(value, (2 * p + bit) * width, width, 1)
            for p in range(pairs)
        ],
        1,
    )


def pick_rows(value, height, bit):
    rows, cols = value.shape
    return lax.dynamic_index_in_dim(
        value.reshape(rows // (2 * height), 2, height, cols), bit, 1, keepdims=False
    ).reshape(rows // 2, cols)


def dp_masks(last):
    size = lax.axis_size("dp")
    masks = [1 << k for k in range(size.bit_length() - 1)]
    if last in masks:
        masks.remove(last)
        masks.append(last)
    return masks


def outer_kernel(width, on_left, count, bit_ref, *refs):
    parts, (other_ref, send_ref, keep_ref, *picks) = refs[:count], refs[count:]

    @pl.when(pl.program_id(0) == 0)
    def _():
        for bit, pick_ref in zip((1 - bit_ref[0], bit_ref[0]), picks):
            for p in range(pick_ref.shape[1] // width):
                there = pl.ds(pl.multiple_of((2 * p + bit) * width, width), width)
                row = 0
                for part in parts:
                    pick_ref[row : row + part.shape[0], p * width : (p + 1) * width] = part[:, there]
                    row += part.shape[0]

    for pick_ref, out_ref in zip(picks, (send_ref, keep_ref)):
        if on_left:
            value = dot(pick_ref[...], other_ref[...], 0, 0)
        else:
            value = dot(other_ref[...], pick_ref[...], 0, 0)
        out_ref[...] = value.astype(out_ref.dtype)


def outer(bit, picked, other, width, on_left, part, parts):
    rows, cols = other.shape[0], other.shape[1] // parts
    half = picked[0].shape[1] // 2
    step = 256 if cols % 512 == 0 else cols
    skip = part * (cols // step)
    shape = (half, cols) if on_left else (cols, half)
    tile = (half, step) if on_left else (step, half)
    out = pl.BlockSpec(tile, (lambda i: (0, i)) if on_left else (lambda i: (i, 0)))
    return pl.pallas_call(
        functools.partial(outer_kernel, width, on_left, len(picked)),
        grid=(cols // step,),
        out_shape=(shaped(shape, BF16), shaped(shape, F32)),
        in_specs=[SMEM] + [VMEM] * len(picked) + [pl.BlockSpec((rows, step), lambda i: (0, i + skip))],
        out_specs=(out,) * 2,
        scratch_shapes=[pltpu.VMEM((rows, half), BF16)] * 2,
        cost_estimate=cost(0, 0),
        name="outer",
    )(bit, *picked, other)


def split_kernel(axis, width, bit_ref, keep_ref, got_ref, send_ref, stay_ref):
    for bit, out_ref in ((1 - bit_ref[0], send_ref), (bit_ref[0], stay_ref)):
        for p in range(out_ref.shape[axis] // width):
            there = pl.ds(pl.multiple_of((2 * p + bit) * width, width), width)
            here = slice(p * width, (p + 1) * width)
            source, target = ((there, slice(None)), (here, slice(None)))
            if axis == 1:
                source, target = source[::-1], target[::-1]
            value = keep_ref[source] + got_ref[source].astype(F32)
            out_ref[target] = value.astype(out_ref.dtype)


def split(bit, keep, got, width, axis):
    cut = lambda shape: tuple(n // 2 if k == axis else n for k, n in enumerate(shape))
    size = keep.shape[1 - axis]
    step = size // 2 if size % 256 == 0 else size
    tile = tuple(n if k == axis else step for k, n in enumerate(keep.shape))
    index = (lambda i: (0, i)) if axis == 0 else (lambda i: (i, 0))
    return pl.pallas_call(
        functools.partial(split_kernel, axis, width),
        grid=(size // step,),
        out_shape=(shaped(cut(keep.shape), BF16), shaped(cut(keep.shape), F32)),
        in_specs=[SMEM, pl.BlockSpec(tile, index), pl.BlockSpec(tile, index)],
        out_specs=(pl.BlockSpec(cut(tile), index),) * 2,
        cost_estimate=cost(16 * 10**9, 0),
        name="split",
    )(bit, keep, got)


class Scatter:
    def __init__(self, axis, extent, last=0):
        self.axis, self.extent, self.masks = axis, extent, dp_masks(last)

    def place(self):
        mask = self.masks[0]
        lower = sum(1 for other in self.masks if other < mask)
        return bit_of("dp", mask), self.extent << lower

    def product(self, picked, other, part=0, parts=1):
        bit, width = self.place()
        if width % 128 == 0:
            bit = jnp.full((1,), bit, jnp.int32)
            send, self.keep = outer(bit, picked, other, width, self.axis == 0, part, parts)
            return send
        span = other.shape[1] // parts
        other = other[:, part * span : (part + 1) * span]
        picked = jnp.concatenate(picked, 0)
        send, keep = pick_cols(picked, width, 1 - bit), pick_cols(picked, width, bit)
        if self.axis == 0:
            send, self.keep = dot(send, other, 0, 0), dot(keep, other, 0, 0)
        else:
            send, self.keep = dot(other, send, 0, 0), dot(other, keep, 0, 0)
        return send.astype(BF16)

    def start(self, send):
        self.got = swap(send, "dp", self.masks.pop(0))

    def split(self):
        bit, width = self.place()
        if width % 128 == 0:
            send, self.keep = split(jnp.full((1,), bit, jnp.int32), self.keep, self.got, width, self.axis)
            return send
        pick = (pick_rows, pick_cols)[self.axis]
        total = self.keep + self.got.astype(F32)
        self.keep = pick(total, width, bit)
        return pick(total, width, 1 - bit).astype(BF16)

    def finish(self):
        while self.masks:
            self.start(self.split())
        return self.keep + self.got.astype(F32)


def low_kernel(keep_ref, got_ref, out_ref):
    out_ref[...] = (keep_ref[...] + got_ref[...].astype(F32)).astype(BF16)


def low_rows(keep, got, rows):
    total, width = keep.shape
    step = rows // 2
    first = (total - rows) // step
    there = pl.BlockSpec((step, width), lambda i: (i + first, 0))
    return pl.pallas_call(
        low_kernel,
        grid=(rows // step,),
        out_shape=shaped((rows, width), BF16),
        in_specs=[there, there],
        out_specs=pl.BlockSpec((step, width), lambda i: (i, 0)),
        cost_estimate=cost(16 * 10**9, 0),
        name="low_rows",
    )(keep, got)


def stack_kernel(*refs):
    *parts, out_ref = refs
    row = 0
    for part in parts:
        out_ref[row : row + part.shape[0], :] = part[...]
        row += part.shape[0]


def stack(*parts):
    return pl.pallas_call(
        stack_kernel,
        out_shape=shaped((sum(part.shape[0] for part in parts), parts[0].shape[1]), parts[0].dtype),
        in_specs=[VMEM] * len(parts),
        out_specs=VMEM,
        cost_estimate=cost(0, 0),
        name="stack",
    )(*parts)


def project_kernel(inner_ref, weight_ref, send_ref, keep_ref):
    half = inner_ref.shape[0] // 2
    step = half // 2

    def body(rows):
        later = pl.ds(pl.multiple_of(half + rows.start, step), step)
        send_ref[rows, :] = dot(inner_ref[later, :], weight_ref[...]).astype(BF16)
        keep_ref[rows, :] = dot(inner_ref[rows, :], weight_ref[...])

    each_rows(half, step, body)


def project(inner, weight):
    half = inner.shape[0] // 2
    return pl.pallas_call(
        project_kernel,
        out_shape=(shaped((half, D), BF16), shaped((half, D), F32)),
        in_specs=[VMEM] * 2,
        out_specs=(VMEM,) * 2,
        cost_estimate=cost(0, 0),
        name="project",
    )(inner, weight)


def norm_one_kernel(a_ref, b_ref, c_ref, d_ref, gain_ref, bias_ref, out_ref, all_ref, cols_ref):
    step = pl.program_id(0)
    per = pl.num_programs(0) // 4
    value = jnp.where(
        step < 2 * per,
        jnp.where(step < per, a_ref[...], b_ref[...]),
        jnp.where(step < 3 * per, c_ref[...], d_ref[...]),
    )
    all_ref[...] = value
    value = value.astype(F32)
    mean = jnp.mean(value, axis=-1, keepdims=True)
    centered = value - mean
    inverse = lax.rsqrt(jnp.mean(centered * centered, axis=-1, keepdims=True) + EPS)
    lane = lax.broadcasted_iota(jnp.int32, cols_ref.shape, 1)
    cols_ref[...] = jnp.where(lane == 0, mean, inverse)
    out_ref[...] = (centered * inverse * gain_ref[...] + bias_ref[...]).astype(BF16)


def norm_one(parts, gain, bias):
    rows, width = parts[0].shape
    per = rows // STEP

    def spec(first, count, width=width):
        return pl.BlockSpec((STEP, width), lambda i: (jnp.clip(i - first, 0, count - 1), 0))

    return pl.pallas_call(
        norm_one_kernel,
        grid=(4 * per,),
        out_shape=(
            shaped((4 * rows, width), BF16),
            shaped((4 * rows, width), BF16),
            shaped((4 * rows, 128), F32),
        ),
        in_specs=[spec(k * per, per) for k in range(4)] + [VMEM, VMEM],
        out_specs=(spec(0, 4 * per), spec(0, 4 * per), spec(0, 4 * per, 128)),
        cost_estimate=cost(0, 0),
        name="norm_one",
    )(*parts, row(gain), row(bias))


def key_range(block, size):
    low = max(0, block * size - (LONGEST // size) * size)
    return low, (block + 1) * size - low


def write_bias(bias_ref, seg_col_ref, seg_row_ref, rows, keys_at):
    shape = (keys_at.size, rows.size)
    key_pos = keys_at.start + lax.broadcasted_iota(jnp.int32, shape, 0)
    row_pos = rows.start + lax.broadcasted_iota(jnp.int32, shape, 1)
    same = seg_col_ref[keys_at, :] == seg_row_ref[:, rows]
    bias_ref[: keys_at.size, :] = jnp.where((key_pos <= row_pos) & same, 0.0, -1000000000.0)


def each_block(blocks, size, body):
    short = min(LONGEST // size, blocks)
    for block in range(short):
        body(block, *key_range(block, size))

    def one(block, carry):
        low = pl.multiple_of((block - short) * size, size)
        body(block, low, (short + 1) * size)
        return carry

    lax.fori_loop(short, blocks, one, 0)


def attend_kernel(size, masks, place_ref, order_ref, normed_ref, qkv_b_ref, seg_col_ref, seg_row_ref,
                  scale_ref, *refs):
    *pieces, qkv_ref, o_ref, u_ref, lse_ref, qkv_w_ref, out_w_ref, send_ref, keep_ref = refs[:-3]
    bias_ref, vt_ref, ot_ref = refs[-3:]
    length, width = o_ref.shape
    heads = width // HD
    if masks is None:
        qkv_w_ref[...] = pieces[0][...]
        out_w_ref[...] = pieces[1][...]
    else:
        fill(0, masks, order_ref, pieces, qkv_w_ref)
        fill(1, masks, order_ref, pieces, out_w_ref, 3 * width, pieces[0].shape[1])
    head_of = lax.broadcasted_iota(jnp.int32, (size, width), 1) // HD
    def project_block(block, carry):
        rows = pl.ds(pl.multiple_of(block * size, size), size)
        here = pl.ds(pl.multiple_of(place_ref[block] * size, size), size)
        product = dot(normed_ref[here, :], qkv_w_ref[...]) + qkv_b_ref[...]
        qkv_ref[rows, :] = product.astype(BF16)
        vt_ref[:, rows] = product[:, 2 * width :].T.astype(BF16)
        return carry

    def attend_block(block, low, count):
        rows, keys_at = pl.ds(block * size, size), pl.ds(low, count)
        here = pl.ds(pl.multiple_of(place_ref[block] * size, size), size)
        write_bias(bias_ref, seg_col_ref, seg_row_ref, rows, keys_at)
        query = qkv_ref[rows, :width].astype(F32) * SCALE
        keys = qkv_ref[keys_at, width : 2 * width]
        for head in range(heads):
            masked = jnp.where(head_of == head, query, 0.0).astype(BF16)
            scores = dot(keys, masked, 1, 1) + bias_ref[:count, :]
            highest = jnp.max(scores, axis=0, keepdims=True)
            raised = jnp.exp(scores - highest)
            total = jnp.sum(raised, axis=0, keepdims=True)
            lse_ref[block, head : head + 1, :] = highest + jnp.log(total)
            probs = (raised * (1.0 / total)).astype(BF16)
            part = slice(head * HD, (head + 1) * HD)
            ot_ref[part, :] = dot(vt_ref[part, keys_at], probs)
        mixed = ot_ref[...].T
        o_ref[rows, :] = mixed
        u_ref[here, :] = (mixed * scale_ref[...]).astype(BF16)

    lax.fori_loop(0, length // size, project_block, 0)
    each_block(length // size, size, attend_block)
    half = length // 2
    send_ref[...] = dot(u_ref[half:, :], out_w_ref[...]).astype(BF16)
    keep_ref[...] = dot(u_ref[:half, :], out_w_ref[...])


def attend_back_kernel(size, place_ref, qkv_ref, own_ref, rest_ref, out_w_ref, o_ref, lse_ref,
                       seg_col_ref, seg_row_ref, scale_ref, dqkv_ref, sums_ref,
                       bias_ref, kt_ref, dqt_ref, probs_ref, ds_ref, q_ref, do_ref, dk_ref, dv_ref,
                       du_ref, acc_ref):
    length, width = o_ref.shape
    heads = width // HD
    du_ref[: length // 2, :] = dot(own_ref[...], out_w_ref[...], 1, 1)
    du_ref[length // 2 :, :] = dot(rest_ref[...], out_w_ref[...], 1, 1)
    kt_ref[...] = qkv_ref[:, width : 2 * width].astype(F32).T.astype(BF16)
    head_of = lax.broadcasted_iota(jnp.int32, (size, width), 1) // HD
    blocks = length // size
    acc_ref[...] = jnp.zeros_like(acc_ref)

    def back_block(block, low, count):
        rows, keys_at = pl.ds(block * size, size), pl.ds(low, count)
        here = pl.ds(pl.multiple_of(place_ref[block] * size, size), size)
        write_bias(bias_ref, seg_col_ref, seg_row_ref, rows, keys_at)
        query = qkv_ref[rows, :width].astype(F32) * SCALE
        keys = qkv_ref[keys_at, width : 2 * width]
        values = qkv_ref[keys_at, 2 * width :]
        du = du_ref[here, :]
        acc_ref[0:8, :] += fold(du * o_ref[rows, :])
        grad = du * scale_ref[...]
        for head in range(heads):
            masked = jnp.where(head_of == head, query, 0.0).astype(BF16)
            grad_here = jnp.where(head_of == head, grad, 0.0).astype(BF16)
            stack = slice(head * size, (head + 1) * size)
            q_ref[stack, :] = masked
            do_ref[stack, :] = grad_here
            scores = dot(keys, masked, 1, 1) + bias_ref[:count, :]
            full = jnp.exp(scores - lse_ref[block, head : head + 1, :])
            probs_ref[:count, stack] = full.astype(BF16)
            dp = dot(values, grad_here, 1, 1)
            delta = jnp.sum(full * dp, axis=0, keepdims=True)
            ds = (full * (dp - delta)).astype(BF16)
            ds_ref[:count, stack] = ds
            part = slice(head * HD, (head + 1) * HD)
            dqt_ref[part, :] = dot(kt_ref[part, keys_at], ds)
        dq = (dqt_ref[...].T * SCALE).astype(BF16)
        dqkv_ref[here, :width] = dq
        acc_ref[8:16, :] += fold(dq.astype(F32))
        dk = dot(ds_ref[:count, :], q_ref[...])
        dv = dot(probs_ref[:count, :], do_ref[...])
        old = count - size
        if old:
            before = pl.ds(low, old)
            dk_ref[before, :] += dk[:old]
            dv_ref[before, :] += dv[:old]
        dk_ref[rows, :] = dk[old:]
        dv_ref[rows, :] = dv[old:]

    each_block(blocks, size, back_block)

    def finish_block(block, carry):
        rows = pl.ds(pl.multiple_of(block * size, size), size)
        here = pl.ds(pl.multiple_of(place_ref[block] * size, size), size)
        dqkv_ref[here, width : 2 * width] = dk_ref[rows, :].astype(BF16)
        dv = dv_ref[rows, :].astype(BF16)
        dqkv_ref[here, 2 * width :] = dv
        acc_ref[16:24, :] += fold(dv.astype(F32))
        return carry

    lax.fori_loop(0, blocks, finish_block, 0)
    sums_ref[...] = jnp.concatenate(
        [jnp.sum(acc_ref[8 * k : 8 * k + 8, :], axis=0, keepdims=True) for k in (1, 2, 0)]
        + [jnp.zeros((5, width), F32)],
        axis=0,
    )


def attend(place, order, normed, masks, pieces, qkv_b, seg_col, seg_row, scale_row):
    length, width = normed.shape[0], scale_row.shape[1]
    size = length // 4
    heads = width // HD
    most = LONGEST + size
    return pl.pallas_call(
        functools.partial(attend_kernel, size, masks),
        out_shape=(
            shaped((length, 3 * width), BF16),
            shaped((length, width), F32),
            shaped((length, width), BF16),
            shaped((4, heads, size), F32),
            shaped((D, 3 * width), BF16),
            shaped((width, D), BF16),
            shaped((length // 2, D), BF16),
            shaped((length // 2, D), F32),
        ),
        in_specs=[SMEM] * 2 + [VMEM] * (5 + len(pieces)),
        out_specs=(VMEM,) * 8,
        scratch_shapes=[
            pltpu.VMEM((most, size), F32),
            pltpu.VMEM((width, length), BF16),
            pltpu.VMEM((width, size), F32),
        ],
        cost_estimate=cost(0, 0),
        name="attend",
    )(place, order, normed, qkv_b, seg_col, seg_row, scale_row, *pieces)


def attend_back(place, qkv, own, rest, out_w, mixed, lse, seg_col, seg_row, scale_row):
    length, width = mixed.shape
    size = length // 4
    heads = width // HD
    most = LONGEST + size
    pairs = 4 * heads * most * size
    return pl.pallas_call(
        functools.partial(attend_back_kernel, size),
        out_shape=(shaped((length, 3 * width), BF16), shaped((8, width), F32)),
        in_specs=[SMEM] + [VMEM] * 9,
        out_specs=(VMEM,) * 2,
        scratch_shapes=[
            pltpu.VMEM((most, size), F32),
            pltpu.VMEM((width, length), BF16),
            pltpu.VMEM((width, size), F32),
            pltpu.VMEM((most, heads * size), BF16),
            pltpu.VMEM((most, heads * size), BF16),
            pltpu.VMEM((heads * size, width), BF16),
            pltpu.VMEM((heads * size, width), BF16),
            pltpu.VMEM((length, width), F32),
            pltpu.VMEM((length, width), F32),
            pltpu.VMEM((length, width), F32),
            pltpu.VMEM((24, width), F32),
        ],
        cost_estimate=cost(16 * 10**9, 0),
        name="attend_back",
    )(place, qkv, own, rest, out_w, mixed, lse, seg_col, seg_row, scale_row)


def middle_kernel(keep_ref, got_ref, other_ref, mine_ref, pair_ref, b_out_ref, post_g_ref, post_b_ref,
                  ln2_g_ref, ln2_b_ref, ffn_in_ref, unit2_ref, cols_ref):
    first = pl.program_id(0) < pl.num_programs(0) // 2
    tokens = jnp.where(first, mine_ref[...], pair_ref[...]).astype(F32)
    part = keep_ref[...] + got_ref[...].astype(F32)
    projected = part + other_ref[...].astype(F32) + b_out_ref[...]
    unit2, inv2 = norm_stats(projected)
    unit2_ref[...] = unit2
    hidden = tokens + (unit2 * post_g_ref[...] + post_b_ref[...])
    mean3 = jnp.mean(hidden, axis=-1, keepdims=True)
    centered = hidden - mean3
    inv3 = lax.rsqrt(jnp.mean(centered * centered, axis=-1, keepdims=True) + EPS)
    ffn_in_ref[...] = (centered * inv3 * ln2_g_ref[...] + ln2_b_ref[...]).astype(BF16)
    lane = lax.broadcasted_iota(jnp.int32, cols_ref.shape, 1)
    cols_ref[...] = jnp.where(lane == 0, inv2, jnp.where(lane == 1, mean3, inv3))


def pair_specs(rows, width):
    half = rows // 2 // STEP
    straight = pl.BlockSpec((STEP, width), lambda i: (i, 0))
    crossed = pl.BlockSpec((STEP, width), lambda i: ((i + half) % (2 * half), 0))
    mine = pl.BlockSpec((STEP, width), lambda i: (jnp.minimum(i, half - 1), 0))
    theirs = pl.BlockSpec((STEP, width), lambda i: (jnp.maximum(i - half, 0), 0))
    return straight, crossed, mine, theirs


def middle(keep, got, other, mine, pair, b_out, post_gain, post_bias, ln2_gain, ln2_bias):
    rows, width = keep.shape
    straight, crossed, own, theirs = pair_specs(rows, width)
    columns = pl.BlockSpec((STEP, 128), lambda i: (i, 0))
    return pl.pallas_call(
        middle_kernel,
        grid=(rows // STEP,),
        out_shape=(
            shaped((rows, width), BF16),
            shaped((rows, width), F32),
            shaped((rows, 128), F32),
        ),
        in_specs=[straight, straight, crossed, own, theirs] + [VMEM] * 5,
        out_specs=(straight, straight, columns),
        cost_estimate=cost(0, 0),
        name="middle",
    )(keep, got, other, mine, pair, row(b_out), row(post_gain), row(post_bias), row(ln2_gain),
      row(ln2_bias))


def middle_back_kernel(keep_ref, got_ref, other_ref, mine_ref, pair_ref, tokens_ref, tokens2_ref,
                       unit2_ref, cols_ref, post_g_ref, post_b_ref, ln2_g_ref, proj_ref, grad_ref, sums_ref,
                       acc_ref):
    step = pl.program_id(0)
    half = pl.num_programs(0) // 2
    first = step < half

    @pl.when(step == 0)
    def _():
        acc_ref[...] = jnp.zeros_like(acc_ref)

    part = keep_ref[...] + got_ref[...].astype(F32)
    incoming = part + other_ref[...].astype(F32)
    tokens = jnp.where(first, tokens_ref[...], tokens2_ref[...]).astype(F32)
    unit2 = unit2_ref[...]
    inv2, mean3, inv3 = (cols_ref[:, k : k + 1] for k in range(3))
    hidden = tokens + (unit2 * post_g_ref[...] + post_b_ref[...])
    unit3 = (hidden - mean3) * inv3
    outgoing = jnp.where(first, mine_ref[...], pair_ref[...]).astype(F32)
    grad = outgoing + norm_backward(incoming, unit3, inv3, ln2_g_ref[...])
    proj = norm_backward(grad, unit2, inv2, post_g_ref[...]).astype(BF16)
    proj_ref[...] = proj

    @pl.when(first)
    def _():
        grad_ref[...] = grad
        for k, value in enumerate(
            (incoming * unit3, incoming, grad * unit2, grad, proj.astype(F32), outgoing)
        ):
            acc_ref[8 * k : 8 * k + 8, :] += fold(value)

    @pl.when(step == half - 1)
    def _():
        sums_ref[...] = jnp.concatenate(
            [jnp.sum(acc_ref[8 * k : 8 * k + 8, :], axis=0, keepdims=True) for k in range(6)]
            + [jnp.zeros((2, acc_ref.shape[1]), F32)],
            axis=0,
        )


def middle_back(keep, got, other, mine, pair, tokens, tokens2, unit2, cols, post_gain, post_bias,
                ln2_gain):
    rows, width = keep.shape
    straight, crossed, own, theirs = pair_specs(rows, width)
    columns = pl.BlockSpec((STEP, 128), lambda i: (i, 0))
    return pl.pallas_call(
        middle_back_kernel,
        grid=(rows // STEP,),
        out_shape=(
            shaped((rows, width), BF16),
            shaped((rows // 2, width), F32),
            shaped((8, width), F32),
        ),
        in_specs=[straight, straight, crossed, own, theirs, own, theirs, straight, columns] + [VMEM] * 3,
        out_specs=(straight, own, VMEM),
        scratch_shapes=[pltpu.VMEM((48, width), F32)],
        cost_estimate=cost(0, 0),
        name="middle_back",
    )(keep, got, other, mine, pair, tokens, tokens2, unit2, cols, row(post_gain), row(post_bias),
      row(ln2_gain))


def ffn_one_kernel(masks, order_ref, in_ref, b_up_ref, *refs):
    *pieces, active_ref, slope_ref, stats_ref, up_ref, cols_ref = refs

    @pl.when(pl.program_id(0) == 0)
    def _():
        fill(0, masks, order_ref, pieces, up_ref)

    active_ref[...] = dot(in_ref[...], up_ref[...]) + b_up_ref[...]
    lane = lax.broadcasted_iota(jnp.int32, (STEP, 128), 1)

    def body(rows):
        before = active_ref[rows, :]
        cdf = 0.5 * (1.0 + lax.erf(before * 0.7071067811865476))
        active = before * cdf
        density = jnp.exp(-0.5 * before * before) * 0.3989422804014327
        slope_ref[rows, :] = cdf + before * density
        active_ref[rows, :] = active
        mean = jnp.mean(active, axis=-1, keepdims=True)
        off = active - mean
        square = jnp.sum(off * off, axis=-1, keepdims=True)
        cols_ref[rows, :] = jnp.where(lane == 0, mean, square)

    each_rows(active_ref.shape[0], STEP, body)
    stats_ref[...] = cols_ref[...].T[:8, :]


def ffn_one(ffn_in, order, masks, pieces, b_up):
    rows, width = ffn_in.shape[0], b_up.shape[0]
    size = 256
    tile = pl.BlockSpec((size, width), lambda i: (i, 0))
    return pl.pallas_call(
        functools.partial(ffn_one_kernel, masks),
        grid=(rows // size,),
        out_shape=(
            shaped((rows, width), F32),
            shaped((rows, width), F32),
            shaped((8, rows), F32),
            shaped((D, width), BF16),
        ),
        in_specs=[SMEM, pl.BlockSpec((size, D), lambda i: (i, 0)), VMEM] + [VMEM] * len(pieces),
        out_specs=(tile, tile, pl.BlockSpec((8, size), lambda i: (0, i)), VMEM),
        scratch_shapes=[pltpu.VMEM((size, 128), F32)],
        cost_estimate=cost(0, 0),
        name="ffn_one",
    )(order, ffn_in, row(b_up), *pieces)


def ffn_grad_kernel(masks, order_ref, grad_ref, keep_ref, send_ref, stats_k_ref, stats_s_ref, gain_ref,
                    *refs):
    *pieces, inner_ref, stats_ref, down_ref, cols_ref = refs
    step = pl.program_id(0)
    first = step < pl.num_programs(0) // 2

    @pl.when(step == 0)
    def _():
        fill(1, masks, order_ref, pieces, down_ref, 0, pieces[0].shape[-1])

    inner_ref[...] = dot(grad_ref[...], down_ref[...], 1, 1)
    lane = lax.broadcasted_iota(jnp.int32, (STEP, 128), 1)

    def body(rows):
        active = jnp.where(first, keep_ref[rows, :], send_ref[rows, :])
        scaled = inner_ref[rows, :] * gain_ref[...]
        plain = jnp.sum(scaled, axis=-1, keepdims=True)
        cross = jnp.sum(scaled * active, axis=-1, keepdims=True)
        cols_ref[rows, :] = jnp.where(lane == 2, plain, cross)

    each_rows(inner_ref.shape[0], STEP, body)
    stats = jnp.where(first, stats_k_ref[...], stats_s_ref[...])
    index = lax.broadcasted_iota(jnp.int32, stats.shape, 0)
    stats_ref[...] = jnp.where(index < 2, stats, cols_ref[...].T[:8, :])


def ffn_grad(grad, order, masks, pieces, active_k, active_s, stats_k, stats_s, gain):
    rows, width = grad.shape[0], gain.shape[0]
    size = 256
    half = rows // size // 2
    keep = lambda i: jnp.minimum(i, half - 1)
    send = lambda i: jnp.maximum(i - half, 0)
    tile = (size, width)
    return pl.pallas_call(
        functools.partial(ffn_grad_kernel, masks),
        grid=(rows // size,),
        out_shape=(
            shaped((rows, width), F32),
            shaped((8, rows), F32),
            shaped((width, D), BF16),
        ),
        in_specs=[
            SMEM,
            pl.BlockSpec((size, D), lambda i: (i, 0)),
            pl.BlockSpec(tile, lambda i: (keep(i), 0)),
            pl.BlockSpec(tile, lambda i: (send(i), 0)),
            pl.BlockSpec((8, size), lambda i: (0, keep(i))),
            pl.BlockSpec((8, size), lambda i: (0, send(i))),
            VMEM,
        ]
        + [VMEM] * len(pieces),
        out_specs=(
            pl.BlockSpec(tile, lambda i: (i, 0)),
            pl.BlockSpec((8, size), lambda i: (0, i)),
            VMEM,
        ),
        scratch_shapes=[pltpu.VMEM((size, 128), F32)],
        cost_estimate=cost(0, 0),
        name="ffn_grad",
    )(order, grad, active_k, active_s, stats_k, stats_s, row(gain), *pieces)


def ffn_two_kernel(mk_ref, ms_ref, sk_ref, ss_ref, grad_ref, s0_ref, s1_ref, s2_ref, s3_ref, gain_ref,
                   shift_ref, up_ref, inner_ref, before_ref, send_ref, keep_ref, sums_ref, cols_ref,
                   acc_ref):
    step = pl.program_id(0)
    half = pl.num_programs(0) // 2
    count, width = inner_ref.shape

    @pl.when(step == 0)
    def _():
        acc_ref[...] = jnp.zeros_like(acc_ref)

    values = [ref[...] for ref in (s0_ref, s1_ref, s2_ref, s3_ref)]
    mean = 0.25 * ((values[0][0:1] + values[1][0:1]) + (values[2][0:1] + values[3][0:1]))
    square = plain = cross = jnp.zeros_like(mean)
    for value in values:
        gap = value[0:1] - mean
        square = square + (value[1:2] + width * (gap * gap))
        plain = plain + value[2:3]
        cross = cross + value[3:4]
    inverse = lax.rsqrt(square / FF + EPS)
    cross = (cross - mean * plain) * inverse
    table = jnp.concatenate(
        [mean, inverse, plain / FF, cross / FF, jnp.zeros((124, count), F32)], axis=0
    )
    cols_ref[...] = table.T

    def work(active_ref, slope_ref, out_ref):
        def body(rows):
            cols = cols_ref[rows, :]
            mean, inverse, plain, cross = (cols[:, k : k + 1] for k in range(4))
            unit = (active_ref[rows, :] - mean) * inverse
            inner_ref[rows, :] = (unit * gain_ref[...] + shift_ref[...]).astype(BF16)
            grad = grad_ref[rows, :]
            moved = inverse * (grad * gain_ref[...] - plain - unit * cross)
            before = (moved * slope_ref[rows, :]).astype(BF16)
            before_ref[rows, :] = before
            for k, value in enumerate((before.astype(F32), grad * unit, grad)):
                acc_ref[8 * k : 8 * k + 8, :] += fold(value)

        each_rows(count, STEP, body)
        out_ref[...] = dot(before_ref[...], up_ref[...], 1, 1).astype(out_ref.dtype)

    @pl.when(step < half)
    def _():
        work(ms_ref, ss_ref, send_ref)

    @pl.when(step >= half)
    def _():
        work(mk_ref, sk_ref, keep_ref)

    @pl.when(step == 2 * half - 1)
    def _():
        sums_ref[...] = jnp.concatenate(
            [jnp.sum(acc_ref[8 * k : 8 * k + 8, :], axis=0, keepdims=True) for k in range(3)]
            + [jnp.zeros((5, width), F32)],
            axis=0,
        )


def ffn_two(active_k, active_s, slope_k, slope_s, inner_grad, stats, gain, shift, up_w):
    rows, width = active_k.shape
    size = 256
    half = rows // size
    keep = lambda i: jnp.maximum(i - half, 0)
    send = lambda i: jnp.minimum(i, half - 1)
    keep_spec = lambda shape: pl.BlockSpec(shape, lambda i: (keep(i), 0))
    send_spec = lambda shape: pl.BlockSpec(shape, lambda i: (send(i), 0))
    tile = (size, width)
    block = lambda i: (i + half) % (2 * half)
    both = pl.BlockSpec(tile, lambda i: (block(i), 0))
    held = (lambda b: b, lambda b: (b + 2) % 4, lambda b: b + 1 - 2 * (b % 2), lambda b: 3 - b)
    return pl.pallas_call(
        ffn_two_kernel,
        grid=(2 * half,),
        out_shape=(
            shaped((2 * rows, width), BF16),
            shaped((2 * rows, width), BF16),
            shaped((rows, D), BF16),
            shaped((rows, D), F32),
            shaped((8, width), F32),
        ),
        in_specs=[keep_spec(tile), send_spec(tile), keep_spec(tile), send_spec(tile), both]
        + [pl.BlockSpec((8, size), lambda i, at=at: (0, at(block(i)))) for at in held]
        + [VMEM] * 3,
        out_specs=(both, both, send_spec((size, D)), keep_spec((size, D)), VMEM),
        scratch_shapes=[pltpu.VMEM((size, 128), F32), pltpu.VMEM((24, width), F32)],
        cost_estimate=cost(0, 0),
        name="ffn_two",
    )(active_k, active_s, slope_k, slope_s, inner_grad, *stats, row(gain), row(shift), up_w)


def normed_grad_kernel(side_ref, grad_ref, weight_ref, all_ref, cols_ref, sums_ref, middle_ref, ffn_ref,
                       send_ref, keep_ref, late_ref, acc_ref):
    step = pl.program_id(0)
    half = pl.num_programs(0) // 2
    width = late_ref.shape[1]

    @pl.when(step == 0)
    def _():
        acc_ref[...] = jnp.zeros_like(acc_ref)

    grad = dot(grad_ref[...], weight_ref[...], 1, 1)
    unit = (all_ref[...].astype(F32) - cols_ref[:, 0:1]) * cols_ref[:, 1:2]
    for k, value in enumerate((grad * unit, grad)):
        acc_ref[8 * k : 8 * k + 8, :] += fold(value)

    @pl.when(step < half)
    def _():
        send_ref[...] = grad.astype(BF16)

    @pl.when(step >= half)
    def _():
        keep_ref[...] = grad

    @pl.when(step == 2 * half - 1)
    def _():
        here = side_ref[0]
        wide = [
            jnp.concatenate(
                [jnp.where(here == k, sums_ref[r : r + 1, :], 0.0) for k in range(4)], axis=1
            )
            for r in range(3)
        ]
        place = lax.broadcasted_iota(jnp.int32, (4, width), 0) == here
        late_ref[...] = jnp.concatenate(
            [jnp.sum(acc_ref[8 * k : 8 * k + 8, :], axis=0, keepdims=True) for k in range(2)]
            + wide
            + [middle_ref[0:6, :], jnp.zeros((1, width), F32)]
            + [jnp.where(place, ffn_ref[k : k + 1, :], 0.0) for k in range(3)],
            axis=0,
        )


def normed_grad(here, grad_qkv, qkv_w, x_all, cols, sums, middle_sums, ffn_sums):
    length, width = x_all.shape
    size = 256
    half = length // size // 2
    block = lambda i: ((i + half) % (2 * half), 0)
    return pl.pallas_call(
        normed_grad_kernel,
        grid=(2 * half,),
        out_shape=(
            shaped((length // 2, width), BF16),
            shaped((length // 2, width), F32),
            shaped((24, width), F32),
        ),
        in_specs=[
            SMEM,
            pl.BlockSpec((size, grad_qkv.shape[1]), block),
            VMEM,
            pl.BlockSpec((size, width), block),
            pl.BlockSpec((size, 128), block),
            VMEM,
            VMEM,
            VMEM,
        ],
        out_specs=(
            pl.BlockSpec((size, width), lambda i: (jnp.minimum(i, half - 1), 0)),
            pl.BlockSpec((size, width), lambda i: (jnp.maximum(i - half, 0), 0)),
            VMEM,
        ),
        scratch_shapes=[pltpu.VMEM((16, width), F32)],
        cost_estimate=cost(0, 0),
        name="normed_grad",
    )(here, grad_qkv, qkv_w, x_all, cols, sums, middle_sums, ffn_sums)


def last_kernel(keep_ref, got_ref, other_ref, tokens_ref, cols_ref, gain_ref, hidden_ref, grad_ref):
    incoming = keep_ref[...] + got_ref[...].astype(F32) + other_ref[...].astype(F32)
    inverse = cols_ref[:, 1:2]
    unit = (tokens_ref[...].astype(F32) - cols_ref[:, 0:1]) * inverse
    grad_ref[...] = hidden_ref[...] + norm_backward(incoming, unit, inverse, gain_ref[...])


def last(keep, got, other, tokens, cols, gain, grad_hidden):
    rows, width = tokens.shape
    tile = pl.BlockSpec((STEP, width), lambda i: (i, 0))
    return pl.pallas_call(
        last_kernel,
        grid=(rows // STEP,),
        out_shape=shaped((rows, width), F32),
        in_specs=[tile] * 4 + [pl.BlockSpec((STEP, 128), lambda i: (i, 0)), VMEM, tile],
        out_specs=tile,
        cost_estimate=cost(0, 0),
        name="last",
    )(keep, got, other, tokens, cols, row(gain), grad_hidden)


def output_kernel(keep_ref, got_ref, other_ref, tokens_ref, unit2_ref, post_g_ref, post_b_ref, b_down_ref,
                  out_ref):
    hidden = tokens_ref[...].astype(F32) + (unit2_ref[...] * post_g_ref[...] + post_b_ref[...])
    branch = keep_ref[...] + got_ref[...].astype(F32) + other_ref[...].astype(F32)
    out_ref[...] = (hidden + (branch + b_down_ref[...])).astype(BF16)


def output_rows(keep, got, other, tokens, unit2, post_gain, post_bias, b_down):
    rows, width = tokens.shape
    tile = pl.BlockSpec((STEP, width), lambda i: (i, 0))
    return pl.pallas_call(
        output_kernel,
        grid=(rows // STEP,),
        out_shape=shaped((rows, width), BF16),
        in_specs=[tile] * 5 + [VMEM] * 3,
        out_specs=tile,
        cost_estimate=cost(0, 0),
        name="output_rows",
    )(keep, got, other, tokens, unit2, row(post_gain), row(post_bias), row(b_down))


def per_device(
    tokens,
    segments,
    ln1_gain,
    ln1_bias,
    w_query,
    b_query,
    w_key,
    w_value,
    b_value,
    head_scale,
    w_out,
    b_out,
    post_gain,
    post_bias,
    ln2_gain,
    ln2_bias,
    w_up,
    b_up,
    ffn_gain,
    ffn_bias,
    w_down,
    b_down,
    cotangent,
):
    index = lax.axis_index("tensor")
    rows = tokens.shape[0]
    two = 2 * rows
    columns = w_query.shape[1]
    hidden_here = w_up.shape[1]
    shard = D // lax.axis_size("dp")
    order = jnp.array([0, 2, 1, 3], jnp.int32)
    place = order[jnp.arange(4, dtype=jnp.int32) ^ index]
    here = jnp.full((1,), index, jnp.int32)

    def own_part(vector, width):
        return lax.dynamic_slice_in_dim(vector, index * width, width, 0)

    segment = segments[0]
    seg_col, seg_row = segment[:, None], segment[None, :]
    scale_row = row(jnp.repeat(own_part(head_scale, columns // HD), HD))
    qkv_b = jnp.concatenate(
        [own_part(b_query, columns), jnp.zeros((columns,), F32), own_part(b_value, columns)]
    )
    gain_here, shift_here = own_part(ffn_gain, hidden_here), own_part(ffn_bias, hidden_here)
    b_up_here = own_part(b_up, hidden_here)

    order_dp = lax.axis_index("dp") ^ jnp.arange(lax.axis_size("dp"), dtype=jnp.int32)
    quick = shard % 128 == 0 and lax.axis_size("dp") == 8

    attn = None
    if quick:
        packed, tokens = phase(pack(w_query, w_key, w_value, w_out), tokens)
        attn = Shards(packed)
        attn.send(4, 0)
        attn.send(1, 0)
        first = attn.get(4, 1)
    else:
        first = []
        attn_full = [
            lax.all_gather(jnp.concatenate([w_query, w_key, w_value], 1), "dp", axis=0, tiled=True),
            lax.all_gather(w_out, "dp", axis=1, tiled=True),
        ]
        up_full = [lax.all_gather(w_up, "dp", axis=0, tiled=True)]
        down_full = [lax.all_gather(w_down, "dp", axis=1, tiled=True)]
        attn_masks = up_masks = down_masks = None
    x_pair = swap(tokens, "tensor", 2)
    x_side = swap(tokens, "tensor", 1)
    up_s, down_s = Shards(w_up), Shards(w_down)
    own_up, own_down = up_s.held[0], down_s.held[0]
    (x_pair, x_side, own_up, own_down, cotangent, b_up_here, gain_here, shift_here, qkv_b, scale_row,
     seg_col, place, order_dp), first = phase(
        (x_pair, x_side, own_up, own_down, cotangent, b_up_here, gain_here, shift_here, qkv_b,
         scale_row, seg_col, place, order_dp), first)
    if quick:
        attn.put([4, 1], first)

    x_cross = swap(x_pair, "tensor", 1)
    if quick:
        attn.send(2, 0, 4)
        attn.send(1, 4)
        first = attn.get(2, 6, 5)
    g_pair = swap(cotangent, "tensor", 2)
    normed, x_all, cols1 = norm_one([tokens, x_pair, x_side, x_cross], ln1_gain, ln1_bias)
    (normed, x_all, cols1, own_up, own_down, g_pair, cotangent), first = phase(
        (normed, x_all, cols1, own_up, own_down, g_pair, cotangent), first)

    if quick:
        attn.put([2, 6, 5], first)
        attn.send(1, 2, 6)
        up_s.put([0], [own_up])
        up_s.send(4, 0)
        attn_masks, attn_full = attn.all()
        first = up_s.get(4)
    g_side = swap(cotangent, "tensor", 1)
    g_cross = swap(g_pair, "tensor", 1)
    (normed, own_down, own_up, g_side, g_cross), attn_full, first = phase(
        (normed, own_down, own_up, g_side, g_cross), attn_full, first)

    if quick:
        up_s.put([0, 4], [own_up] + first)
        up_s.send(2, 0, 4)
        up_s.send(1, 0, 4)
        first = up_s.get(2, 6, 1, 5)
    qkv, mixed, scaled, lse, qkv_w, out_w, send, keep = attend(
        place, order_dp, normed, attn_masks, attn_full, row(qkv_b), seg_col, seg_row, scale_row
    )
    (qkv, mixed, scaled, lse, qkv_w, out_w, send, keep, own_down, g_side, g_cross), first = phase(
        (qkv, mixed, scaled, lse, qkv_w, out_w, send, keep, own_down, g_side, g_cross), first)

    got = swap(send, "tensor", 1)
    if quick:
        up_s.put([2, 6, 1, 5], first)
        up_s.send(1, 2, 6)
        down_s.put([0], [own_down])
        down_s.send(4, 0)
        first = up_s.get(3, 7) + down_s.get(4)
    low, got, keep, g_side = phase(low_rows(keep, got, two), got, keep, g_side)
    other = swap(low, "tensor", 2)
    (g_all, own_down), first = phase((stack(cotangent, g_pair, g_side, g_cross), own_down), first)
    if quick:
        up_s.put([3, 7], first[:2])
        down_s.put([0, 4], [own_down, first[2]])
        down_s.send(2, 0, 4)
        down_s.send(1, 0, 4)
        other, keep, got = phase(other, keep, got)
        up_masks, up_full = up_s.all()
        first = down_s.get(2, 6, 1, 5)

    ffn_in, unit2, cols = middle(
        keep, got, other, tokens, x_pair, b_out, post_gain, post_bias, ln2_gain, ln2_bias
    )
    (ffn_in, unit2, cols), first = phase((ffn_in, unit2, cols), first)
    ffn_rest = swap(ffn_in, "tensor", 1)
    if quick:
        down_s.put([2, 6, 1, 5], first)
        down_s.send(1, 2, 6)
        down_masks, down_full = down_s.all()
    active_k, slope_k, stats_k, up_w = ffn_one(ffn_in, order_dp, up_masks, up_full, b_up_here)
    active_k, slope_k, stats_k, up_w, ffn_rest = phase(active_k, slope_k, stats_k, up_w, ffn_rest)
    active_s, slope_s, stats_s, _ = ffn_one(ffn_rest, order_dp, None, [up_w], b_up_here)
    (active_s, stats_s, slope_s), down_full = phase((active_s, stats_s, slope_s), down_full)
    inner_grad, stats, down_w = ffn_grad(
        g_all, order_dp, down_masks, down_full, active_k, active_s, stats_k, stats_s, gain_here
    )
    stats = [stats] + [swap(stats, "tensor", mask) for mask in (1, 2, 3)]
    inner, grad_before, send, keep, ffn_sums = ffn_two(
        active_k, active_s, slope_k, slope_s, inner_grad, stats, gain_here, shift_here, up_w
    )

    down_g, up_g, out_g = Scatter(1, shard, 1), Scatter(0, shard), Scatter(1, shard)
    qkv_a, qkv_b = Scatter(0, shard), Scatter(0, shard)
    got = swap(send, "tensor", 1)
    down_send = down_g.product([g_all], inner)
    down_send, down_g.keep, inner, grad_before, got, keep = phase(
        down_send, down_g.keep, inner, grad_before, got, keep
    )
    low, down_send, inner, grad_before = phase(low_rows(keep, got, two), down_send, inner, grad_before)
    other = swap(low, "tensor", 2)
    down_g.start(down_send)
    up_send = up_g.product([ffn_in, ffn_rest], grad_before)
    up_send, up_g.keep, inner = phase(up_send, up_g.keep, inner)
    up_g.start(up_send)
    out_send, out_keep = project(inner, down_w)
    other, down_g.got, out_send, out_keep = phase(other, down_g.got, out_send, out_keep)

    down_send = down_g.split()
    down_send, down_g.keep, other, out_send = phase(down_send, down_g.keep, other, out_send)
    down_g.start(down_send)
    out_got = swap(out_send, "tensor", 1)
    grad_proj, grad_hidden, middle_sums = middle_back(
        keep, got, other, cotangent, g_pair, tokens, x_pair, unit2, cols, post_gain, post_bias,
        ln2_gain,
    )
    grad_proj, up_g.got, out_got, out_keep = phase(grad_proj, up_g.got, out_got, out_keep)
    proj_rest = swap(grad_proj, "tensor", 1)
    up_send = up_g.split()
    out_low = low_rows(out_keep, out_got, rows)
    grad_proj, proj_rest, up_send, up_g.keep, out_low = phase(
        grad_proj, proj_rest, up_send, up_g.keep, out_low
    )
    w_send = out_g.product([grad_proj, proj_rest], scaled)
    w_send, out_g.keep, grad_proj, proj_rest, up_send, out_low = phase(
        w_send, out_g.keep, grad_proj, proj_rest, up_send, out_low
    )

    up_g.start(up_send)
    out_other = swap(out_low, "tensor", 2)
    out_g.start(w_send)
    grad_qkv, sums = attend_back(
        place, qkv, grad_proj, proj_rest, out_w, mixed, lse, seg_col, seg_row, scale_row
    )
    grad_qkv, sums, up_g.got, out_other, out_g.got = phase(
        grad_qkv, sums, up_g.got, out_other, out_g.got
    )

    masks = dp_masks(0)
    up_send, w_send = up_g.split(), out_g.split()
    up_send, up_g.keep, grad_qkv, w_send, out_g.keep = phase(
        up_send, up_g.keep, grad_qkv, w_send, out_g.keep
    )
    up_g.start(up_send)
    out_g.start(w_send)
    a_send = qkv_a.product([normed], grad_qkv, 0, 2)
    a_send, qkv_a.keep, grad_qkv = phase(a_send, qkv_a.keep, grad_qkv)
    qkv_a.start(a_send)
    send, keep, late = normed_grad(
        here, grad_qkv, qkv_w, x_all, cols1, sums, middle_sums, ffn_sums
    )
    b_send = qkv_b.product([normed], grad_qkv, 1, 2)
    send, keep, late, b_send, qkv_b.keep, qkv_a.got, down_g.got, out_g.got = phase(
        send, keep, late, b_send, qkv_b.keep, qkv_a.got, down_g.got, out_g.got
    )
    got = swap(send, "tensor", 1)
    side = swap(late, "tensor", 1)
    qkv_b.start(b_send)
    a_send, w_send, d_send = qkv_a.split(), out_g.split(), down_g.split()
    a_send, qkv_a.keep, w_send, out_g.keep, got, keep, late, d_send, down_g.keep, up_g.got, out_other = phase(
        a_send, qkv_a.keep, w_send, out_g.keep, got, keep, late + side, d_send, down_g.keep, up_g.got,
        out_other
    )
    qkv_a.start(a_send)
    out_g.start(w_send)
    side = swap(late, "tensor", 2)
    low = low_rows(keep, got, rows)
    output = output_rows(out_keep, out_got, out_other, tokens, unit2, post_gain, post_bias, b_down)
    output, low, late, qkv_a.got, qkv_a.keep, qkv_b.got, qkv_b.keep, out_g.got = phase(
        output, low, late + side, qkv_a.got, qkv_a.keep, qkv_b.got, qkv_b.keep, out_g.got
    )
    other = swap(low, "tensor", 2)
    side = swap(late, "dp", masks[0])
    a_send, b_send = qkv_a.split(), qkv_b.split()
    a_send, qkv_a.keep, b_send, qkv_b.keep, late, d_send = phase(
        a_send, qkv_a.keep, b_send, qkv_b.keep, late + side, d_send
    )
    qkv_a.start(a_send)
    side = swap(late, "dp", masks[1])
    qkv_b.start(b_send)
    down_g.start(d_send)
    other, late, qkv_b.got, qkv_b.keep, up_g.got, out_g.got = phase(
        other, late + side, qkv_b.got, qkv_b.keep, up_g.got, out_g.got
    )
    if quick:
        b_send, late = phase(qkv_b.split(), late)
        qkv_b.start(b_send)
    input_grad = last(keep, got, other, tokens, cols1, ln1_gain, grad_hidden)
    g_up, g_out = up_g.finish(), out_g.finish()
    for mask in masks[2:]:
        late = late + swap(late, "dp", mask)
    g_down = down_g.finish()
    g_a, g_b = qkv_a.finish(), qkv_b.finish()
    extra = g_a.shape[1] - columns
    blocks = FF // D
    return (
        output,
        input_grad,
        late[0],
        late[1],
        g_a[:, :columns],
        late[2],
        jnp.concatenate([g_a[:, columns:], g_b[:, : columns - extra]], 1),
        g_b[:, columns - extra :],
        late[3],
        jnp.sum(late[4].reshape(HEADS, HD), axis=1),
        g_out,
        late[9],
        late[7],
        late[8],
        late[5],
        late[6],
        g_up,
        late[12 : 12 + blocks].reshape(FF),
        late[12 + blocks : 12 + 2 * blocks].reshape(FF),
        late[12 + 2 * blocks : 12 + 3 * blocks].reshape(FF),
        g_down,
        late[10],
    )


def solution(mesh):
    return jax.shard_map(
        per_device,
        mesh=mesh,
        in_specs=(
            P(("dp", "tensor"), None),
            P("dp", None),
            P(),
            P(),
            P("dp", "tensor"),
            P(),
            P("dp", "tensor"),
            P("dp", "tensor"),
            P(),
            P(),
            P("tensor", "dp"),
            P(),
            P(),
            P(),
            P(),
            P(),
            P("dp", "tensor"),
            P(),
            P(),
            P(),
            P("tensor", "dp"),
            P(),
            P(("dp", "tensor"), None),
        ),
        out_specs=(
            P(("dp", "tensor"), None),
            P(("dp", "tensor"), None),
            P(),
            P(),
            P("dp", "tensor"),
            P(),
            P("dp", "tensor"),
            P("dp", "tensor"),
            P(),
            P(),
            P("tensor", "dp"),
            P(),
            P(),
            P(),
            P(),
            P(),
            P("dp", "tensor"),
            P(),
            P(),
            P(),
            P("tensor", "dp"),
            P(),
        ),
        check_vma=False,
    )
```

```python
import functools

import jax
import jax.numpy as jnp
from jax import lax
from jax.experimental import pallas as pl
from jax.experimental.pallas import tpu as pltpu
from jax.sharding import PartitionSpec as P

D = 1024
HEADS = 16
HD = 64
FF = 4096
LONGEST = 512
EPS = 1e-05
SCALE = HD ** (-0.5)
F32 = jnp.float32
BF16 = jnp.bfloat16


def dot(left, right, left_dim=1, right_dim=0):
    return lax.dot_general(
        left, right, (((left_dim,), (right_dim,)), ((), ())), preferred_element_type=F32
    )


def swap(value, axis, mask):
    size = lax.axis_size(axis)
    return lax.ppermute(value, axis, [(i, i ^ mask) for i in range(size)])


def bit_of(axis, mask):
    return (lax.axis_index(axis) // mask) % 2


def after(value, *others):
    return lax.optimization_barrier((value,) + others)[0]


def row(vector):
    return vector[None, :]


def each_rows(count, step, body):
    def one(k, carry):
        body(pl.ds(pl.multiple_of(k * step, step), step))
        return carry

    lax.fori_loop(0, count // step, one, 0)


STEP = 128


def fold(value):
    return jnp.sum(value.reshape(value.shape[0] // 8, 8, value.shape[1]), axis=0)


def norm_stats(values):
    mean = jnp.mean(values, axis=-1, keepdims=True)
    centered = values - mean
    inverse = lax.rsqrt(jnp.mean(centered * centered, axis=-1, keepdims=True) + EPS)
    return centered * inverse, inverse


def norm_backward(grad, unit, inverse, gain):
    scaled = grad * gain
    return inverse * (
        scaled
        - jnp.mean(scaled, axis=-1, keepdims=True)
        - unit * jnp.mean(scaled * unit, axis=-1, keepdims=True)
    )


VMEM = pl.BlockSpec(memory_space=pltpu.VMEM)
SMEM = pl.BlockSpec(memory_space=pltpu.SMEM)


def shaped(shape, kind):
    return jax.ShapeDtypeStruct(shape, kind)


def cost(flops, moved, hard=0):
    return pl.CostEstimate(flops=flops, bytes_accessed=moved, transcendentals=hard)


class Shards:
    def __init__(self, shard):
        self.held = {0: shard[None]}

    def send(self, mask, *which):
        for k in which:
            self.held[k ^ mask] = swap(self.held[k], "dp", mask)

    def get(self, *which):
        return [self.held[k] for k in which]

    def put(self, which, values):
        for k, value in zip(which, values):
            self.held[k] = value

    def all(self):
        masks = sorted(self.held)
        return [[k] for k in masks], [self.held[k] for k in masks]


def phase(*values):
    return lax.optimization_barrier(values)


def fill(axis, masks, order_ref, piece_refs, full_ref, start=0, width=None):
    if masks is None:
        full_ref[...] = piece_refs[0][...]
        return
    for group, piece in zip(masks, piece_refs):
        height = piece.shape[1]
        for k, mask in enumerate(group):
            place = order_ref[mask]
            if axis == 0:
                there = pl.ds(pl.multiple_of(place * height, height), height)
                full_ref[there, :] = piece[k, :, start : start + full_ref.shape[1]]
            else:
                there = pl.ds(pl.multiple_of(place * width, width), width)
                for low in range(0, full_ref.shape[0], height):
                    at = start + low // height * width
                    full_ref[low : low + height, there] = piece[k, :, at : at + width]


def pack_kernel(q_ref, k_ref, v_ref, o_ref, out_ref):
    height, width = q_ref.shape
    for k, ref in enumerate((q_ref, k_ref, v_ref)):
        out_ref[:, k * width : (k + 1) * width] = ref[...]
    wide = o_ref.shape[1]
    for k in range(o_ref.shape[0] // height):
        at = 3 * width + k * wide
        out_ref[:, at : at + wide] = o_ref[k * height : (k + 1) * height, :]


def pack(w_query, w_key, w_value, w_out):
    height, width = w_query.shape
    total = 3 * width + w_out.size // height
    return pl.pallas_call(
        pack_kernel,
        out_shape=shaped((height, total), BF16),
        in_specs=[VMEM] * 4,
        out_specs=VMEM,
        cost_estimate=cost(0, 0),
        name="pack",
    )(w_query, w_key, w_value, w_out)


def pick_cols(value, width, bit):
    rows, cols = value.shape
    pairs = cols // (2 * width)
    if width % 128:
        return lax.dynamic_index_in_dim(
            value.reshape(rows, pairs, 2, width), bit, 2, keepdims=False
        ).reshape(rows, pairs * width)
    return jnp.concatenate(
        [
            lax.dynamic_slice_in_dim(value, (2 * p + bit) * width, width, 1)
            for p in range(pairs)
        ],
        1,
    )


def pick_rows(value, height, bit):
    rows, cols = value.shape
    return lax.dynamic_index_in_dim(
        value.reshape(rows // (2 * height), 2, height, cols), bit, 1, keepdims=False
    ).reshape(rows // 2, cols)


def dp_masks(last):
    size = lax.axis_size("dp")
    masks = [1 << k for k in range(size.bit_length() - 1)]
    if last in masks:
        masks.remove(last)
        masks.append(last)
    return masks


def outer_kernel(width, on_left, count, bit_ref, *refs):
    parts, (other_ref, send_ref, keep_ref, *picks) = refs[:count], refs[count:]

    @pl.when(pl.program_id(0) == 0)
    def _():
        for bit, pick_ref in zip((1 - bit_ref[0], bit_ref[0]), picks):
            for p in range(pick_ref.shape[1] // width):
                there = pl.ds(pl.multiple_of((2 * p + bit) * width, width), width)
                row = 0
                for part in parts:
                    pick_ref[row : row + part.shape[0], p * width : (p + 1) * width] = part[:, there]
                    row += part.shape[0]

    for pick_ref, out_ref in zip(picks, (send_ref, keep_ref)):
        if on_left:
            value = dot(pick_ref[...], other_ref[...], 0, 0)
        else:
            value = dot(other_ref[...], pick_ref[...], 0, 0)
        out_ref[...] = value.astype(out_ref.dtype)


def outer(bit, picked, other, width, on_left, part, parts):
    rows, cols = other.shape[0], other.shape[1] // parts
    half = picked[0].shape[1] // 2
    step = 256 if cols % 512 == 0 else cols
    skip = part * (cols // step)
    shape = (half, cols) if on_left else (cols, half)
    tile = (half, step) if on_left else (step, half)
    out = pl.BlockSpec(tile, (lambda i: (0, i)) if on_left else (lambda i: (i, 0)))
    return pl.pallas_call(
        functools.partial(outer_kernel, width, on_left, len(picked)),
        grid=(cols // step,),
        out_shape=(shaped(shape, BF16), shaped(shape, F32)),
        in_specs=[SMEM] + [VMEM] * len(picked) + [pl.BlockSpec((rows, step), lambda i: (0, i + skip))],
        out_specs=(out,) * 2,
        scratch_shapes=[pltpu.VMEM((rows, half), BF16)] * 2,
        cost_estimate=cost(0, 0),
        name="outer",
    )(bit, *picked, other)


def split_kernel(axis, width, bit_ref, keep_ref, got_ref, send_ref, stay_ref):
    for bit, out_ref in ((1 - bit_ref[0], send_ref), (bit_ref[0], stay_ref)):
        for p in range(out_ref.shape[axis] // width):
            there = pl.ds(pl.multiple_of((2 * p + bit) * width, width), width)
            here = slice(p * width, (p + 1) * width)
            source, target = ((there, slice(None)), (here, slice(None)))
            if axis == 1:
                source, target = source[::-1], target[::-1]
            value = keep_ref[source] + got_ref[source].astype(F32)
            out_ref[target] = value.astype(out_ref.dtype)


def split(bit, keep, got, width, axis):
    cut = lambda shape: tuple(n // 2 if k == axis else n for k, n in enumerate(shape))
    size = keep.shape[1 - axis]
    step = size // 2 if size % 256 == 0 else size
    tile = tuple(n if k == axis else step for k, n in enumerate(keep.shape))
    index = (lambda i: (0, i)) if axis == 0 else (lambda i: (i, 0))
    return pl.pallas_call(
        functools.partial(split_kernel, axis, width),
        grid=(size // step,),
        out_shape=(shaped(cut(keep.shape), BF16), shaped(cut(keep.shape), F32)),
        in_specs=[SMEM, pl.BlockSpec(tile, index), pl.BlockSpec(tile, index)],
        out_specs=(pl.BlockSpec(cut(tile), index),) * 2,
        cost_estimate=cost(16 * 10**9, 0),
        name="split",
    )(bit, keep, got)


class Scatter:
    def __init__(self, axis, extent, last=0):
        self.axis, self.extent, self.masks = axis, extent, dp_masks(last)

    def place(self):
        mask = self.masks[0]
        lower = sum(1 for other in self.masks if other < mask)
        return bit_of("dp", mask), self.extent << lower

    def product(self, picked, other, part=0, parts=1):
        bit, width = self.place()
        if width % 128 == 0:
            bit = jnp.full((1,), bit, jnp.int32)
            send, self.keep = outer(bit, picked, other, width, self.axis == 0, part, parts)
            return send
        span = other.shape[1] // parts
        other = other[:, part * span : (part + 1) * span]
        picked = jnp.concatenate(picked, 0)
        send, keep = pick_cols(picked, width, 1 - bit), pick_cols(picked, width, bit)
        if self.axis == 0:
            send, self.keep = dot(send, other, 0, 0), dot(keep, other, 0, 0)
        else:
            send, self.keep = dot(other, send, 0, 0), dot(other, keep, 0, 0)
        return send.astype(BF16)

    def start(self, send):
        self.got = swap(send, "dp", self.masks.pop(0))

    def split(self):
        bit, width = self.place()
        if width % 128 == 0:
            send, self.keep = split(jnp.full((1,), bit, jnp.int32), self.keep, self.got, width, self.axis)
            return send
        pick = (pick_rows, pick_cols)[self.axis]
        total = self.keep + self.got.astype(F32)
        self.keep = pick(total, width, bit)
        return pick(total, width, 1 - bit).astype(BF16)

    def finish(self):
        while self.masks:
            self.start(self.split())
        return self.keep + self.got.astype(F32)


def low_kernel(keep_ref, got_ref, out_ref):
    out_ref[...] = (keep_ref[...] + got_ref[...].astype(F32)).astype(BF16)


def low_rows(keep, got, rows):
    total, width = keep.shape
    step = rows // 2
    first = (total - rows) // step
    there = pl.BlockSpec((step, width), lambda i: (i + first, 0))
    return pl.pallas_call(
        low_kernel,
        grid=(rows // step,),
        out_shape=shaped((rows, width), BF16),
        in_specs=[there, there],
        out_specs=pl.BlockSpec((step, width), lambda i: (i, 0)),
        cost_estimate=cost(16 * 10**9, 0),
        name="low_rows",
    )(keep, got)


def stack_kernel(*refs):
    *parts, out_ref = refs
    row = 0
    for part in parts:
        out_ref[row : row + part.shape[0], :] = part[...]
        row += part.shape[0]


def stack(*parts):
    return pl.pallas_call(
        stack_kernel,
        out_shape=shaped((sum(part.shape[0] for part in parts), parts[0].shape[1]), parts[0].dtype),
        in_specs=[VMEM] * len(parts),
        out_specs=VMEM,
        cost_estimate=cost(0, 0),
        name="stack",
    )(*parts)


def project_kernel(inner_ref, weight_ref, send_ref, keep_ref):
    half = inner_ref.shape[0] // 2
    step = half // 2

    def body(rows):
        later = pl.ds(pl.multiple_of(half + rows.start, step), step)
        send_ref[rows, :] = dot(inner_ref[later, :], weight_ref[...]).astype(BF16)
        keep_ref[rows, :] = dot(inner_ref[rows, :], weight_ref[...])

    each_rows(half, step, body)


def project(inner, weight):
    half = inner.shape[0] // 2
    return pl.pallas_call(
        project_kernel,
        out_shape=(shaped((half, D), BF16), shaped((half, D), F32)),
        in_specs=[VMEM] * 2,
        out_specs=(VMEM,) * 2,
        cost_estimate=cost(0, 0),
        name="project",
    )(inner, weight)


def norm_one_kernel(a_ref, b_ref, c_ref, d_ref, gain_ref, bias_ref, out_ref, all_ref, cols_ref):
    step = pl.program_id(0)
    per = pl.num_programs(0) // 4
    value = jnp.where(
        step < 2 * per,
        jnp.where(step < per, a_ref[...], b_ref[...]),
        jnp.where(step < 3 * per, c_ref[...], d_ref[...]),
    )
    all_ref[...] = value
    value = value.astype(F32)
    mean = jnp.mean(value, axis=-1, keepdims=True)
    centered = value - mean
    inverse = lax.rsqrt(jnp.mean(centered * centered, axis=-1, keepdims=True) + EPS)
    lane = lax.broadcasted_iota(jnp.int32, cols_ref.shape, 1)
    cols_ref[...] = jnp.where(lane == 0, mean, inverse)
    out_ref[...] = (centered * inverse * gain_ref[...] + bias_ref[...]).astype(BF16)


def norm_one(parts, gain, bias):
    rows, width = parts[0].shape
    per = rows // STEP

    def spec(first, count, width=width):
        return pl.BlockSpec((STEP, width), lambda i: (jnp.clip(i - first, 0, count - 1), 0))

    return pl.pallas_call(
        norm_one_kernel,
        grid=(4 * per,),
        out_shape=(
            shaped((4 * rows, width), BF16),
            shaped((4 * rows, width), BF16),
            shaped((4 * rows, 128), F32),
        ),
        in_specs=[spec(k * per, per) for k in range(4)] + [VMEM, VMEM],
        out_specs=(spec(0, 4 * per), spec(0, 4 * per), spec(0, 4 * per, 128)),
        cost_estimate=cost(0, 0),
        name="norm_one",
    )(*parts, row(gain), row(bias))


def key_range(block, size):
    low = max(0, block * size - (LONGEST // size) * size)
    return low, (block + 1) * size - low


def write_bias(bias_ref, seg_col_ref, seg_row_ref, rows, keys_at):
    shape = (keys_at.size, rows.size)
    key_pos = keys_at.start + lax.broadcasted_iota(jnp.int32, shape, 0)
    row_pos = rows.start + lax.broadcasted_iota(jnp.int32, shape, 1)
    same = seg_col_ref[keys_at, :] == seg_row_ref[:, rows]
    bias_ref[: keys_at.size, :] = jnp.where((key_pos <= row_pos) & same, 0.0, -1000000000.0)


def each_block(blocks, size, body):
    short = min(LONGEST // size, blocks)
    for block in range(short):
        body(block, *key_range(block, size))

    def one(block, carry):
        low = pl.multiple_of((block - short) * size, size)
        body(block, low, (short + 1) * size)
        return carry

    lax.fori_loop(short, blocks, one, 0)


def attend_kernel(size, masks, place_ref, order_ref, normed_ref, qkv_b_ref, seg_col_ref, seg_row_ref,
                  scale_ref, *refs):
    *pieces, qkv_ref, o_ref, u_ref, lse_ref, qkv_w_ref, out_w_ref, send_ref, keep_ref = refs[:-3]
    bias_ref, vt_ref, ot_ref = refs[-3:]
    length, width = o_ref.shape
    heads = width // HD
    if masks is None:
        qkv_w_ref[...] = pieces[0][...]
        out_w_ref[...] = pieces[1][...]
    else:
        fill(0, masks, order_ref, pieces, qkv_w_ref)
        fill(1, masks, order_ref, pieces, out_w_ref, 3 * width, pieces[0].shape[1])
    head_of = lax.broadcasted_iota(jnp.int32, (size, width), 1) // HD
    def project_block(block, carry):
        rows = pl.ds(pl.multiple_of(block * size, size), size)
        here = pl.ds(pl.multiple_of(place_ref[block] * size, size), size)
        product = dot(normed_ref[here, :], qkv_w_ref[...]) + qkv_b_ref[...]
        qkv_ref[rows, :] = product.astype(BF16)
        vt_ref[:, rows] = product[:, 2 * width :].T.astype(BF16)
        return carry

    def attend_block(block, low, count):
        rows, keys_at = pl.ds(block * size, size), pl.ds(low, count)
        here = pl.ds(pl.multiple_of(place_ref[block] * size, size), size)
        write_bias(bias_ref, seg_col_ref, seg_row_ref, rows, keys_at)
        query = qkv_ref[rows, :width].astype(F32) * SCALE
        keys = qkv_ref[keys_at, width : 2 * width]
        for head in range(heads):
            masked = jnp.where(head_of == head, query, 0.0).astype(BF16)
            scores = dot(keys, masked, 1, 1) + bias_ref[:count, :]
            highest = jnp.max(scores, axis=0, keepdims=True)
            raised = jnp.exp(scores - highest)
            total = jnp.sum(raised, axis=0, keepdims=True)
            lse_ref[block, head : head + 1, :] = highest + jnp.log(total)
            probs = (raised * (1.0 / total)).astype(BF16)
            part = slice(head * HD, (head + 1) * HD)
            ot_ref[part, :] = dot(vt_ref[part, keys_at], probs)
        mixed = ot_ref[...].T
        o_ref[rows, :] = mixed
        u_ref[here, :] = (mixed * scale_ref[...]).astype(BF16)

    lax.fori_loop(0, length // size, project_block, 0)
    each_block(length // size, size, attend_block)
    half = length // 2
    send_ref[...] = dot(u_ref[half:, :], out_w_ref[...]).astype(BF16)
    keep_ref[...] = dot(u_ref[:half, :], out_w_ref[...])


def attend_back_kernel(size, place_ref, qkv_ref, own_ref, rest_ref, out_w_ref, o_ref, lse_ref,
                       seg_col_ref, seg_row_ref, scale_ref, dqkv_ref, sums_ref,
                       bias_ref, kt_ref, dqt_ref, probs_ref, ds_ref, q_ref, do_ref, dk_ref, dv_ref,
                       du_ref, acc_ref):
    length, width = o_ref.shape
    heads = width // HD
    du_ref[: length // 2, :] = dot(own_ref[...], out_w_ref[...], 1, 1)
    du_ref[length // 2 :, :] = dot(rest_ref[...], out_w_ref[...], 1, 1)
    kt_ref[...] = qkv_ref[:, width : 2 * width].astype(F32).T.astype(BF16)
    head_of = lax.broadcasted_iota(jnp.int32, (size, width), 1) // HD
    blocks = length // size
    acc_ref[...] = jnp.zeros_like(acc_ref)

    def back_block(block, low, count):
        rows, keys_at = pl.ds(block * size, size), pl.ds(low, count)
        here = pl.ds(pl.multiple_of(place_ref[block] * size, size), size)
        write_bias(bias_ref, seg_col_ref, seg_row_ref, rows, keys_at)
        query = qkv_ref[rows, :width].astype(F32) * SCALE
        keys = qkv_ref[keys_at, width : 2 * width]
        values = qkv_ref[keys_at, 2 * width :]
        du = du_ref[here, :]
        acc_ref[0:8, :] += fold(du * o_ref[rows, :])
        grad = du * scale_ref[...]
        for head in range(heads):
            masked = jnp.where(head_of == head, query, 0.0).astype(BF16)
            grad_here = jnp.where(head_of == head, grad, 0.0).astype(BF16)
            stack = slice(head * size, (head + 1) * size)
            q_ref[stack, :] = masked
            do_ref[stack, :] = grad_here
            scores = dot(keys, masked, 1, 1) + bias_ref[:count, :]
            full = jnp.exp(scores - lse_ref[block, head : head + 1, :])
            probs_ref[:count, stack] = full.astype(BF16)
            dp = dot(values, grad_here, 1, 1)
            delta = jnp.sum(full * dp, axis=0, keepdims=True)
            ds = (full * (dp - delta)).astype(BF16)
            ds_ref[:count, stack] = ds
            part = slice(head * HD, (head + 1) * HD)
            dqt_ref[part, :] = dot(kt_ref[part, keys_at], ds)
        dq = (dqt_ref[...].T * SCALE).astype(BF16)
        dqkv_ref[here, :width] = dq
        acc_ref[8:16, :] += fold(dq.astype(F32))
        dk = dot(ds_ref[:count, :], q_ref[...])
        dv = dot(probs_ref[:count, :], do_ref[...])
        old = count - size
        if old:
            before = pl.ds(low, old)
            dk_ref[before, :] += dk[:old]
            dv_ref[before, :] += dv[:old]
        dk_ref[rows, :] = dk[old:]
        dv_ref[rows, :] = dv[old:]

    each_block(blocks, size, back_block)

    def finish_block(block, carry):
        rows = pl.ds(pl.multiple_of(block * size, size), size)
        here = pl.ds(pl.multiple_of(place_ref[block] * size, size), size)
        dqkv_ref[here, width : 2 * width] = dk_ref[rows, :].astype(BF16)
        dv = dv_ref[rows, :].astype(BF16)
        dqkv_ref[here, 2 * width :] = dv
        acc_ref[16:24, :] += fold(dv.astype(F32))
        return carry

    lax.fori_loop(0, blocks, finish_block, 0)
    sums_ref[...] = jnp.concatenate(
        [jnp.sum(acc_ref[8 * k : 8 * k + 8, :], axis=0, keepdims=True) for k in (1, 2, 0)]
        + [jnp.zeros((5, width), F32)],
        axis=0,
    )


def attend(place, order, normed, masks, pieces, qkv_b, seg_col, seg_row, scale_row):
    length, width = normed.shape[0], scale_row.shape[1]
    size = length // 4
    heads = width // HD
    most = LONGEST + size
    return pl.pallas_call(
        functools.partial(attend_kernel, size, masks),
        out_shape=(
            shaped((length, 3 * width), BF16),
            shaped((length, width), F32),
            shaped((length, width), BF16),
            shaped((4, heads, size), F32),
            shaped((D, 3 * width), BF16),
            shaped((width, D), BF16),
            shaped((length // 2, D), BF16),
            shaped((length // 2, D), F32),
        ),
        in_specs=[SMEM] * 2 + [VMEM] * (5 + len(pieces)),
        out_specs=(VMEM,) * 8,
        scratch_shapes=[
            pltpu.VMEM((most, size), F32),
            pltpu.VMEM((width, length), BF16),
            pltpu.VMEM((width, size), F32),
        ],
        cost_estimate=cost(0, 0),
        name="attend",
    )(place, order, normed, qkv_b, seg_col, seg_row, scale_row, *pieces)


def attend_back(place, qkv, own, rest, out_w, mixed, lse, seg_col, seg_row, scale_row):
    length, width = mixed.shape
    size = length // 4
    heads = width // HD
    most = LONGEST + size
    pairs = 4 * heads * most * size
    return pl.pallas_call(
        functools.partial(attend_back_kernel, size),
        out_shape=(shaped((length, 3 * width), BF16), shaped((8, width), F32)),
        in_specs=[SMEM] + [VMEM] * 9,
        out_specs=(VMEM,) * 2,
        scratch_shapes=[
            pltpu.VMEM((most, size), F32),
            pltpu.VMEM((width, length), BF16),
            pltpu.VMEM((width, size), F32),
            pltpu.VMEM((most, heads * size), BF16),
            pltpu.VMEM((most, heads * size), BF16),
            pltpu.VMEM((heads * size, width), BF16),
            pltpu.VMEM((heads * size, width), BF16),
            pltpu.VMEM((length, width), F32),
            pltpu.VMEM((length, width), F32),
            pltpu.VMEM((length, width), F32),
            pltpu.VMEM((24, width), F32),
        ],
        cost_estimate=cost(16 * 10**9, 0),
        name="attend_back",
    )(place, qkv, own, rest, out_w, mixed, lse, seg_col, seg_row, scale_row)


def middle_kernel(keep_ref, got_ref, other_ref, mine_ref, pair_ref, b_out_ref, post_g_ref, post_b_ref,
                  ln2_g_ref, ln2_b_ref, ffn_in_ref, unit2_ref, cols_ref):
    first = pl.program_id(0) < pl.num_programs(0) // 2
    tokens = jnp.where(first, mine_ref[...], pair_ref[...]).astype(F32)
    part = keep_ref[...] + got_ref[...].astype(F32)
    projected = part + other_ref[...].astype(F32) + b_out_ref[...]
    unit2, inv2 = norm_stats(projected)
    unit2_ref[...] = unit2
    hidden = tokens + (unit2 * post_g_ref[...] + post_b_ref[...])
    mean3 = jnp.mean(hidden, axis=-1, keepdims=True)
    centered = hidden - mean3
    inv3 = lax.rsqrt(jnp.mean(centered * centered, axis=-1, keepdims=True) + EPS)
    ffn_in_ref[...] = (centered * inv3 * ln2_g_ref[...] + ln2_b_ref[...]).astype(BF16)
    lane = lax.broadcasted_iota(jnp.int32, cols_ref.shape, 1)
    cols_ref[...] = jnp.where(lane == 0, inv2, jnp.where(lane == 1, mean3, inv3))


def pair_specs(rows, width):
    half = rows // 2 // STEP
    straight = pl.BlockSpec((STEP, width), lambda i: (i, 0))
    crossed = pl.BlockSpec((STEP, width), lambda i: ((i + half) % (2 * half), 0))
    mine = pl.BlockSpec((STEP, width), lambda i: (jnp.minimum(i, half - 1), 0))
    theirs = pl.BlockSpec((STEP, width), lambda i: (jnp.maximum(i - half, 0), 0))
    return straight, crossed, mine, theirs


def middle(keep, got, other, mine, pair, b_out, post_gain, post_bias, ln2_gain, ln2_bias):
    rows, width = keep.shape
    straight, crossed, own, theirs = pair_specs(rows, width)
    columns = pl.BlockSpec((STEP, 128), lambda i: (i, 0))
    return pl.pallas_call(
        middle_kernel,
        grid=(rows // STEP,),
        out_shape=(
            shaped((rows, width), BF16),
            shaped((rows, width), F32),
            shaped((rows, 128), F32),
        ),
        in_specs=[straight, straight, crossed, own, theirs] + [VMEM] * 5,
        out_specs=(straight, straight, columns),
        cost_estimate=cost(0, 0),
        name="middle",
    )(keep, got, other, mine, pair, row(b_out), row(post_gain), row(post_bias), row(ln2_gain),
      row(ln2_bias))


def middle_back_kernel(keep_ref, got_ref, other_ref, mine_ref, pair_ref, tokens_ref, tokens2_ref,
                       unit2_ref, cols_ref, post_g_ref, post_b_ref, ln2_g_ref, proj_ref, grad_ref, sums_ref,
                       acc_ref):
    step = pl.program_id(0)
    half = pl.num_programs(0) // 2
    first = step < half

    @pl.when(step == 0)
    def _():
        acc_ref[...] = jnp.zeros_like(acc_ref)

    part = keep_ref[...] + got_ref[...].astype(F32)
    incoming = part + other_ref[...].astype(F32)
    tokens = jnp.where(first, tokens_ref[...], tokens2_ref[...]).astype(F32)
    unit2 = unit2_ref[...]
    inv2, mean3, inv3 = (cols_ref[:, k : k + 1] for k in range(3))
    hidden = tokens + (unit2 * post_g_ref[...] + post_b_ref[...])
    unit3 = (hidden - mean3) * inv3
    outgoing = jnp.where(first, mine_ref[...], pair_ref[...]).astype(F32)
    grad = outgoing + norm_backward(incoming, unit3, inv3, ln2_g_ref[...])
    proj = norm_backward(grad, unit2, inv2, post_g_ref[...]).astype(BF16)
    proj_ref[...] = proj

    @pl.when(first)
    def _():
        grad_ref[...] = grad
        for k, value in enumerate(
            (incoming * unit3, incoming, grad * unit2, grad, proj.astype(F32), outgoing)
        ):
            acc_ref[8 * k : 8 * k + 8, :] += fold(value)

    @pl.when(step == half - 1)
    def _():
        sums_ref[...] = jnp.concatenate(
            [jnp.sum(acc_ref[8 * k : 8 * k + 8, :], axis=0, keepdims=True) for k in range(6)]
            + [jnp.zeros((2, acc_ref.shape[1]), F32)],
            axis=0,
        )


def middle_back(keep, got, other, mine, pair, tokens, tokens2, unit2, cols, post_gain, post_bias,
                ln2_gain):
    rows, width = keep.shape
    straight, crossed, own, theirs = pair_specs(rows, width)
    columns = pl.BlockSpec((STEP, 128), lambda i: (i, 0))
    return pl.pallas_call(
        middle_back_kernel,
        grid=(rows // STEP,),
        out_shape=(
            shaped((rows, width), BF16),
            shaped((rows // 2, width), F32),
            shaped((8, width), F32),
        ),
        in_specs=[straight, straight, crossed, own, theirs, own, theirs, straight, columns] + [VMEM] * 3,
        out_specs=(straight, own, VMEM),
        scratch_shapes=[pltpu.VMEM((48, width), F32)],
        cost_estimate=cost(0, 0),
        name="middle_back",
    )(keep, got, other, mine, pair, tokens, tokens2, unit2, cols, row(post_gain), row(post_bias),
      row(ln2_gain))


def ffn_one_kernel(masks, order_ref, in_ref, b_up_ref, *refs):
    *pieces, active_ref, slope_ref, stats_ref, up_ref, cols_ref = refs

    @pl.when(pl.program_id(0) == 0)
    def _():
        fill(0, masks, order_ref, pieces, up_ref)

    active_ref[...] = dot(in_ref[...], up_ref[...]) + b_up_ref[...]
    lane = lax.broadcasted_iota(jnp.int32, (STEP, 128), 1)

    def body(rows):
        before = active_ref[rows, :]
        cdf = 0.5 * (1.0 + lax.erf(before * 0.7071067811865476))
        active = before * cdf
        density = jnp.exp(-0.5 * before * before) * 0.3989422804014327
        slope_ref[rows, :] = cdf + before * density
        active_ref[rows, :] = active
        mean = jnp.mean(active, axis=-1, keepdims=True)
        off = active - mean
        square = jnp.sum(off * off, axis=-1, keepdims=True)
        cols_ref[rows, :] = jnp.where(lane == 0, mean, square)

    each_rows(active_ref.shape[0], STEP, body)
    stats_ref[...] = cols_ref[...].T[:8, :]


def ffn_one(ffn_in, order, masks, pieces, b_up):
    rows, width = ffn_in.shape[0], b_up.shape[0]
    size = 256
    tile = pl.BlockSpec((size, width), lambda i: (i, 0))
    return pl.pallas_call(
        functools.partial(ffn_one_kernel, masks),
        grid=(rows // size,),
        out_shape=(
            shaped((rows, width), F32),
            shaped((rows, width), F32),
            shaped((8, rows), F32),
            shaped((D, width), BF16),
        ),
        in_specs=[SMEM, pl.BlockSpec((size, D), lambda i: (i, 0)), VMEM] + [VMEM] * len(pieces),
        out_specs=(tile, tile, pl.BlockSpec((8, size), lambda i: (0, i)), VMEM),
        scratch_shapes=[pltpu.VMEM((size, 128), F32)],
        cost_estimate=cost(0, 0),
        name="ffn_one",
    )(order, ffn_in, row(b_up), *pieces)


def ffn_grad_kernel(masks, order_ref, grad_ref, keep_ref, send_ref, stats_k_ref, stats_s_ref, gain_ref,
                    *refs):
    *pieces, inner_ref, stats_ref, down_ref, cols_ref = refs
    step = pl.program_id(0)
    first = step < pl.num_programs(0) // 2

    @pl.when(step == 0)
    def _():
        fill(1, masks, order_ref, pieces, down_ref, 0, pieces[0].shape[-1])

    inner_ref[...] = dot(grad_ref[...], down_ref[...], 1, 1)
    lane = lax.broadcasted_iota(jnp.int32, (STEP, 128), 1)

    def body(rows):
        active = jnp.where(first, keep_ref[rows, :], send_ref[rows, :])
        scaled = inner_ref[rows, :] * gain_ref[...]
        plain = jnp.sum(scaled, axis=-1, keepdims=True)
        cross = jnp.sum(scaled * active, axis=-1, keepdims=True)
        cols_ref[rows, :] = jnp.where(lane == 2, plain, cross)

    each_rows(inner_ref.shape[0], STEP, body)
    stats = jnp.where(first, stats_k_ref[...], stats_s_ref[...])
    index = lax.broadcasted_iota(jnp.int32, stats.shape, 0)
    stats_ref[...] = jnp.where(index < 2, stats, cols_ref[...].T[:8, :])


def ffn_grad(grad, order, masks, pieces, active_k, active_s, stats_k, stats_s, gain):
    rows, width = grad.shape[0], gain.shape[0]
    size = 256
    half = rows // size // 2
    keep = lambda i: jnp.minimum(i, half - 1)
    send = lambda i: jnp.maximum(i - half, 0)
    tile = (size, width)
    return pl.pallas_call(
        functools.partial(ffn_grad_kernel, masks),
        grid=(rows // size,),
        out_shape=(
            shaped((rows, width), F32),
            shaped((8, rows), F32),
            shaped((width, D), BF16),
        ),
        in_specs=[
            SMEM,
            pl.BlockSpec((size, D), lambda i: (i, 0)),
            pl.BlockSpec(tile, lambda i: (keep(i), 0)),
            pl.BlockSpec(tile, lambda i: (send(i), 0)),
            pl.BlockSpec((8, size), lambda i: (0, keep(i))),
            pl.BlockSpec((8, size), lambda i: (0, send(i))),
            VMEM,
        ]
        + [VMEM] * len(pieces),
        out_specs=(
            pl.BlockSpec(tile, lambda i: (i, 0)),
            pl.BlockSpec((8, size), lambda i: (0, i)),
            VMEM,
        ),
        scratch_shapes=[pltpu.VMEM((size, 128), F32)],
        cost_estimate=cost(0, 0),
        name="ffn_grad",
    )(order, grad, active_k, active_s, stats_k, stats_s, row(gain), *pieces)


def ffn_two_kernel(mk_ref, ms_ref, sk_ref, ss_ref, grad_ref, s0_ref, s1_ref, s2_ref, s3_ref, gain_ref,
                   shift_ref, up_ref, inner_ref, before_ref, send_ref, keep_ref, sums_ref, cols_ref,
                   acc_ref):
    step = pl.program_id(0)
    half = pl.num_programs(0) // 2
    count, width = inner_ref.shape

    @pl.when(step == 0)
    def _():
        acc_ref[...] = jnp.zeros_like(acc_ref)

    values = [ref[...] for ref in (s0_ref, s1_ref, s2_ref, s3_ref)]
    mean = 0.25 * ((values[0][0:1] + values[1][0:1]) + (values[2][0:1] + values[3][0:1]))
    square = plain = cross = jnp.zeros_like(mean)
    for value in values:
        gap = value[0:1] - mean
        square = square + (value[1:2] + width * (gap * gap))
        plain = plain + value[2:3]
        cross = cross + value[3:4]
    inverse = lax.rsqrt(square / FF + EPS)
    cross = (cross - mean * plain) * inverse
    table = jnp.concatenate(
        [mean, inverse, plain / FF, cross / FF, jnp.zeros((124, count), F32)], axis=0
    )
    cols_ref[...] = table.T

    def work(active_ref, slope_ref, out_ref):
        def body(rows):
            cols = cols_ref[rows, :]
            mean, inverse, plain, cross = (cols[:, k : k + 1] for k in range(4))
            unit = (active_ref[rows, :] - mean) * inverse
            inner_ref[rows, :] = (unit * gain_ref[...] + shift_ref[...]).astype(BF16)
            grad = grad_ref[rows, :]
            moved = inverse * (grad * gain_ref[...] - plain - unit * cross)
            before = (moved * slope_ref[rows, :]).astype(BF16)
            before_ref[rows, :] = before
            for k, value in enumerate((before.astype(F32), grad * unit, grad)):
                acc_ref[8 * k : 8 * k + 8, :] += fold(value)

        each_rows(count, STEP, body)
        out_ref[...] = dot(before_ref[...], up_ref[...], 1, 1).astype(out_ref.dtype)

    @pl.when(step < half)
    def _():
        work(ms_ref, ss_ref, send_ref)

    @pl.when(step >= half)
    def _():
        work(mk_ref, sk_ref, keep_ref)

    @pl.when(step == 2 * half - 1)
    def _():
        sums_ref[...] = jnp.concatenate(
            [jnp.sum(acc_ref[8 * k : 8 * k + 8, :], axis=0, keepdims=True) for k in range(3)]
            + [jnp.zeros((5, width), F32)],
            axis=0,
        )


def ffn_two(active_k, active_s, slope_k, slope_s, inner_grad, stats, gain, shift, up_w):
    rows, width = active_k.shape
    size = 256
    half = rows // size
    keep = lambda i: jnp.maximum(i - half, 0)
    send = lambda i: jnp.minimum(i, half - 1)
    keep_spec = lambda shape: pl.BlockSpec(shape, lambda i: (keep(i), 0))
    send_spec = lambda shape: pl.BlockSpec(shape, lambda i: (send(i), 0))
    tile = (size, width)
    block = lambda i: (i + half) % (2 * half)
    both = pl.BlockSpec(tile, lambda i: (block(i), 0))
    held = (lambda b: b, lambda b: (b + 2) % 4, lambda b: b + 1 - 2 * (b % 2), lambda b: 3 - b)
    return pl.pallas_call(
        ffn_two_kernel,
        grid=(2 * half,),
        out_shape=(
            shaped((2 * rows, width), BF16),
            shaped((2 * rows, width), BF16),
            shaped((rows, D), BF16),
            shaped((rows, D), F32),
            shaped((8, width), F32),
        ),
        in_specs=[keep_spec(tile), send_spec(tile), keep_spec(tile), send_spec(tile), both]
        + [pl.BlockSpec((8, size), lambda i, at=at: (0, at(block(i)))) for at in held]
        + [VMEM] * 3,
        out_specs=(both, both, send_spec((size, D)), keep_spec((size, D)), VMEM),
        scratch_shapes=[pltpu.VMEM((size, 128), F32), pltpu.VMEM((24, width), F32)],
        cost_estimate=cost(0, 0),
        name="ffn_two",
    )(active_k, active_s, slope_k, slope_s, inner_grad, *stats, row(gain), row(shift), up_w)


def normed_grad_kernel(side_ref, grad_ref, weight_ref, all_ref, cols_ref, sums_ref, middle_ref, ffn_ref,
                       send_ref, keep_ref, late_ref, acc_ref):
    step = pl.program_id(0)
    half = pl.num_programs(0) // 2
    width = late_ref.shape[1]

    @pl.when(step == 0)
    def _():
        acc_ref[...] = jnp.zeros_like(acc_ref)

    grad = dot(grad_ref[...], weight_ref[...], 1, 1)
    unit = (all_ref[...].astype(F32) - cols_ref[:, 0:1]) * cols_ref[:, 1:2]
    for k, value in enumerate((grad * unit, grad)):
        acc_ref[8 * k : 8 * k + 8, :] += fold(value)

    @pl.when(step < half)
    def _():
        send_ref[...] = grad.astype(BF16)

    @pl.when(step >= half)
    def _():
        keep_ref[...] = grad

    @pl.when(step == 2 * half - 1)
    def _():
        here = side_ref[0]
        wide = [
            jnp.concatenate(
                [jnp.where(here == k, sums_ref[r : r + 1, :], 0.0) for k in range(4)], axis=1
            )
            for r in range(3)
        ]
        place = lax.broadcasted_iota(jnp.int32, (4, width), 0) == here
        late_ref[...] = jnp.concatenate(
            [jnp.sum(acc_ref[8 * k : 8 * k + 8, :], axis=0, keepdims=True) for k in range(2)]
            + wide
            + [middle_ref[0:6, :], jnp.zeros((1, width), F32)]
            + [jnp.where(place, ffn_ref[k : k + 1, :], 0.0) for k in range(3)],
            axis=0,
        )


def normed_grad(here, grad_qkv, qkv_w, x_all, cols, sums, middle_sums, ffn_sums):
    length, width = x_all.shape
    size = 256
    half = length // size // 2
    block = lambda i: ((i + half) % (2 * half), 0)
    return pl.pallas_call(
        normed_grad_kernel,
        grid=(2 * half,),
        out_shape=(
            shaped((length // 2, width), BF16),
            shaped((length // 2, width), F32),
            shaped((24, width), F32),
        ),
        in_specs=[
            SMEM,
            pl.BlockSpec((size, grad_qkv.shape[1]), block),
            VMEM,
            pl.BlockSpec((size, width), block),
            pl.BlockSpec((size, 128), block),
            VMEM,
            VMEM,
            VMEM,
        ],
        out_specs=(
            pl.BlockSpec((size, width), lambda i: (jnp.minimum(i, half - 1), 0)),
            pl.BlockSpec((size, width), lambda i: (jnp.maximum(i - half, 0), 0)),
            VMEM,
        ),
        scratch_shapes=[pltpu.VMEM((16, width), F32)],
        cost_estimate=cost(0, 0),
        name="normed_grad",
    )(here, grad_qkv, qkv_w, x_all, cols, sums, middle_sums, ffn_sums)


def last_kernel(keep_ref, got_ref, other_ref, tokens_ref, cols_ref, gain_ref, hidden_ref, grad_ref):
    incoming = keep_ref[...] + got_ref[...].astype(F32) + other_ref[...].astype(F32)
    inverse = cols_ref[:, 1:2]
    unit = (tokens_ref[...].astype(F32) - cols_ref[:, 0:1]) * inverse
    grad_ref[...] = hidden_ref[...] + norm_backward(incoming, unit, inverse, gain_ref[...])


def last(keep, got, other, tokens, cols, gain, grad_hidden):
    rows, width = tokens.shape
    tile = pl.BlockSpec((STEP, width), lambda i: (i, 0))
    return pl.pallas_call(
        last_kernel,
        grid=(rows // STEP,),
        out_shape=shaped((rows, width), F32),
        in_specs=[tile] * 4 + [pl.BlockSpec((STEP, 128), lambda i: (i, 0)), VMEM, tile],
        out_specs=tile,
        cost_estimate=cost(0, 0),
        name="last",
    )(keep, got, other, tokens, cols, row(gain), grad_hidden)


def output_kernel(keep_ref, got_ref, other_ref, tokens_ref, unit2_ref, post_g_ref, post_b_ref, b_down_ref,
                  out_ref):
    hidden = tokens_ref[...].astype(F32) + (unit2_ref[...] * post_g_ref[...] + post_b_ref[...])
    branch = keep_ref[...] + got_ref[...].astype(F32) + other_ref[...].astype(F32)
    out_ref[...] = (hidden + (branch + b_down_ref[...])).astype(BF16)


def output_rows(keep, got, other, tokens, unit2, post_gain, post_bias, b_down):
    rows, width = tokens.shape
    tile = pl.BlockSpec((STEP, width), lambda i: (i, 0))
    return pl.pallas_call(
        output_kernel,
        grid=(rows // STEP,),
        out_shape=shaped((rows, width), BF16),
        in_specs=[tile] * 5 + [VMEM] * 3,
        out_specs=tile,
        cost_estimate=cost(0, 0),
        name="output_rows",
    )(keep, got, other, tokens, unit2, row(post_gain), row(post_bias), row(b_down))


def per_device(
    tokens,
    segments,
    ln1_gain,
    ln1_bias,
    w_query,
    b_query,
    w_key,
    w_value,
    b_value,
    head_scale,
    w_out,
    b_out,
    post_gain,
    post_bias,
    ln2_gain,
    ln2_bias,
    w_up,
    b_up,
    ffn_gain,
    ffn_bias,
    w_down,
    b_down,
    cotangent,
):
    index = lax.axis_index("tensor")
    rows = tokens.shape[0]
    two = 2 * rows
    columns = w_query.shape[1]
    hidden_here = w_up.shape[1]
    shard = D // lax.axis_size("dp")
    order = jnp.array([0, 2, 1, 3], jnp.int32)
    place = order[jnp.arange(4, dtype=jnp.int32) ^ index]
    here = jnp.full((1,), index, jnp.int32)

    def own_part(vector, width):
        return lax.dynamic_slice_in_dim(vector, index * width, width, 0)

    segment = segments[0]
    seg_col, seg_row = segment[:, None], segment[None, :]
    scale_row = row(jnp.repeat(own_part(head_scale, columns // HD), HD))
    qkv_b = jnp.concatenate(
        [own_part(b_query, columns), jnp.zeros((columns,), F32), own_part(b_value, columns)]
    )
    gain_here, shift_here = own_part(ffn_gain, hidden_here), own_part(ffn_bias, hidden_here)
    b_up_here = own_part(b_up, hidden_here)

    order_dp = lax.axis_index("dp") ^ jnp.arange(lax.axis_size("dp"), dtype=jnp.int32)
    quick = shard % 128 == 0 and lax.axis_size("dp") == 8

    attn = None
    if quick:
        packed, tokens = phase(pack(w_query, w_key, w_value, w_out), tokens)
        attn = Shards(packed)
        attn.send(4, 0)
        attn.send(1, 0)
        first = attn.get(4, 1)
    else:
        first = []
        attn_full = [
            lax.all_gather(jnp.concatenate([w_query, w_key, w_value], 1), "dp", axis=0, tiled=True),
            lax.all_gather(w_out, "dp", axis=1, tiled=True),
        ]
        up_full = [lax.all_gather(w_up, "dp", axis=0, tiled=True)]
        down_full = [lax.all_gather(w_down, "dp", axis=1, tiled=True)]
        attn_masks = up_masks = down_masks = None
    x_pair = swap(tokens, "tensor", 2)
    x_side = swap(tokens, "tensor", 1)
    up_s, down_s = Shards(w_up), Shards(w_down)
    own_up, own_down = up_s.held[0], down_s.held[0]
    (x_pair, x_side, own_up, own_down, cotangent, b_up_here, gain_here, shift_here, qkv_b, scale_row,
     seg_col, place, order_dp), first = phase(
        (x_pair, x_side, own_up, own_down, cotangent, b_up_here, gain_here, shift_here, qkv_b,
         scale_row, seg_col, place, order_dp), first)
    if quick:
        attn.put([4, 1], first)

    x_cross = swap(x_pair, "tensor", 1)
    if quick:
        attn.send(2, 0, 4)
        attn.send(1, 4)
        first = attn.get(2, 6, 5)
    g_pair = swap(cotangent, "tensor", 2)
    normed, x_all, cols1 = norm_one([tokens, x_pair, x_side, x_cross], ln1_gain, ln1_bias)
    (normed, x_all, cols1, own_up, own_down, g_pair, cotangent), first = phase(
        (normed, x_all, cols1, own_up, own_down, g_pair, cotangent), first)

    if quick:
        attn.put([2, 6, 5], first)
        attn.send(1, 2, 6)
        up_s.put([0], [own_up])
        up_s.send(4, 0)
        attn_masks, attn_full = attn.all()
        far = up_s.get(4)
    else:
        far = []
    g_side = swap(cotangent, "tensor", 1)
    g_cross = swap(g_pair, "tensor", 1)
    (normed, own_down, own_up, g_side, g_cross), attn_full = phase(
        (normed, own_down, own_up, g_side, g_cross), attn_full)

    if quick:
        up_s.put([0], [own_up])
        up_s.send(2, 0)
        up_s.send(1, 0)
        first = far + up_s.get(2, 1)
    qkv, mixed, scaled, lse, qkv_w, out_w, send, keep = attend(
        place, order_dp, normed, attn_masks, attn_full, row(qkv_b), seg_col, seg_row, scale_row
    )
    (qkv, mixed, scaled, lse, qkv_w, out_w, send, keep, own_down, g_side, g_cross), first = phase(
        (qkv, mixed, scaled, lse, qkv_w, out_w, send, keep, own_down, g_side, g_cross), first)

    got = swap(send, "tensor", 1)
    if quick:
        up_s.put([4, 2, 1], first)
        up_s.send(2, 4)
        up_s.send(1, 4, 2)
        down_s.put([0], [own_down])
        down_s.send(4, 0)
        down_s.send(1, 0)
        first = up_s.get(6, 5, 3) + down_s.get(4, 1)
    low, got, keep, g_side = phase(low_rows(keep, got, two), got, keep, g_side)
    other = swap(low, "tensor", 2)
    (g_all, own_down), first = phase((stack(cotangent, g_pair, g_side, g_cross), own_down), first)
    if quick:
        up_s.put([6, 5, 3], first[:3])
        down_s.put([0, 4, 1], [own_down] + first[3:])
        up_s.send(1, 6)
        down_s.send(2, 0, 4)
        down_s.send(1, 4)
        other, keep, got = phase(other, keep, got)
        first = down_s.get(2, 6, 5) + up_s.get(7)

    ffn_in, unit2, cols = middle(
        keep, got, other, tokens, x_pair, b_out, post_gain, post_bias, ln2_gain, ln2_bias
    )
    (ffn_in, unit2, cols), first = phase((ffn_in, unit2, cols), first)
    ffn_rest = swap(ffn_in, "tensor", 1)
    if quick:
        down_s.put([2, 6, 5], first[:3])
        up_s.put([7], first[3:])
        up_masks, up_full = up_s.all()
        down_s.send(1, 2, 6)
        down_masks, down_full = down_s.all()
    active_k, slope_k, stats_k, up_w = ffn_one(ffn_in, order_dp, up_masks, up_full, b_up_here)
    active_k, slope_k, stats_k, up_w, ffn_rest = phase(active_k, slope_k, stats_k, up_w, ffn_rest)
    active_s, slope_s, stats_s, _ = ffn_one(ffn_rest, order_dp, None, [up_w], b_up_here)
    (active_s, stats_s, slope_s), down_full = phase((active_s, stats_s, slope_s), down_full)
    inner_grad, stats, down_w = ffn_grad(
        g_all, order_dp, down_masks, down_full, active_k, active_s, stats_k, stats_s, gain_here
    )
    stats = [stats] + [swap(stats, "tensor", mask) for mask in (1, 2, 3)]
    inner, grad_before, send, keep, ffn_sums = ffn_two(
        active_k, active_s, slope_k, slope_s, inner_grad, stats, gain_here, shift_here, up_w
    )

    down_g, up_g, out_g = Scatter(1, shard, 1), Scatter(0, shard), Scatter(1, shard)
    qkv_a, qkv_b = Scatter(0, shard), Scatter(0, shard)
    got = swap(send, "tensor", 1)
    down_send = down_g.product([g_all], inner)
    down_send, down_g.keep, inner, grad_before, got, keep = phase(
        down_send, down_g.keep, inner, grad_before, got, keep
    )
    low, down_send, inner, grad_before = phase(low_rows(keep, got, two), down_send, inner, grad_before)
    other = swap(low, "tensor", 2)
    down_g.start(down_send)
    up_send = up_g.product([ffn_in, ffn_rest], grad_before)
    up_send, up_g.keep, inner = phase(up_send, up_g.keep, inner)
    up_g.start(up_send)
    out_send, out_keep = project(inner, down_w)
    other, down_g.got, out_send, out_keep = phase(other, down_g.got, out_send, out_keep)

    down_send = down_g.split()
    down_send, down_g.keep, other, out_send = phase(down_send, down_g.keep, other, out_send)
    down_g.start(down_send)
    out_got = swap(out_send, "tensor", 1)
    grad_proj, grad_hidden, middle_sums = middle_back(
        keep, got, other, cotangent, g_pair, tokens, x_pair, unit2, cols, post_gain, post_bias,
        ln2_gain,
    )
    grad_proj, up_g.got, out_got, out_keep = phase(grad_proj, up_g.got, out_got, out_keep)
    proj_rest = swap(grad_proj, "tensor", 1)
    up_send = up_g.split()
    out_low = low_rows(out_keep, out_got, rows)
    grad_proj, proj_rest, up_send, up_g.keep, out_low = phase(
        grad_proj, proj_rest, up_send, up_g.keep, out_low
    )
    w_send = out_g.product([grad_proj, proj_rest], scaled)
    w_send, out_g.keep, grad_proj, proj_rest, up_send, out_low = phase(
        w_send, out_g.keep, grad_proj, proj_rest, up_send, out_low
    )

    up_g.start(up_send)
    out_other = swap(out_low, "tensor", 2)
    out_g.start(w_send)
    grad_qkv, sums = attend_back(
        place, qkv, grad_proj, proj_rest, out_w, mixed, lse, seg_col, seg_row, scale_row
    )
    grad_qkv, sums, up_g.got, out_other, out_g.got = phase(
        grad_qkv, sums, up_g.got, out_other, out_g.got
    )

    masks = dp_masks(0)
    up_send, w_send = up_g.split(), out_g.split()
    up_send, up_g.keep, grad_qkv, w_send, out_g.keep = phase(
        up_send, up_g.keep, grad_qkv, w_send, out_g.keep
    )
    up_g.start(up_send)
    out_g.start(w_send)
    a_send = qkv_a.product([normed], grad_qkv, 0, 2)
    a_send, qkv_a.keep, grad_qkv = phase(a_send, qkv_a.keep, grad_qkv)
    qkv_a.start(a_send)
    send, keep, late = normed_grad(
        here, grad_qkv, qkv_w, x_all, cols1, sums, middle_sums, ffn_sums
    )
    b_send = qkv_b.product([normed], grad_qkv, 1, 2)
    send, keep, late, b_send, qkv_b.keep, qkv_a.got, down_g.got, out_g.got = phase(
        send, keep, late, b_send, qkv_b.keep, qkv_a.got, down_g.got, out_g.got
    )
    got = swap(send, "tensor", 1)
    side = swap(late, "tensor", 1)
    qkv_b.start(b_send)
    a_send, w_send, d_send = qkv_a.split(), out_g.split(), down_g.split()
    a_send, qkv_a.keep, w_send, out_g.keep, got, keep, late, d_send, down_g.keep, up_g.got, out_other = phase(
        a_send, qkv_a.keep, w_send, out_g.keep, got, keep, late + side, d_send, down_g.keep, up_g.got,
        out_other
    )
    qkv_a.start(a_send)
    out_g.start(w_send)
    side = swap(late, "tensor", 2)
    low = low_rows(keep, got, rows)
    output = output_rows(out_keep, out_got, out_other, tokens, unit2, post_gain, post_bias, b_down)
    output, low, late, qkv_a.got, qkv_a.keep, qkv_b.got, qkv_b.keep, out_g.got = phase(
        output, low, late + side, qkv_a.got, qkv_a.keep, qkv_b.got, qkv_b.keep, out_g.got
    )
    other = swap(low, "tensor", 2)
    side = swap(late, "dp", masks[0])
    a_send, b_send = qkv_a.split(), qkv_b.split()
    a_send, qkv_a.keep, b_send, qkv_b.keep, late, d_send = phase(
        a_send, qkv_a.keep, b_send, qkv_b.keep, late + side, d_send
    )
    qkv_a.start(a_send)
    side = swap(late, "dp", masks[1])
    qkv_b.start(b_send)
    down_g.start(d_send)
    late, qkv_b.got, qkv_b.keep, up_g.got, out_g.got = phase(
        late + side, qkv_b.got, qkv_b.keep, up_g.got, out_g.got
    )
    if quick:
        b_send, late, other = phase(qkv_b.split(), late, other)
        qkv_b.start(b_send)
    input_grad = last(keep, got, other, tokens, cols1, ln1_gain, grad_hidden)
    g_up, g_out = up_g.finish(), out_g.finish()
    for mask in masks[2:]:
        late = late + swap(late, "dp", mask)
    g_down = down_g.finish()
    g_a, g_b = qkv_a.finish(), qkv_b.finish()
    extra = g_a.shape[1] - columns
    blocks = FF // D
    return (
        output,
        input_grad,
        late[0],
        late[1],
        g_a[:, :columns],
        late[2],
        jnp.concatenate([g_a[:, columns:], g_b[:, : columns - extra]], 1),
        g_b[:, columns - extra :],
        late[3],
        jnp.sum(late[4].reshape(HEADS, HD), axis=1),
        g_out,
        late[9],
        late[7],
        late[8],
        late[5],
        late[6],
        g_up,
        late[12 : 12 + blocks].reshape(FF),
        late[12 + blocks : 12 + 2 * blocks].reshape(FF),
        late[12 + 2 * blocks : 12 + 3 * blocks].reshape(FF),
        g_down,
        late[10],
    )


def solution(mesh):
    return jax.shard_map(
        per_device,
        mesh=mesh,
        in_specs=(
            P(("dp", "tensor"), None),
            P("dp", None),
            P(),
            P(),
            P("dp", "tensor"),
            P(),
            P("dp", "tensor"),
            P("dp", "tensor"),
            P(),
            P(),
            P("tensor", "dp"),
            P(),
            P(),
            P(),
            P(),
            P(),
            P("dp", "tensor"),
            P(),
            P(),
            P(),
            P("tensor", "dp"),
            P(),
            P(("dp", "tensor"), None),
        ),
        out_specs=(
            P(("dp", "tensor"), None),
            P(("dp", "tensor"), None),
            P(),
            P(),
            P("dp", "tensor"),
            P(),
            P("dp", "tensor"),
            P("dp", "tensor"),
            P(),
            P(),
            P("tensor", "dp"),
            P(),
            P(),
            P(),
            P(),
            P(),
            P("dp", "tensor"),
            P(),
            P(),
            P(),
            P("tensor", "dp"),
            P(),
        ),
        check_vma=False,
    )
```
